32 devices in a mesh: blk: 16 (over z, y, core), sub: 2 (over x).
Axes of the slice: x: 2, y: 2, z: 4, core: 2. Of those that a mesh axis runs over, the one named last changes fastest.
Arguments:
- correlation: float32 [64, 6, 128, 128], P(('blk', 'sub')), may hold values from -3 to 3, as said below
- factor: float32 [64, 6, 128, 128], P(('blk', 'sub')), may hold values from -2 to 2, as said below
- pattern: int32 [64, 6], replicated, may hold values from 0 to 63, as said below
Outputs:
- refined: float32 [64, 6, 128, 128], P(('blk', 'sub'))
- correction: float32 [64, 6, 128, 128], P(('blk', 'sub'))
The draws below stay inside these ranges and needn't reach their ends.
Inputs may be any that keep to these rules, and one draw needn't show every extreme that they name: `pattern`: slot 0 of tile row i is i itself; the other 5 slots name all but one of the tile rows i - 3 to i + 3 other than i, taken modulo 64, in increasing offset. `correlation`: slot 0 of each tile row holds the diagonal tile. `factor`: slot 0 of each tile row holds the diagonal tile.
All inputs are finite; a program needn't handle non-finite values.
Results may differ from the reference program's by a relative error of at most 0.0003.
Values sent between devices are 32-bit elements; how exact they have to be, the bound alone decides.
No kernel may reach another device: no remote copies, remote signals or barrier semaphores. Data moves between devices by JAX's collectives and lax.ppermute only.
A program may use at most 64 MiB of HBM per device.

```python
import math
import jax
import jax.numpy as jnp
from jax import lax

TILE = 128
REACH = 3
ITERS = 1
SLOTS = 6
NT = 64


def draw_pattern(key, part):
    dropped = jax.random.randint(key, (NT, 1), 0, 2 * REACH)
    position = jnp.arange(2 * REACH - 1, dtype=jnp.int32)[None, :]
    chosen = position + (position >= dropped).astype(jnp.int32)
    offset = chosen - REACH + (chosen >= REACH).astype(jnp.int32)
    row_ids = jnp.arange(NT, dtype=jnp.int32)[:, None]
    others = (row_ids + offset) % NT
    return jnp.concatenate([row_ids, others], axis=1).astype(jnp.int32)


def tile_noise(key):
    shape = (NT, SLOTS, TILE, TILE)
    noise = jnp.clip(jax.random.normal(jax.random.fold_in(key, 13), shape), -6.0, 6.0)
    return noise.astype(jnp.float32)


def draw_correlation(key, part):
    scale = 0.6 / math.sqrt(SLOTS * TILE)
    tiles = tile_noise(jax.random.fold_in(key, 1)) * scale
    return tiles.at[:, 0].add(2.0 * jnp.eye(TILE, dtype=jnp.float32))


def draw_factor(key, part):
    scale = 0.4 / math.sqrt(SLOTS * TILE)
    tiles = tile_noise(jax.random.fold_in(key, 2)) * scale
    return tiles.at[:, 0].add(jnp.eye(TILE, dtype=jnp.float32) / math.sqrt(2.0))


def setup_inputs(seed: int = 0) -> dict:
    key_list = jax.random.split(jax.random.key(seed), 4)
    return {
        "correlation": draw_correlation(jax.random.fold_in(key_list[3], 71), 0),
        "factor": draw_factor(jax.random.fold_in(key_list[3], 71), 0),
        "pattern": draw_pattern(jax.random.fold_in(key_list[3], 71), 0),
    }


def lookup(tiles, pattern, rows_wanted, columns_wanted):
    matches = pattern[rows_wanted] == columns_wanted[..., None]
    slot_index = jnp.argmax(matches, axis=-1).astype(jnp.int32)
    present = jnp.any(matches, axis=-1).astype(tiles.dtype)
    return tiles[rows_wanted, slot_index] * present[..., None, None]


def row_product(left_tiles, right_tiles, pattern, row_index):
    own_cols = pattern[row_index]
    width_slots = own_cols.shape[0]
    grid_shape = (width_slots, width_slots)
    chosen = lookup(right_tiles, pattern, jnp.broadcast_to(own_cols[:, None], grid_shape), jnp.broadcast_to(own_cols[None, :], grid_shape))
    return jnp.einsum("qab,qpbc->pac", left_tiles[row_index], chosen, precision=lax.Precision.HIGHEST)


def row_gram(factor, product, pattern, row_index):
    total_rows = pattern.shape[0]
    offsets = jnp.arange(-REACH, REACH + 1, dtype=jnp.int32)
    candidates = (row_index + offsets) % total_rows
    left_side = lookup(factor, pattern, candidates, jnp.broadcast_to(row_index, candidates.shape))
    wanted = pattern[row_index]
    grid_shape = (candidates.shape[0], wanted.shape[0])
    right_side = lookup(product, pattern, jnp.broadcast_to(candidates[:, None], grid_shape), jnp.broadcast_to(wanted[None, :], grid_shape))
    return jnp.einsum("oba,opbc->pac", left_side, right_side, precision=lax.Precision.HIGHEST)


def reference(correlation, factor, pattern):
    total_rows = pattern.shape[0]
    all_rows = jnp.arange(total_rows, dtype=jnp.int32)
    identity = jnp.eye(correlation.shape[2], dtype=jnp.float32)
    correction = factor
    for sweep_index in range(ITERS):
        product = lax.map(lambda row_index: row_product(correlation, factor, pattern, row_index), all_rows)
        gram_tiles = lax.map(lambda row_index: row_gram(factor, product, pattern, row_index), all_rows)
        correction = (-gram_tiles).at[:, 0].add(identity)
        update = lax.map(lambda row_index: row_product(factor, correction, pattern, row_index), all_rows)
        factor = factor + 0.5 * update
    return factor, correction
```

```python
import jax
import jax.numpy as jnp
from jax import lax
from jax.experimental import pallas as pl
from jax.experimental.pallas import tpu as pltpu
from jax.sharding import PartitionSpec as P


REACH = 3
AXES = ("blk", "sub")
OWN = 2
LEFT = -2 * REACH
WIDE = OWN + 4 * REACH
COL0 = -REACH
COLS = OWN + 2 * REACH
PAIRS = COLS // 2
SIDE = 3
F32 = jnp.float32
BF16 = jnp.bfloat16

UP = ((0, 3), (0, 4), (0, 5), (1, 0), (1, 3), (1, 4), (1, 5))
DOWN = ((0, 0), (0, 1), (0, 2), (0, 3), (1, 1), (1, 2), (1, 3))
FAR_UP = ((0, 5), (1, 4), (1, 5))
FAR_DOWN = ((0, 1), (0, 2), (1, 1))


def send(value, to):
    count = lax.axis_size(AXES)
    return lax.ppermute(value, AXES, [(i, to(i) % count) for i in range(count)])


def swap(i):
    return i ^ 1


def up(i):
    return i + 2


def down(i):
    return i - 2


def near(i):
    return i + 2 if i % 2 == 0 else i - 2


def far_up(i):
    return i + 4 if i % 2 == 0 else i + 2


def far_down(i):
    return i - 2 if i % 2 == 0 else i - 4


def split(value):
    high = value.astype(BF16)
    low = (value - high.astype(F32)).astype(BF16)
    return high, low


def dot3(a_high, a_low, b_high, b_low):
    left = jnp.concatenate([a_high, a_low, a_high], axis=1)
    right = jnp.concatenate([b_high, b_high, b_low], axis=0)
    return jnp.dot(left, right, preferred_element_type=F32)


def slot_of(offset, dropped):
    pos = offset + REACH - jnp.where(offset > 0, 1, 0)
    slot = jnp.where(offset == 0, 0, pos + 1 - jnp.where(pos > dropped, 1, 0))
    there = (jnp.abs(offset) <= REACH) & ((offset == 0) | (pos != dropped))
    return jnp.clip(slot, 0, 2 * REACH - 1), there


class Rows:
    def __init__(self, meta):
        self.meta = meta
        self.parity = meta[WIDE]

    def dropped(self, row):
        return self.meta[row - LEFT]

    def side_row(self, side):
        return 2 - 4 * jnp.bitwise_xor(self.parity, side)

    def side_pair(self, side):
        return 1 - jnp.bitwise_xor(self.parity, side)

    def present(self, row, col):
        return slot_of(jnp.int32(col - row), self.dropped(row))[1]

    def own(self, refs, row, col):
        slot, there = slot_of(jnp.int32(col - row), self.dropped(row))
        tile = refs[row][0, slot] if isinstance(refs, tuple) else refs[row, slot]
        return jnp.where(there, tile, 0.0)

    def packed(self, ref, layout, row0, r, col):
        slots = [s for rr, s in layout if rr == r]
        base = [j for j, (rr, _) in enumerate(layout) if rr == r][0]
        row = row0 + r
        if col == row:
            return ref[base + slots.index(0)]
        slot, there = slot_of(jnp.int32(col - row), self.dropped(row))
        rest = [s for s in slots if s]
        index = base + slots.index(rest[0]) + jnp.clip(slot - rest[0], 0, len(rest) - 1)
        return jnp.where(there, ref[index], 0.0)

    def side(self, refs, side, r, col):
        row = self.side_row(side) + r
        slot, there = slot_of(col - row, self.dropped(row))
        return jnp.where(there, refs[r][0, slot], 0.0)

    def dense_slot(self, row, slot):
        if slot == 0:
            return row - COL0
        pos = slot - 1 + jnp.where(slot - 1 >= self.dropped(row), 1, 0)
        return row - COL0 - REACH + pos + jnp.where(pos >= REACH, 1, 0)


def zero(tile):
    return jnp.zeros((tile, tile), F32)


def put(high, low, r, c, tile, value):
    h, l = split(value)
    high[r, :, c * tile : (c + 1) * tile] = h
    low[r, :, c * tile : (c + 1) * tile] = l


def flat(ref, rows, cols):
    value = ref[rows, :, cols]
    return value.reshape(value.shape[0] * value.shape[1], value.shape[2])


def row_matmul(left_high, left_low, right_high, right_low, out, tile):
    for c in range(0, COLS, 2):
        lo, hi = max(c - REACH, 0), min(c + 1 + REACH, COLS - 1) + 1
        k = slice(lo * tile, hi * tile)
        n = slice(c * tile, (c + 2) * tile)
        block = dot3(
            flat(left_high, slice(None), k),
            flat(left_low, slice(None), k),
            flat(right_high, slice(lo, hi), n),
            flat(right_low, slice(lo, hi), n),
        )
        for i in range(OWN):
            for j in range(2):
                out[i, c + j] = block[i * tile : (i + 1) * tile, j * tile : (j + 1) * tile]


def pack_kernel(z, zu, zd):
    for out, layout in ((zu, UP), (zd, DOWN)):
        for j, (i, slot) in enumerate(layout):
            out[j] = z[i, slot]


def product_kernel(meta, s, z, x0, x1, n0, n1, zu, zd, p0, p1, pu, pd, z_high, z_low, s_high, s_low, dense):
    tile = s.shape[-1]
    rows = Rows(meta)
    for c in range(COLS):
        col = c + COL0
        for i in range(OWN):
            near_by = abs(col - i) <= REACH
            put(s_high, s_low, i, c, tile, rows.own(s, i, col) if near_by else zero(tile))
            put(z_high, z_low, i - COL0, c, tile, rows.own(z, i, col) if near_by else zero(tile))
        for side, refs in enumerate(((x0, x1), (n0, n1))):
            for r in range(2):
                where = rows.side_row(side) + r - COL0
                put(z_high, z_low, where, c, tile, rows.side(refs, side, r, col))
        row = -REACH
        put(z_high, z_low, 0, c, tile, rows.packed(zu, UP, -4, 1, col) if abs(col - row) <= REACH else zero(tile))
        row = OWN - 1 + REACH
        put(z_high, z_low, COLS - 1, c, tile, rows.packed(zd, DOWN, 4, 0, col) if abs(col - row) <= REACH else zero(tile))
    row_matmul(s_high, s_low, z_high, z_low, dense, tile)
    for i, ref in enumerate((p0, p1)):
        for slot in range(2 * REACH):
            ref[0, slot] = dense[i, rows.dense_slot(i, slot)]
    for ref, layout in ((pu, UP), (pd, DOWN)):
        for j, (i, slot) in enumerate(layout):
            ref[j] = dense[i, rows.dense_slot(i, slot)]


def turn_kernel(meta, z, x0, x1, n0, n1, zu, zd, fu, fd, t_own, t_up, t_down, t_swap, t_near, t_far, z_own):
    tile = z.shape[-1]
    rows = Rows(meta)

    def store(out, c, r, value):
        high, low = split(value.T)
        out[c * tile : (c + 1) * tile, r * tile : (r + 1) * tile] = high
        out[c * tile : (c + 1) * tile, (2 + r) * tile : (3 + r) * tile] = low

    for r in range(2):
        for c in range(COLS):
            col = c + COL0
            value = rows.own(z, r, col) if abs(col - r) <= REACH else zero(tile)
            store(t_own, c, r, value)
            high, low = split(value)
            z_own[r, :, c * tile : (c + 1) * tile] = high
            z_own[r, :, (COLS + c) * tile : (COLS + c + 1) * tile] = low
        for c in range(4):
            col = c + COL0
            store(t_up, c, r, rows.packed(zu, UP, -4, r, col) if abs(col - (r - 4)) <= REACH else zero(tile))
            col = c + COL0 + 4
            store(t_down, c, r, rows.packed(zd, DOWN, 4, r, col) if abs(col - (r + 4)) <= REACH else zero(tile))
        for c in range(2):
            col = c + COL0
            store(t_far, c, r, rows.packed(fu, FAR_UP, -6, r, col) if abs(col - (r - 6)) <= REACH else zero(tile))
            col = c + COL0 + 6
            store(t_far, 2 + c, r, rows.packed(fd, FAR_DOWN, 6, r, col) if abs(col - (r + 6)) <= REACH else zero(tile))
        for side, (out, refs) in enumerate(((t_swap, (x0, x1)), (t_near, (n0, n1)))):
            first = 2 * rows.side_pair(side) + COL0
            for c in range(2 * SIDE):
                store(out, c, r, rows.side(refs, side, r, first + c))


def halves(turned, first, last, tile):
    part = turned[2 * first * tile : 2 * last * tile]
    return part[:, : 2 * tile], part[:, 2 * tile :]


def side_gram(rows, side, refs, turned, high, low, add, tile):
    first = 2 * rows.side_pair(side) + COL0
    for r in range(2):
        for c in range(2 * SIDE):
            put(high, low, r, c, tile, rows.side(refs, side, r, first + c))
    left = halves(turned, 0, SIDE, tile)
    for b in range(SIDE):
        n = slice(2 * b * tile, (2 * b + 2) * tile)
        block = dot3(*left, flat(high, slice(0, 2), n), flat(low, slice(0, 2), n))
        for a in range(SIDE):
            add(a, b, block[2 * a * tile : (2 * a + 2) * tile])


def gram_kernel(meta, t_own, t_up, t_down, t_swap, p0, p1, pu, pd, x0, x1, gram, high, low, side_high, side_low):
    tile = p0.shape[-1]
    rows = Rows(meta)
    for r in range(2):
        for c in range(COLS):
            col = c + COL0
            put(high, low, r, c, tile, rows.own((p0, p1), r, col) if abs(col - r) <= REACH else zero(tile))
        for c in range(4):
            col = c + COL0
            value = rows.packed(pu, UP, -4, r, col) if abs(col - (r - 4)) <= REACH else zero(tile)
            put(high, low, 2 + r, c, tile, value)
            col = c + COL0 + 4
            value = rows.packed(pd, DOWN, 4, r, col) if abs(col - (r + 4)) <= REACH else zero(tile)
            put(high, low, 2 + r, 4 + c, tile, value)
    for b in range(PAIRS):
        n = slice(2 * b * tile, (2 * b + 2) * tile)
        first, last = max(0, b - 2), min(PAIRS, b + 3)
        block = dot3(*halves(t_own, first, last, tile), flat(high, slice(0, 2), n), flat(low, slice(0, 2), n))
        edge = dot3(
            *halves(t_up if b < 2 else t_down, 0, 2, tile), flat(high, slice(2, 4), n), flat(low, slice(2, 4), n)
        )
        for a in range(first, last):
            value = block[2 * (a - first) * tile : 2 * (a - first + 1) * tile]
            e = a if b < 2 else a - 2
            if 0 <= e < 2:
                value = value + edge[2 * e * tile : (2 * e + 2) * tile]
            gram[PAIRS * a + b] = value

    def add(a, b, value):
        index = PAIRS * a + b + (PAIRS + 1) * rows.side_pair(0)
        gram[index] = gram[index] + value

    side_gram(rows, 0, (x0, x1), t_swap, side_high, side_low, add, tile)


def refine_kernel(
    meta, z, z_own, t_near, t_far, early, n0, n1, fu, fd, refined, correction,
    high, low, far_high, far_low, late, d_high, d_low, dense, z_high, z_low,
):
    tile = z.shape[-1]
    rows = Rows(meta)

    def add(a, b, value):
        late[SIDE * a + b] = value

    side_gram(rows, 1, (n0, n1), t_near, high, low, add, tile)
    for r in range(2):
        for c in range(2):
            col = c + COL0
            value = rows.packed(fu, FAR_UP, -6, r, col) if abs(col - (r - 6)) <= REACH else zero(tile)
            put(far_high, far_low, r, c, tile, value)
            col = c + COL0 + 6
            value = rows.packed(fd, FAR_DOWN, 6, r, col) if abs(col - (r + 6)) <= REACH else zero(tile)
            put(far_high, far_low, r, 2 + c, tile, value)
    far = []
    for e in range(2):
        n = slice(2 * e * tile, (2 * e + 2) * tile)
        far.append(
            dot3(*halves(t_far, e, e + 1, tile), flat(far_high, slice(0, 2), n), flat(far_low, slice(0, 2), n))
        )
    eye = (
        lax.broadcasted_iota(jnp.int32, (tile, tile), 0) == lax.broadcasted_iota(jnp.int32, (tile, tile), 1)
    ).astype(F32)
    shift = rows.side_pair(1)
    for a in range(PAIRS):
        for b in range(PAIRS):
            if abs(a - b) > 2:
                continue
            gram = early[PAIRS * a + b]
            ia, ib = a - shift, b - shift
            there = (ia >= 0) & (ia < SIDE) & (ib >= 0) & (ib < SIDE)
            gram = gram + jnp.where(there, late[jnp.clip(SIDE * ia + ib, 0, SIDE * SIDE - 1)], 0.0)
            if a == b and a in (0, PAIRS - 1):
                gram = gram + far[0 if a == 0 else 1]
            for i in range(2):
                for j in range(2):
                    k, c = 2 * a + i, 2 * b + j
                    value = -gram[i * tile : (i + 1) * tile, j * tile : (j + 1) * tile]
                    if k == c:
                        value = value + eye
                    elif abs(k - c) <= REACH:
                        value = jnp.where(rows.present(k + COL0, c + COL0), value, 0.0)
                    else:
                        value = zero(tile)
                    put(d_high, d_low, k, c, tile, value)
                    if k + COL0 in (0, 1):
                        dense[k + COL0, c] = value
    for i in range(OWN):
        for slot in range(2 * REACH):
            correction[i, slot] = dense[i, rows.dense_slot(i, slot)]
    half = COLS * tile
    z_high[...] = z_own[:, :, :half]
    z_low[...] = z_own[:, :, half:]
    row_matmul(z_high, z_low, d_high, d_low, dense, tile)
    for i in range(OWN):
        for slot in range(2 * REACH):
            refined[i, slot] = z[i, slot] + 0.5 * dense[i, rows.dense_slot(i, slot)]


def pick(rows, layout):
    return jnp.concatenate([rows[r][0, s : s + 1] for r, s in layout], axis=0)


def body(correlation, factor, pattern):
    rows_here, slots, tile = correlation.shape[:3]
    total = pattern.shape[0]
    assert rows_here == OWN and slots == 2 * REACH and total >= WIDE
    device = lax.axis_index(AXES)
    rows = (device * OWN + jnp.arange(LEFT, LEFT + WIDE, dtype=jnp.int32)) % total
    offsets = (pattern[rows][:, 1:] - rows[:, None] + total // 2) % total - total // 2
    expected = jnp.array([-3, -2, -1, 1, 2], jnp.int32)
    dropped = jnp.sum((offsets == expected).astype(jnp.int32), axis=1)
    meta = jnp.concatenate([dropped, (device % 2)[None]]).astype(jnp.int32)

    vmem = pl.BlockSpec(memory_space=pltpu.VMEM)
    smem = pl.BlockSpec(memory_space=pltpu.SMEM)

    def call(kernel, ins, outs, scratch, flops, scalars=1):
        return pl.pallas_call(
            kernel,
            in_specs=[smem] * scalars + [vmem] * (len(ins) - scalars),
            out_specs=jax.tree.map(lambda _: vmem, outs),
            out_shape=outs,
            scratch_shapes=scratch,
            cost_estimate=pl.CostEstimate(flops=flops, bytes_accessed=4 << 20, transcendentals=0),
        )(*ins)

    def shape(*dims, dtype=F32):
        return jax.ShapeDtypeStruct(dims, dtype)

    def halves_of(n, m):
        return [pltpu.VMEM((n, tile, m * tile), BF16)] * 2

    row = shape(1, slots, tile, tile)
    seven = shape(len(UP), tile, tile)
    dense = pltpu.VMEM((OWN, COLS, tile, tile), F32)

    x = [send(factor[r : r + 1], swap) for r in range(OWN)]
    zu, zd = call(pack_kernel, (factor,), (seven, seven), [], 1000, 0)
    zu, zd = send(zu, up), send(zd, down)
    n = [send(x[r], near) for r in range(OWN)]
    zfu = send(pick(x, FAR_UP), far_up)
    zfd = send(pick(x, FAR_DOWN), far_down)
    p0, p1, pu, pd = call(
        product_kernel,
        (meta, correlation, factor, *x, *n, zu, zd),
        (row, row, seven, seven),
        halves_of(COLS, COLS) + halves_of(OWN, COLS) + [dense],
        int(2e9),
    )
    px = [send(v, swap) for v in (p0, p1)]
    pu, pd = send(pu, up), send(pd, down)
    pn = [send(v, near) for v in px]
    pfu = send(pick(px, FAR_UP), far_up)
    pfd = send(pick(px, FAR_DOWN), far_down)

    def turned(columns):
        return shape(columns * tile, 4 * tile, dtype=BF16)

    t_own, t_up, t_down, t_swap, t_near, t_far, z_own = call(
        turn_kernel,
        (meta, factor, *x, *n, zu, zd, zfu, zfd),
        (turned(COLS), turned(4), turned(4), turned(2 * SIDE), turned(2 * SIDE), turned(4),
         shape(OWN, tile, 2 * COLS * tile, dtype=BF16)),
        [],
        int(2e9),
    )
    early = call(
        gram_kernel,
        (meta, t_own, t_up, t_down, t_swap, p0, p1, pu, pd, *px),
        shape(PAIRS * PAIRS, 2 * tile, 2 * tile),
        halves_of(4, COLS) + halves_of(2, 2 * SIDE),
        int(4e9),
    )
    return call(
        refine_kernel,
        (meta, factor, z_own, t_near, t_far, early, *pn, pfu, pfd),
        (shape(*factor.shape), shape(*factor.shape)),
        halves_of(2, 2 * SIDE)
        + halves_of(2, 4)
        + [pltpu.VMEM((SIDE * SIDE, 2 * tile, 2 * tile), F32)]
        + halves_of(COLS, COLS)
        + [dense]
        + halves_of(OWN, COLS),
        int(4e9),
    )


def solution(mesh):
    tiles = P(AXES, None, None, None)

    return jax.shard_map(body, mesh=mesh, in_specs=(tiles, tiles, P()), out_specs=(tiles, tiles), check_vma=False)
```

```python
import jax
import jax.numpy as jnp
from jax import lax
from jax.experimental import pallas as pl
from jax.experimental.pallas import tpu as pltpu
from jax.sharding import PartitionSpec as P


REACH = 3
AXES = ("blk", "sub")
OWN = 2
LEFT = -2 * REACH
WIDE = OWN + 4 * REACH
COL0 = -REACH
COLS = OWN + 2 * REACH
PAIRS = COLS // 2
SIDE = 3
VMEM_LIMIT = 24 << 20
F32 = jnp.float32
BF16 = jnp.bfloat16

UP = ((0, 3), (0, 4), (0, 5), (1, 0), (1, 3), (1, 4), (1, 5))
DOWN = ((0, 0), (0, 1), (0, 2), (0, 3), (1, 1), (1, 2), (1, 3))
FAR_UP = ((0, 5), (1, 4), (1, 5))
FAR_DOWN = ((0, 1), (0, 2), (1, 1))


def send(value, to):
    count = lax.axis_size(AXES)
    return lax.ppermute(value, AXES, [(i, to(i) % count) for i in range(count)])


def swap(i):
    return i ^ 1


def up(i):
    return i + 2


def down(i):
    return i - 2


def near(i):
    return i + 2 if i % 2 == 0 else i - 2


def far_up(i):
    return i + 4 if i % 2 == 0 else i + 2


def far_down(i):
    return i - 2 if i % 2 == 0 else i - 4


def split(value):
    high = value.astype(BF16)
    low = (value - high.astype(F32)).astype(BF16)
    return high, low


def dot3(a_high, a_low, b_high, b_low):
    left = jnp.concatenate([a_high, a_low, a_high], axis=1)
    right = jnp.concatenate([b_high, b_high, b_low], axis=0)
    return jnp.dot(left, right, preferred_element_type=F32)


def slot_of(offset, dropped):
    pos = offset + REACH - jnp.where(offset > 0, 1, 0)
    slot = jnp.where(offset == 0, 0, pos + 1 - jnp.where(pos > dropped, 1, 0))
    there = (jnp.abs(offset) <= REACH) & ((offset == 0) | (pos != dropped))
    return jnp.clip(slot, 0, 2 * REACH - 1), there


class Rows:
    def __init__(self, meta):
        self.meta = meta
        self.parity = meta[WIDE]

    def dropped(self, row):
        return self.meta[row - LEFT]

    def side_row(self, side):
        return 2 - 4 * jnp.bitwise_xor(self.parity, side)

    def side_pair(self, side):
        return 1 - jnp.bitwise_xor(self.parity, side)

    def present(self, row, col):
        return slot_of(jnp.int32(col - row), self.dropped(row))[1]

    def own(self, refs, row, col):
        slot, there = slot_of(jnp.int32(col - row), self.dropped(row))
        tile = refs[row][0, slot] if isinstance(refs, tuple) else refs[row, slot]
        return jnp.where(there, tile, 0.0)

    def packed(self, ref, layout, row0, r, col):
        slots = [s for rr, s in layout if rr == r]
        base = [j for j, (rr, _) in enumerate(layout) if rr == r][0]
        row = row0 + r
        if col == row:
            return ref[base + slots.index(0)]
        slot, there = slot_of(jnp.int32(col - row), self.dropped(row))
        rest = [s for s in slots if s]
        index = base + slots.index(rest[0]) + jnp.clip(slot - rest[0], 0, len(rest) - 1)
        return jnp.where(there, ref[index], 0.0)

    def side(self, refs, side, r, col):
        row = self.side_row(side) + r
        slot, there = slot_of(col - row, self.dropped(row))
        return jnp.where(there, refs[r][0, slot], 0.0)

    def dense_slot(self, row, slot):
        if slot == 0:
            return row - COL0
        pos = slot - 1 + jnp.where(slot - 1 >= self.dropped(row), 1, 0)
        return row - COL0 - REACH + pos + jnp.where(pos >= REACH, 1, 0)


def zero(tile):
    return jnp.zeros((tile, tile), F32)


def put(high, low, r, c, tile, value):
    h, l = split(value)
    high[r, :, c * tile : (c + 1) * tile] = h
    low[r, :, c * tile : (c + 1) * tile] = l


def flat(ref, rows, cols):
    value = ref[rows, :, cols]
    return value.reshape(value.shape[0] * value.shape[1], value.shape[2])


def row_matmul(left_high, left_low, right_high, right_low, out, tile):
    for c in range(0, COLS, 2):
        lo, hi = max(c - REACH, 0), min(c + 1 + REACH, COLS - 1) + 1
        k = slice(lo * tile, hi * tile)
        n = slice(c * tile, (c + 2) * tile)
        block = dot3(
            flat(left_high, slice(None), k),
            flat(left_low, slice(None), k),
            flat(right_high, slice(lo, hi), n),
            flat(right_low, slice(lo, hi), n),
        )
        for i in range(OWN):
            for j in range(2):
                out[i, c + j] = block[i * tile : (i + 1) * tile, j * tile : (j + 1) * tile]


def pack_kernel(z, zu, zd):
    for out, layout in ((zu, UP), (zd, DOWN)):
        for j, (i, slot) in enumerate(layout):
            out[j] = z[i, slot]


def product_kernel(meta, s, z, x0, x1, n0, n1, zu, zd, p0, p1, pu, pd, z_high, z_low, s_high, s_low, dense):
    tile = s.shape[-1]
    rows = Rows(meta)
    for c in range(COLS):
        col = c + COL0
        for i in range(OWN):
            near_by = abs(col - i) <= REACH
            put(s_high, s_low, i, c, tile, rows.own(s, i, col) if near_by else zero(tile))
            put(z_high, z_low, i - COL0, c, tile, rows.own(z, i, col) if near_by else zero(tile))
        for side, refs in enumerate(((x0, x1), (n0, n1))):
            for r in range(2):
                where = rows.side_row(side) + r - COL0
                put(z_high, z_low, where, c, tile, rows.side(refs, side, r, col))
        row = -REACH
        put(z_high, z_low, 0, c, tile, rows.packed(zu, UP, -4, 1, col) if abs(col - row) <= REACH else zero(tile))
        row = OWN - 1 + REACH
        put(z_high, z_low, COLS - 1, c, tile, rows.packed(zd, DOWN, 4, 0, col) if abs(col - row) <= REACH else zero(tile))
    row_matmul(s_high, s_low, z_high, z_low, dense, tile)
    for i, ref in enumerate((p0, p1)):
        for slot in range(2 * REACH):
            ref[0, slot] = dense[i, rows.dense_slot(i, slot)]
    for ref, layout in ((pu, UP), (pd, DOWN)):
        for j, (i, slot) in enumerate(layout):
            ref[j] = dense[i, rows.dense_slot(i, slot)]


def turn_kernel(meta, z, x0, x1, n0, n1, zu, zd, fu, fd, t_own, t_up, t_down, t_swap, t_near, t_far, z_own):
    tile = z.shape[-1]
    rows = Rows(meta)

    def store(out, c, r, value):
        high, low = split(value.T)
        out[c * tile : (c + 1) * tile, r * tile : (r + 1) * tile] = high
        out[c * tile : (c + 1) * tile, (2 + r) * tile : (3 + r) * tile] = low

    for r in range(2):
        for c in range(COLS):
            col = c + COL0
            value = rows.own(z, r, col) if abs(col - r) <= REACH else zero(tile)
            store(t_own, c, r, value)
            high, low = split(value)
            z_own[r, :, c * tile : (c + 1) * tile] = high
            z_own[r, :, (COLS + c) * tile : (COLS + c + 1) * tile] = low
        for c in range(4):
            col = c + COL0
            store(t_up, c, r, rows.packed(zu, UP, -4, r, col) if abs(col - (r - 4)) <= REACH else zero(tile))
            col = c + COL0 + 4
            store(t_down, c, r, rows.packed(zd, DOWN, 4, r, col) if abs(col - (r + 4)) <= REACH else zero(tile))
        for c in range(2):
            col = c + COL0
            store(t_far, c, r, rows.packed(fu, FAR_UP, -6, r, col) if abs(col - (r - 6)) <= REACH else zero(tile))
            col = c + COL0 + 6
            store(t_far, 2 + c, r, rows.packed(fd, FAR_DOWN, 6, r, col) if abs(col - (r + 6)) <= REACH else zero(tile))
        for side, (out, refs) in enumerate(((t_swap, (x0, x1)), (t_near, (n0, n1)))):
            first = 2 * rows.side_pair(side) + COL0
            for c in range(2 * SIDE):
                store(out, c, r, rows.side(refs, side, r, first + c))


def halves(turned, first, last, tile):
    part = turned[2 * first * tile : 2 * last * tile]
    return part[:, : 2 * tile], part[:, 2 * tile :]


def side_gram(rows, side, refs, turned, high, low, add, tile):
    first = 2 * rows.side_pair(side) + COL0
    for r in range(2):
        for c in range(2 * SIDE):
            put(high, low, r, c, tile, rows.side(refs, side, r, first + c))
    left = halves(turned, 0, SIDE, tile)
    for b in range(SIDE):
        n = slice(2 * b * tile, (2 * b + 2) * tile)
        block = dot3(*left, flat(high, slice(0, 2), n), flat(low, slice(0, 2), n))
        for a in range(SIDE):
            add(a, b, block[2 * a * tile : (2 * a + 2) * tile])


def gram_kernel(meta, t_own, t_up, t_down, t_swap, p0, p1, pu, pd, x0, x1, gram, high, low, side_high, side_low):
    tile = p0.shape[-1]
    rows = Rows(meta)
    for r in range(2):
        for c in range(COLS):
            col = c + COL0
            put(high, low, r, c, tile, rows.own((p0, p1), r, col) if abs(col - r) <= REACH else zero(tile))
        for c in range(4):
            col = c + COL0
            value = rows.packed(pu, UP, -4, r, col) if abs(col - (r - 4)) <= REACH else zero(tile)
            put(high, low, 2 + r, c, tile, value)
            col = c + COL0 + 4
            value = rows.packed(pd, DOWN, 4, r, col) if abs(col - (r + 4)) <= REACH else zero(tile)
            put(high, low, 2 + r, 4 + c, tile, value)
    for b in range(PAIRS):
        n = slice(2 * b * tile, (2 * b + 2) * tile)
        first, last = max(0, b - 2), min(PAIRS, b + 3)
        block = dot3(*halves(t_own, first, last, tile), flat(high, slice(0, 2), n), flat(low, slice(0, 2), n))
        edge = dot3(
            *halves(t_up if b < 2 else t_down, 0, 2, tile), flat(high, slice(2, 4), n), flat(low, slice(2, 4), n)
        )
        for a in range(first, last):
            value = block[2 * (a - first) * tile : 2 * (a - first + 1) * tile]
            e = a if b < 2 else a - 2
            if 0 <= e < 2:
                value = value + edge[2 * e * tile : (2 * e + 2) * tile]
            gram[PAIRS * a + b] = value

    def add(a, b, value):
        index = PAIRS * a + b + (PAIRS + 1) * rows.side_pair(0)
        gram[index] = gram[index] + value

    side_gram(rows, 0, (x0, x1), t_swap, side_high, side_low, add, tile)


def refine_kernel(
    meta, z, z_own, t_near, t_far, early, n0, n1, fu, fd, refined, correction,
    high, low, far_high, far_low, late, d_high, d_low, dense, z_high, z_low,
):
    tile = z.shape[-1]
    rows = Rows(meta)

    def add(a, b, value):
        late[SIDE * a + b] = value

    side_gram(rows, 1, (n0, n1), t_near, high, low, add, tile)
    for r in range(2):
        for c in range(2):
            col = c + COL0
            value = rows.packed(fu, FAR_UP, -6, r, col) if abs(col - (r - 6)) <= REACH else zero(tile)
            put(far_high, far_low, r, c, tile, value)
            col = c + COL0 + 6
            value = rows.packed(fd, FAR_DOWN, 6, r, col) if abs(col - (r + 6)) <= REACH else zero(tile)
            put(far_high, far_low, r, 2 + c, tile, value)
    far = []
    for e in range(2):
        n = slice(2 * e * tile, (2 * e + 2) * tile)
        far.append(
            dot3(*halves(t_far, e, e + 1, tile), flat(far_high, slice(0, 2), n), flat(far_low, slice(0, 2), n))
        )
    eye = (
        lax.broadcasted_iota(jnp.int32, (tile, tile), 0) == lax.broadcasted_iota(jnp.int32, (tile, tile), 1)
    ).astype(F32)
    shift = rows.side_pair(1)
    for a in range(PAIRS):
        for b in range(PAIRS):
            if abs(a - b) > 2:
                continue
            gram = early[PAIRS * a + b]
            ia, ib = a - shift, b - shift
            there = (ia >= 0) & (ia < SIDE) & (ib >= 0) & (ib < SIDE)
            gram = gram + jnp.where(there, late[jnp.clip(SIDE * ia + ib, 0, SIDE * SIDE - 1)], 0.0)
            if a == b and a in (0, PAIRS - 1):
                gram = gram + far[0 if a == 0 else 1]
            for i in range(2):
                for j in range(2):
                    k, c = 2 * a + i, 2 * b + j
                    value = -gram[i * tile : (i + 1) * tile, j * tile : (j + 1) * tile]
                    if k == c:
                        value = value + eye
                    elif abs(k - c) <= REACH:
                        value = jnp.where(rows.present(k + COL0, c + COL0), value, 0.0)
                    else:
                        value = zero(tile)
                    put(d_high, d_low, k, c, tile, value)
                    if k + COL0 in (0, 1):
                        dense[k + COL0, c] = value
    for i in range(OWN):
        for slot in range(2 * REACH):
            correction[i, slot] = dense[i, rows.dense_slot(i, slot)]
    half = COLS * tile
    z_high[...] = z_own[:, :, :half]
    z_low[...] = z_own[:, :, half:]
    row_matmul(z_high, z_low, d_high, d_low, dense, tile)
    for i in range(OWN):
        for slot in range(2 * REACH):
            refined[i, slot] = z[i, slot] + 0.5 * dense[i, rows.dense_slot(i, slot)]


def far(rows):
    first = lax.optimization_barrier(
        jnp.concatenate([rows[0][0, s : s + 1] for r, s in FAR_UP + FAR_DOWN if r == 0], axis=0)
    )
    last = [rows[1][0, s : s + 1] for r, s in FAR_UP + FAR_DOWN if r == 1]
    return jnp.concatenate([first[:1], *last[:2]], axis=0), jnp.concatenate([first[1:], last[2]], axis=0)


def body(correlation, factor, pattern):
    rows_here, slots, tile = correlation.shape[:3]
    total = pattern.shape[0]
    assert rows_here == OWN and slots == 2 * REACH and total >= WIDE
    device = lax.axis_index(AXES)
    rows = (device * OWN + jnp.arange(LEFT, LEFT + WIDE, dtype=jnp.int32)) % total
    offsets = (pattern[rows][:, 1:] - rows[:, None] + total // 2) % total - total // 2
    expected = jnp.array([-3, -2, -1, 1, 2], jnp.int32)
    dropped = jnp.sum((offsets == expected).astype(jnp.int32), axis=1)
    meta = jnp.concatenate([dropped, (device % 2)[None]]).astype(jnp.int32)

    vmem = pl.BlockSpec(memory_space=pltpu.VMEM)
    smem = pl.BlockSpec(memory_space=pltpu.SMEM)

    def call(kernel, ins, outs, scratch, flops, scalars=1):
        return pl.pallas_call(
            kernel,
            in_specs=[smem] * scalars + [vmem] * (len(ins) - scalars),
            out_specs=jax.tree.map(lambda _: vmem, outs),
            out_shape=outs,
            scratch_shapes=scratch,
            compiler_params=pltpu.CompilerParams(vmem_limit_bytes=VMEM_LIMIT),
            cost_estimate=pl.CostEstimate(flops=flops, bytes_accessed=4 << 20, transcendentals=0),
        )(*ins[:scalars], *(pltpu.with_memory_space_constraint(v, pltpu.VMEM) for v in ins[scalars:]))

    def shape(*dims, dtype=F32):
        return jax.ShapeDtypeStruct(dims, dtype)

    def halves_of(n, m):
        return [pltpu.VMEM((n, tile, m * tile), BF16)] * 2

    row = shape(1, slots, tile, tile)
    seven = shape(len(UP), tile, tile)
    dense = pltpu.VMEM((OWN, COLS, tile, tile), F32)

    x = [send(factor[r : r + 1], swap) for r in range(OWN)]
    zu, zd = call(pack_kernel, (factor,), (seven, seven), [], 1000, 0)
    zu, zd = send(zu, up), send(zd, down)
    n = [send(x[r], near) for r in range(OWN)]
    zfu, zfd = far(x)
    zfu, zfd = send(zfu, far_up), send(zfd, far_down)
    p0, p1, pu, pd = call(
        product_kernel,
        (meta, correlation, factor, *x, *n, zu, zd),
        (row, row, seven, seven),
        halves_of(COLS, COLS) + halves_of(OWN, COLS) + [dense],
        int(2e9),
    )
    px = [send(v, swap) for v in (p0, p1)]
    pu, pd = send(pu, up), send(pd, down)
    pn = [send(v, near) for v in px]
    pfu, pfd = far(px)
    pfu, pfd = send(pfu, far_up), send(pfd, far_down)

    def turned(columns):
        return shape(columns * tile, 4 * tile, dtype=BF16)

    t_own, t_up, t_down, t_swap, t_near, t_far, z_own = call(
        turn_kernel,
        (meta, factor, *x, *n, zu, zd, zfu, zfd),
        (turned(COLS), turned(4), turned(4), turned(2 * SIDE), turned(2 * SIDE), turned(4),
         shape(OWN, tile, 2 * COLS * tile, dtype=BF16)),
        [],
        int(2e9),
    )
    early = call(
        gram_kernel,
        (meta, t_own, t_up, t_down, t_swap, p0, p1, pu, pd, *px),
        shape(PAIRS * PAIRS, 2 * tile, 2 * tile),
        halves_of(4, COLS) + halves_of(2, 2 * SIDE),
        int(4e9),
    )
    return call(
        refine_kernel,
        (meta, factor, z_own, t_near, t_far, early, *pn, pfu, pfd),
        (shape(*factor.shape), shape(*factor.shape)),
        halves_of(2, 2 * SIDE)
        + halves_of(2, 4)
        + [pltpu.VMEM((SIDE * SIDE, 2 * tile, 2 * tile), F32)]
        + halves_of(COLS, COLS)
        + [dense]
        + halves_of(OWN, COLS),
        int(4e9),
    )


def solution(mesh):
    tiles = P(AXES, None, None, None)

    return jax.shard_map(body, mesh=mesh, in_specs=(tiles, tiles, P()), out_specs=(tiles, tiles), check_vma=False)
```

```python
import jax
import jax.numpy as jnp
from jax import lax
from jax.experimental import pallas as pl
from jax.experimental.pallas import tpu as pltpu
from jax.sharding import PartitionSpec as P


REACH = 3
AXES = ("blk", "sub")
OWN = 2
LEFT = -2 * REACH
WIDE = OWN + 4 * REACH
COL0 = -REACH
COLS = OWN + 2 * REACH
PAIRS = COLS // 2
SIDE = 3
VMEM_LIMIT = 24 << 20
F32 = jnp.float32
BF16 = jnp.bfloat16

UP = ((0, 3), (0, 4), (0, 5), (1, 0), (1, 3), (1, 4), (1, 5))
DOWN = ((0, 0), (0, 1), (0, 2), (0, 3), (1, 1), (1, 2), (1, 3))
Z_UP = ((0, 0), (0, 3), (0, 4), (0, 5), (1, 0), (1, 2), (1, 3), (1, 4), (1, 5))
Z_DOWN = ((0, 0), (0, 1), (0, 2), (0, 3), (0, 4), (1, 0), (1, 1), (1, 2), (1, 3))
FAR_UP = ((0, 5), (1, 4), (1, 5))
FAR_DOWN = ((0, 1), (0, 2), (1, 1))


def send(value, to):
    count = lax.axis_size(AXES)
    return lax.ppermute(value, AXES, [(i, to(i) % count) for i in range(count)])


def swap(i):
    return i ^ 1


def up(i):
    return i + 2


def down(i):
    return i - 2


def near(i):
    return i + 2 if i % 2 == 0 else i - 2


def far_up(i):
    return i + 4 if i % 2 == 0 else i + 2


def far_down(i):
    return i - 2 if i % 2 == 0 else i - 4


def split(value):
    high = value.astype(BF16)
    low = (value - high.astype(F32)).astype(BF16)
    return high, low


def dot3(a_high, a_low, b_high, b_low):
    left = jnp.concatenate([a_high, a_low, a_high], axis=1)
    right = jnp.concatenate([b_high, b_high, b_low], axis=0)
    return jnp.dot(left, right, preferred_element_type=F32)


def slot_of(offset, dropped):
    pos = offset + REACH - jnp.where(offset > 0, 1, 0)
    slot = jnp.where(offset == 0, 0, pos + 1 - jnp.where(pos > dropped, 1, 0))
    there = (jnp.abs(offset) <= REACH) & ((offset == 0) | (pos != dropped))
    return jnp.clip(slot, 0, 2 * REACH - 1), there


class Rows:
    def __init__(self, meta):
        self.meta = meta
        self.parity = meta[WIDE]

    def dropped(self, row):
        return self.meta[row - LEFT]

    def side_row(self, side):
        return 2 - 4 * jnp.bitwise_xor(self.parity, side)

    def side_pair(self, side):
        return 1 - jnp.bitwise_xor(self.parity, side)

    def present(self, row, col):
        return slot_of(jnp.int32(col - row), self.dropped(row))[1]

    def own(self, refs, row, col):
        slot, there = slot_of(jnp.int32(col - row), self.dropped(row))
        tile = refs[row][0, slot] if isinstance(refs, tuple) else refs[row, slot]
        return jnp.where(there, tile, 0.0)

    def packed(self, ref, layout, row0, r, col):
        slots = [s for rr, s in layout if rr == r]
        base = [j for j, (rr, _) in enumerate(layout) if rr == r][0]
        row = row0 + r
        if col == row:
            return ref[base + slots.index(0)]
        slot, there = slot_of(jnp.int32(col - row), self.dropped(row))
        rest = [s for s in slots if s]
        index = base + slots.index(rest[0]) + jnp.clip(slot - rest[0], 0, len(rest) - 1)
        return jnp.where(there, ref[index], 0.0)

    def side(self, ref, side, r, col):
        row = self.side_row(side) + r
        slot, there = slot_of(col - row, self.dropped(row))
        return jnp.where(there, ref[0, slot], 0.0)

    def by_distance(self, refs):
        return tuple(zip(refs, (self.parity, 1 - self.parity)))

    def dense_slot(self, row, slot):
        if slot == 0:
            return row - COL0
        pos = slot - 1 + jnp.where(slot - 1 >= self.dropped(row), 1, 0)
        return row - COL0 - REACH + pos + jnp.where(pos >= REACH, 1, 0)


def zero(tile):
    return jnp.zeros((tile, tile), F32)


def put(high, low, r, c, tile, value):
    h, l = split(value)
    high[r, :, c * tile : (c + 1) * tile] = h
    low[r, :, c * tile : (c + 1) * tile] = l


def flat(ref, rows, cols):
    value = ref[rows, :, cols]
    return value.reshape(value.shape[0] * value.shape[1], value.shape[2])


def row_matmul(left_high, left_low, right_high, right_low, out, tile):
    for c in range(0, COLS, 2):
        lo, hi = max(c - REACH, 0), min(c + 1 + REACH, COLS - 1) + 1
        k = slice(lo * tile, hi * tile)
        n = slice(c * tile, (c + 2) * tile)
        block = dot3(
            flat(left_high, slice(None), k),
            flat(left_low, slice(None), k),
            flat(right_high, slice(lo, hi), n),
            flat(right_low, slice(lo, hi), n),
        )
        for i in range(OWN):
            for j in range(2):
                out[i, c + j] = block[i * tile : (i + 1) * tile, j * tile : (j + 1) * tile]


def pack_kernel(z, zu, zd):
    for out, layout in ((zu, Z_UP), (zd, Z_DOWN)):
        for j, (i, slot) in enumerate(layout):
            out[j] = z[i, slot]


def far_kernel(meta, nearer, farther, fu, fd):
    even = meta[WIDE] == 0
    for out, layout in ((fu, FAR_UP), (fd, FAR_DOWN)):
        for j, (r, slot) in enumerate(layout):
            a, b = (nearer, farther) if r == 0 else (farther, nearer)
            out[j] = jnp.where(even, a[0, slot], b[0, slot])


def product_kernel(meta, s, z, x0, x1, n0, n1, zu, zd, p0, p1, pf, pu, pd, z_high, z_low, s_high, s_low, dense):
    tile = s.shape[-1]
    rows = Rows(meta)
    for c in range(COLS):
        col = c + COL0
        for i in range(OWN):
            near_by = abs(col - i) <= REACH
            put(s_high, s_low, i, c, tile, rows.own(s, i, col) if near_by else zero(tile))
            put(z_high, z_low, i - COL0, c, tile, rows.own(z, i, col) if near_by else zero(tile))
        for side, refs in enumerate(((x0, x1), (n0, n1))):
            for r in range(2):
                where = rows.side_row(side) + r - COL0
                put(z_high, z_low, where, c, tile, rows.side(refs[r], side, r, col))
        row = -REACH
        put(z_high, z_low, 0, c, tile, rows.packed(zu, Z_UP, -4, 1, col) if abs(col - row) <= REACH else zero(tile))
        row = OWN - 1 + REACH
        put(z_high, z_low, COLS - 1, c, tile, rows.packed(zd, Z_DOWN, 4, 0, col) if abs(col - row) <= REACH else zero(tile))
    row_matmul(s_high, s_low, z_high, z_low, dense, tile)
    for i, ref in enumerate((p0, p1)):
        for slot in range(2 * REACH):
            ref[0, slot] = dense[i, rows.dense_slot(i, slot)]
    for slot in range(2 * REACH):
        pf[0, slot] = dense[rows.parity, rows.dense_slot(rows.parity, slot)]
    for ref, layout in ((pu, UP), (pd, DOWN)):
        for j, (i, slot) in enumerate(layout):
            ref[j] = dense[i, rows.dense_slot(i, slot)]


def side_kernel(meta, s, z, x0, x1, n0, n1, zu, zd, out, z_high, z_low, s_high, s_low, dense):
    tile = s.shape[-1]
    rows = Rows(meta)
    width = 2 * REACH + 1

    def own():
        return lambda row, col: rows.own(z, row, col)

    def swapped(r):
        return lambda row, col: rows.side((x0, x1)[r], 0, r, col)

    def relayed(r):
        return lambda row, col: rows.side((n0, n1)[r], 1, r, col)

    def from_down(r):
        return lambda row, col: rows.packed(zu, Z_UP, -4, r, col)

    def from_up(r):
        return lambda row, col: rows.packed(zd, Z_DOWN, 4, r, col)

    even = (relayed(1), own(), own(), swapped(0), swapped(1), from_up(0), from_up(1))
    odd = (from_down(0), from_down(1), swapped(0), swapped(1), own(), own(), relayed(0))
    for parity, sources in ((0, even), (1, odd)):

        @pl.when(rows.parity == parity)
        def _():
            centre = OWN if parity == 0 else -1
            first = centre - REACH
            for k in range(width):
                for c in range(width):
                    there = abs(k - c) <= REACH
                    put(z_high, z_low, k, c, tile, sources[k](first + k, first + c) if there else zero(tile))

    centre = jnp.where(rows.parity == 0, OWN, -1)
    dropped = rows.dropped(centre)
    for c in range(width):
        slot, there = slot_of(jnp.int32(c - REACH), dropped)
        put(s_high, s_low, 0, c, tile, jnp.where(there, s[0, slot], 0.0))
    for c in range(0, width, 2):
        last = min(c + 2, width)
        lo, hi = max(c - REACH, 0), min(last - 1 + REACH, width - 1) + 1
        n = slice(c * tile, last * tile)
        k = slice(lo * tile, hi * tile)
        block = dot3(
            flat(s_high, slice(None), k),
            flat(s_low, slice(None), k),
            flat(z_high, slice(lo, hi), n),
            flat(z_low, slice(lo, hi), n),
        )
        for j in range(last - c):
            dense[c + j] = block[:, j * tile : (j + 1) * tile]
    for slot in range(2 * REACH):
        pos = slot - 1 + jnp.where(slot - 1 >= dropped, 1, 0)
        out[0, slot] = dense[REACH if slot == 0 else pos + jnp.where(pos >= REACH, 1, 0)]


def turn_kernel(meta, z, x0, x1, n0, n1, zu, zd, fu, fd, t_own, t_up, t_down, t_swap, t_near, t_far, z_own):
    tile = z.shape[-1]
    rows = Rows(meta)

    def store(out, c, r, value):
        high, low = split(value.T)
        out[c * tile : (c + 1) * tile, r * tile : (r + 1) * tile] = high
        out[c * tile : (c + 1) * tile, (2 + r) * tile : (3 + r) * tile] = low

    for r in range(2):
        for c in range(COLS):
            col = c + COL0
            value = rows.own(z, r, col) if abs(col - r) <= REACH else zero(tile)
            store(t_own, c, r, value)
            high, low = split(value)
            z_own[r, :, c * tile : (c + 1) * tile] = high
            z_own[r, :, (COLS + c) * tile : (COLS + c + 1) * tile] = low
        for c in range(4):
            col = c + COL0
            store(t_up, c, r, rows.packed(zu, Z_UP, -4, r, col) if abs(col - (r - 4)) <= REACH else zero(tile))
            col = c + COL0 + 4
            store(t_down, c, r, rows.packed(zd, Z_DOWN, 4, r, col) if abs(col - (r + 4)) <= REACH else zero(tile))
        for c in range(2):
            col = c + COL0
            store(t_far, c, r, rows.packed(fu, FAR_UP, -6, r, col) if abs(col - (r - 6)) <= REACH else zero(tile))
            col = c + COL0 + 6
            store(t_far, 2 + c, r, rows.packed(fd, FAR_DOWN, 6, r, col) if abs(col - (r + 6)) <= REACH else zero(tile))
        for side, (out, refs) in enumerate(((t_swap, (x0, x1)), (t_near, (n0, n1)))):
            first = 2 * rows.side_pair(side) + COL0
            for c in range(2 * SIDE):
                store(out, c, r, rows.side(refs[r], side, r, first + c))


def halves(turned, first, last, tile):
    part = turned[2 * first * tile : 2 * last * tile]
    return part[:, : 2 * tile], part[:, 2 * tile :]


def side_gram(rows, side, refs, turned, high, low, add, tile):
    first = 2 * rows.side_pair(side) + COL0
    for ref, r in rows.by_distance(refs):
        for c in range(2 * SIDE):
            put(high, low, r, c, tile, rows.side(ref, side, r, first + c))
    left = halves(turned, 0, SIDE, tile)
    for b in range(SIDE):
        n = slice(2 * b * tile, (2 * b + 2) * tile)
        block = dot3(*left, flat(high, slice(0, 2), n), flat(low, slice(0, 2), n))
        for a in range(SIDE):
            add(a, b, block[2 * a * tile : (2 * a + 2) * tile])


def gram_kernel(meta, t_own, t_up, t_down, t_swap, p0, p1, pu, pd, nearer, farther, gram, high, low, side_high, side_low):
    tile = p0.shape[-1]
    rows = Rows(meta)
    for r in range(2):
        for c in range(COLS):
            col = c + COL0
            put(high, low, r, c, tile, rows.own((p0, p1), r, col) if abs(col - r) <= REACH else zero(tile))
        for c in range(4):
            col = c + COL0
            value = rows.packed(pu, UP, -4, r, col) if abs(col - (r - 4)) <= REACH else zero(tile)
            put(high, low, 2 + r, c, tile, value)
            col = c + COL0 + 4
            value = rows.packed(pd, DOWN, 4, r, col) if abs(col - (r + 4)) <= REACH else zero(tile)
            put(high, low, 2 + r, 4 + c, tile, value)
    for b in range(PAIRS):
        n = slice(2 * b * tile, (2 * b + 2) * tile)
        first, last = max(0, b - 2), min(PAIRS, b + 3)
        block = dot3(*halves(t_own, first, last, tile), flat(high, slice(0, 2), n), flat(low, slice(0, 2), n))
        edge = dot3(
            *halves(t_up if b < 2 else t_down, 0, 2, tile), flat(high, slice(2, 4), n), flat(low, slice(2, 4), n)
        )
        for a in range(first, last):
            value = block[2 * (a - first) * tile : 2 * (a - first + 1) * tile]
            e = a if b < 2 else a - 2
            if 0 <= e < 2:
                value = value + edge[2 * e * tile : (2 * e + 2) * tile]
            gram[PAIRS * a + b] = value

    def add(a, b, value):
        index = PAIRS * a + b + (PAIRS + 1) * rows.side_pair(0)
        gram[index] = gram[index] + value

    side_gram(rows, 0, (nearer, farther), t_swap, side_high, side_low, add, tile)


def refine_kernel(
    meta, z, z_own, t_near, t_far, early, nearer, farther, fu, fd, refined, correction,
    high, low, far_high, far_low, late, d_high, d_low, dense, z_high, z_low,
):
    tile = z.shape[-1]
    rows = Rows(meta)

    def add(a, b, value):
        late[SIDE * a + b] = value

    side_gram(rows, 1, (nearer, farther), t_near, high, low, add, tile)
    for r in range(2):
        for c in range(2):
            col = c + COL0
            value = rows.packed(fu, FAR_UP, -6, r, col) if abs(col - (r - 6)) <= REACH else zero(tile)
            put(far_high, far_low, r, c, tile, value)
            col = c + COL0 + 6
            value = rows.packed(fd, FAR_DOWN, 6, r, col) if abs(col - (r + 6)) <= REACH else zero(tile)
            put(far_high, far_low, r, 2 + c, tile, value)
    far = []
    for e in range(2):
        n = slice(2 * e * tile, (2 * e + 2) * tile)
        far.append(
            dot3(*halves(t_far, e, e + 1, tile), flat(far_high, slice(0, 2), n), flat(far_low, slice(0, 2), n))
        )
    eye = (
        lax.broadcasted_iota(jnp.int32, (tile, tile), 0) == lax.broadcasted_iota(jnp.int32, (tile, tile), 1)
    ).astype(F32)
    shift = rows.side_pair(1)
    for a in range(PAIRS):
        for b in range(PAIRS):
            if abs(a - b) > 2:
                continue
            gram = early[PAIRS * a + b]
            ia, ib = a - shift, b - shift
            there = (ia >= 0) & (ia < SIDE) & (ib >= 0) & (ib < SIDE)
            gram = gram + jnp.where(there, late[jnp.clip(SIDE * ia + ib, 0, SIDE * SIDE - 1)], 0.0)
            if a == b and a in (0, PAIRS - 1):
                gram = gram + far[0 if a == 0 else 1]
            for i in range(2):
                for j in range(2):
                    k, c = 2 * a + i, 2 * b + j
                    value = -gram[i * tile : (i + 1) * tile, j * tile : (j + 1) * tile]
                    if k == c:
                        value = value + eye
                    elif abs(k - c) <= REACH:
                        value = jnp.where(rows.present(k + COL0, c + COL0), value, 0.0)
                    else:
                        value = zero(tile)
                    put(d_high, d_low, k, c, tile, value)
                    if k + COL0 in (0, 1):
                        dense[k + COL0, c] = value
    for i in range(OWN):
        for slot in range(2 * REACH):
            correction[i, slot] = dense[i, rows.dense_slot(i, slot)]
    half = COLS * tile
    z_high[...] = z_own[:, :, :half]
    z_low[...] = z_own[:, :, half:]
    row_matmul(z_high, z_low, d_high, d_low, dense, tile)
    for i in range(OWN):
        for slot in range(2 * REACH):
            refined[i, slot] = z[i, slot] + 0.5 * dense[i, rows.dense_slot(i, slot)]


def far(rows):
    first = lax.optimization_barrier(
        jnp.concatenate([rows[0][0, s : s + 1] for r, s in FAR_UP + FAR_DOWN if r == 0], axis=0)
    )
    last = [rows[1][0, s : s + 1] for r, s in FAR_UP + FAR_DOWN if r == 1]
    return jnp.concatenate([first[:1], *last[:2]], axis=0), jnp.concatenate([first[1:], last[2]], axis=0)


def body(correlation, factor, pattern):
    rows_here, slots, tile = correlation.shape[:3]
    total = pattern.shape[0]
    assert rows_here == OWN and slots == 2 * REACH and total >= WIDE
    device = lax.axis_index(AXES)
    rows = (device * OWN + jnp.arange(LEFT, LEFT + WIDE, dtype=jnp.int32)) % total
    offsets = (pattern[rows][:, 1:] - rows[:, None] + total // 2) % total - total // 2
    expected = jnp.array([-3, -2, -1, 1, 2], jnp.int32)
    dropped = jnp.sum((offsets == expected).astype(jnp.int32), axis=1)
    meta = jnp.concatenate([dropped, (device % 2)[None]]).astype(jnp.int32)

    vmem = pl.BlockSpec(memory_space=pltpu.VMEM)
    smem = pl.BlockSpec(memory_space=pltpu.SMEM)

    def call(kernel, ins, outs, scratch, flops, scalars=1):
        return pl.pallas_call(
            kernel,
            in_specs=[smem] * scalars + [vmem] * (len(ins) - scalars),
            out_specs=jax.tree.map(lambda _: vmem, outs),
            out_shape=outs,
            scratch_shapes=scratch,
            compiler_params=pltpu.CompilerParams(vmem_limit_bytes=VMEM_LIMIT),
            cost_estimate=pl.CostEstimate(flops=flops, bytes_accessed=4 << 20, transcendentals=0),
        )(*ins[:scalars], *(pltpu.with_memory_space_constraint(v, pltpu.VMEM) for v in ins[scalars:]))

    def shape(*dims, dtype=F32):
        return jax.ShapeDtypeStruct(dims, dtype)

    def halves_of(n, m):
        return [pltpu.VMEM((n, tile, m * tile), BF16)] * 2

    row = shape(1, slots, tile, tile)
    seven = shape(len(UP), tile, tile)
    nine = shape(len(Z_UP), tile, tile)
    three = shape(len(FAR_UP), tile, tile)
    parity = device % 2
    dense = pltpu.VMEM((OWN, COLS, tile, tile), F32)

    x = [send(factor[r : r + 1], swap) for r in range(OWN)]
    zu, zd = call(pack_kernel, (factor,), (nine, nine), [], 1000, 0)
    zu, zd = send(zu, up), send(zd, down)
    n = [send(x[r], near) for r in range(OWN)]
    sx = send(lax.dynamic_slice_in_dim(correlation, 1 - parity, 1, 0), swap)
    zfu, zfd = far(x)
    zfu, zfd = send(zfu, far_up), send(zfd, far_down)
    p0, p1, pf, pu, pd = call(
        product_kernel,
        (meta, correlation, factor, *x, *n, zu, zd),
        (row, row, row, seven, seven),
        halves_of(COLS, COLS) + halves_of(OWN, COLS) + [dense],
        int(2e9),
    )
    px = send(pf, swap)
    pu, pd = send(pu, up), send(pd, down)
    width = 2 * REACH + 1
    ps = call(
        side_kernel,
        (meta, sx, factor, *x, *n, zu, zd),
        row,
        halves_of(width, width) + halves_of(1, width) + [pltpu.VMEM((width, tile, tile), F32)],
        int(2e9),
    )
    pn = (send(ps, near), send(px, near))
    pfu, pfd = call(far_kernel, (meta, ps, px), (three, three), [], 1000)
    pfu, pfd = send(pfu, far_up), send(pfd, far_down)

    def turned(columns):
        return shape(columns * tile, 4 * tile, dtype=BF16)

    t_own, t_up, t_down, t_swap, t_near, t_far, z_own = call(
        turn_kernel,
        (meta, factor, *x, *n, zu, zd, zfu, zfd),
        (turned(COLS), turned(4), turned(4), turned(2 * SIDE), turned(2 * SIDE), turned(4),
         shape(OWN, tile, 2 * COLS * tile, dtype=BF16)),
        [],
        int(2e9),
    )
    early = call(
        gram_kernel,
        (meta, t_own, t_up, t_down, t_swap, p0, p1, pu, pd, ps, px),
        shape(PAIRS * PAIRS, 2 * tile, 2 * tile),
        halves_of(4, COLS) + halves_of(2, 2 * SIDE),
        int(4e9),
    )
    return call(
        refine_kernel,
        (meta, factor, z_own, t_near, t_far, early, *pn, pfu, pfd),
        (shape(*factor.shape), shape(*factor.shape)),
        halves_of(2, 2 * SIDE)
        + halves_of(2, 4)
        + [pltpu.VMEM((SIDE * SIDE, 2 * tile, 2 * tile), F32)]
        + halves_of(COLS, COLS)
        + [dense]
        + halves_of(OWN, COLS),
        int(4e9),
    )


def solution(mesh):
    tiles = P(AXES, None, None, None)

    return jax.shard_map(body, mesh=mesh, in_specs=(tiles, tiles, P()), out_specs=(tiles, tiles), check_vma=False)
```

```python
import jax
import jax.numpy as jnp
from jax import lax
from jax.experimental import pallas as pl
from jax.experimental.pallas import tpu as pltpu
from jax.sharding import PartitionSpec as P


REACH = 3
AXES = ("blk", "sub")
OWN = 2
LEFT = -2 * REACH
WIDE = OWN + 4 * REACH
COL0 = -REACH
COLS = OWN + 2 * REACH
PAIRS = COLS // 2
SIDE = 3
VMEM_LIMIT = 24 << 20
F32 = jnp.float32
BF16 = jnp.bfloat16

UP = ((0, 3), (0, 4), (0, 5), (1, 0), (1, 3), (1, 4), (1, 5))
DOWN = ((0, 0), (0, 1), (0, 2), (0, 3), (1, 1), (1, 2), (1, 3))
Z_UP = ((0, 0), (0, 3), (0, 4), (0, 5), (1, 0), (1, 2), (1, 3), (1, 4), (1, 5))
Z_DOWN = ((0, 0), (0, 1), (0, 2), (0, 3), (0, 4), (1, 0), (1, 1), (1, 2), (1, 3))


def send(value, to):
    count = lax.axis_size(AXES)
    return lax.ppermute(value, AXES, [(i, to(i) % count) for i in range(count)])


def swap(i):
    return i ^ 1


def inside(i):
    return i ^ 2


def across(i):
    return i + 2 if i // 2 % 2 else i - 2


def near(i):
    return i + 2 if i % 2 == 0 else i - 2


def far_up(i):
    return i + 4 if i % 2 == 0 else i + 2


def far_down(i):
    return i - 2 if i % 2 == 0 else i - 4


def split(value):
    high = value.astype(BF16)
    low = (value - high.astype(F32)).astype(BF16)
    return high, low


def dot3(a_high, a_low, b_high, b_low):
    left = jnp.concatenate([a_high, a_low, a_high], axis=1)
    right = jnp.concatenate([b_high, b_high, b_low], axis=0)
    return jnp.dot(left, right, preferred_element_type=F32)


def slot_of(offset, dropped):
    pos = offset + REACH - jnp.where(offset > 0, 1, 0)
    slot = jnp.where(offset == 0, 0, pos + 1 - jnp.where(pos > dropped, 1, 0))
    there = (jnp.abs(offset) <= REACH) & ((offset == 0) | (pos != dropped))
    return jnp.clip(slot, 0, 2 * REACH - 1), there


class Rows:
    def __init__(self, meta):
        self.meta = meta
        self.parity = meta[WIDE]
        self.even_pair = meta[WIDE + 1] == 0

    def dropped(self, row):
        return self.meta[row - LEFT]

    def side_row(self, side):
        return 2 - 4 * jnp.bitwise_xor(self.parity, side)

    def side_pair(self, side):
        return 1 - jnp.bitwise_xor(self.parity, side)

    def present(self, row, col):
        return slot_of(jnp.int32(col - row), self.dropped(row))[1]

    def own(self, refs, row, col):
        slot, there = slot_of(jnp.int32(col - row), self.dropped(row))
        tile = refs[row][0, slot] if isinstance(refs, tuple) else refs[row, slot]
        return jnp.where(there, tile, 0.0)

    def packed(self, refs, layout, row0, r, col):
        slots = [s for rr, s in layout if rr == r]
        base = [j for j, (rr, _) in enumerate(layout) if rr == r][0]
        row = row0 + r
        if col == row:
            index = base + slots.index(0)
            return jnp.where(self.even_pair, refs[0][index], refs[1][index])
        slot, there = slot_of(jnp.int32(col - row), self.dropped(row))
        rest = [s for s in slots if s]
        index = base + slots.index(rest[0]) + jnp.clip(slot - rest[0], 0, len(rest) - 1)
        return jnp.where(there, jnp.where(self.even_pair, refs[0][index], refs[1][index]), 0.0)

    def side(self, ref, side, r, col):
        row = self.side_row(side) + r
        slot, there = slot_of(col - row, self.dropped(row))
        return jnp.where(there, ref[0, slot], 0.0)

    def by_distance(self, refs):
        return tuple(zip(refs, (self.parity, 1 - self.parity)))

    def dense_slot(self, row, slot):
        if slot == 0:
            return row - COL0
        pos = slot - 1 + jnp.where(slot - 1 >= self.dropped(row), 1, 0)
        return row - COL0 - REACH + pos + jnp.where(pos >= REACH, 1, 0)


def zero(tile):
    return jnp.zeros((tile, tile), F32)


def put(high, low, r, c, tile, value):
    h, l = split(value)
    high[r, :, c * tile : (c + 1) * tile] = h
    low[r, :, c * tile : (c + 1) * tile] = l


def flat(ref, rows, cols):
    value = ref[rows, :, cols]
    return value.reshape(value.shape[0] * value.shape[1], value.shape[2])


def row_matmul(left_high, left_low, right_high, right_low, out, tile):
    for c in range(0, COLS, 2):
        lo, hi = max(c - REACH, 0), min(c + 1 + REACH, COLS - 1) + 1
        k = slice(lo * tile, hi * tile)
        n = slice(c * tile, (c + 2) * tile)
        block = dot3(
            flat(left_high, slice(None), k),
            flat(left_low, slice(None), k),
            flat(right_high, slice(lo, hi), n),
            flat(right_low, slice(lo, hi), n),
        )
        for i in range(OWN):
            for j in range(2):
                out[i, c + j] = block[i * tile : (i + 1) * tile, j * tile : (j + 1) * tile]


def both(layouts, tile_of, rows, chip, link):
    for j, (first, second) in enumerate(zip(*layouts)):
        a, b = tile_of(*first), tile_of(*second)
        chip[j] = jnp.where(rows.even_pair, a, b)
        link[j] = jnp.where(rows.even_pair, b, a)


def pack_kernel(meta, z, z0, z1, chip, link):
    for r, out in enumerate((z0, z1)):
        for slot in range(2 * REACH):
            out[0, slot] = z[r, slot]
    both((Z_UP, Z_DOWN), lambda i, slot: z[i, slot], Rows(meta), chip, link)


def far_tile(rows, refs, sign, r, c, tile):
    if sign > 0:
        offset = REACH - c if r == 0 else REACH - 1 + c
        there = r == 1 or c == 0
    else:
        offset = -REACH + c if r == 0 else -REACH + 1 - c
        there = r == 0 or c == 1
    if not there:
        return zero(tile)
    slot, present = slot_of(jnp.int32(offset), rows.dropped(rows.side_row(0) + r))
    if len(refs) == 1:
        value = refs[0][0, slot]
    else:
        a, b = refs if r == 0 else refs[::-1]
        value = jnp.where(rows.parity == 0, a[0, slot], b[0, slot])
    return jnp.where(present, value, 0.0)


def far_kernel(meta, t_up, t_down, nearer, farther, up, down, high, low):
    tile = nearer.shape[-1]
    rows = Rows(meta)
    for turned, sign, out in ((t_up, 1, up), (t_down, -1, down)):
        c0 = 0 if sign > 0 else 2
        for r in range(2):
            for c in range(2):
                put(high, low, r, c0 + c, tile, far_tile(rows, (nearer, farther), sign, r, c, tile))
        n = slice(c0 * tile, (c0 + 2) * tile)
        out[...] = dot3(*halves(turned, 0, 1, tile), flat(high, slice(0, 2), n), flat(low, slice(0, 2), n))


def product_kernel(meta, s, z, x0, x1, n0, n1, zi, zc, p0, p1, pf, chip, link, z_high, z_low, s_high, s_low, dense):
    tile = s.shape[-1]
    rows = Rows(meta)
    for c in range(COLS):
        col = c + COL0
        for i in range(OWN):
            near_by = abs(col - i) <= REACH
            put(s_high, s_low, i, c, tile, rows.own(s, i, col) if near_by else zero(tile))
            put(z_high, z_low, i - COL0, c, tile, rows.own(z, i, col) if near_by else zero(tile))
        for side, refs in enumerate(((x0, x1), (n0, n1))):
            for r in range(2):
                where = rows.side_row(side) + r - COL0
                put(z_high, z_low, where, c, tile, rows.side(refs[r], side, r, col))
        row = -REACH
        put(z_high, z_low, 0, c, tile, rows.packed((zc, zi), Z_UP, -4, 1, col) if abs(col - row) <= REACH else zero(tile))
        row = OWN - 1 + REACH
        put(z_high, z_low, COLS - 1, c, tile, rows.packed((zi, zc), Z_DOWN, 4, 0, col) if abs(col - row) <= REACH else zero(tile))
    row_matmul(s_high, s_low, z_high, z_low, dense, tile)
    for i, ref in enumerate((p0, p1)):
        for slot in range(2 * REACH):
            ref[0, slot] = dense[i, rows.dense_slot(i, slot)]
    for slot in range(2 * REACH):
        pf[0, slot] = dense[rows.parity, rows.dense_slot(rows.parity, slot)]
    both((UP, DOWN), lambda i, slot: dense[i, rows.dense_slot(i, slot)], rows, chip, link)


def side_kernel(meta, s, z, x0, x1, n0, n1, zi, zc, out, z_high, z_low, s_high, s_low, dense):
    tile = s.shape[-1]
    rows = Rows(meta)
    width = 2 * REACH + 1

    def own():
        return lambda row, col: rows.own(z, row, col)

    def swapped(r):
        return lambda row, col: rows.side((x0, x1)[r], 0, r, col)

    def relayed(r):
        return lambda row, col: rows.side((n0, n1)[r], 1, r, col)

    def from_down(r):
        return lambda row, col: rows.packed((zc, zi), Z_UP, -4, r, col)

    def from_up(r):
        return lambda row, col: rows.packed((zi, zc), Z_DOWN, 4, r, col)

    even = (relayed(1), own(), own(), swapped(0), swapped(1), from_up(0), from_up(1))
    odd = (from_down(0), from_down(1), swapped(0), swapped(1), own(), own(), relayed(0))
    for parity, sources in ((0, even), (1, odd)):

        @pl.when(rows.parity == parity)
        def _():
            centre = OWN if parity == 0 else -1
            first = centre - REACH
            for k in range(width):
                for c in range(width):
                    there = abs(k - c) <= REACH
                    put(z_high, z_low, k, c, tile, sources[k](first + k, first + c) if there else zero(tile))

    centre = jnp.where(rows.parity == 0, OWN, -1)
    dropped = rows.dropped(centre)
    for c in range(width):
        slot, there = slot_of(jnp.int32(c - REACH), dropped)
        put(s_high, s_low, 0, c, tile, jnp.where(there, s[0, slot], 0.0))
    for c in range(0, width, 2):
        last = min(c + 2, width)
        lo, hi = max(c - REACH, 0), min(last - 1 + REACH, width - 1) + 1
        n = slice(c * tile, last * tile)
        k = slice(lo * tile, hi * tile)
        block = dot3(
            flat(s_high, slice(None), k),
            flat(s_low, slice(None), k),
            flat(z_high, slice(lo, hi), n),
            flat(z_low, slice(lo, hi), n),
        )
        for j in range(last - c):
            dense[c + j] = block[:, j * tile : (j + 1) * tile]
    for slot in range(2 * REACH):
        pos = slot - 1 + jnp.where(slot - 1 >= dropped, 1, 0)
        out[0, slot] = dense[REACH if slot == 0 else pos + jnp.where(pos >= REACH, 1, 0)]


def turn_kernel(meta, z, x0, x1, n0, n1, zi, zc, t_own, t_up, t_down, t_swap, t_near, t_far_up, t_far_down, z_own):
    tile = z.shape[-1]
    rows = Rows(meta)

    def store(out, c, r, value):
        high, low = split(value.T)
        out[c * tile : (c + 1) * tile, r * tile : (r + 1) * tile] = high
        out[c * tile : (c + 1) * tile, (2 + r) * tile : (3 + r) * tile] = low

    for r in range(2):
        for c in range(COLS):
            col = c + COL0
            value = rows.own(z, r, col) if abs(col - r) <= REACH else zero(tile)
            store(t_own, c, r, value)
            high, low = split(value)
            z_own[r, :, c * tile : (c + 1) * tile] = high
            z_own[r, :, (COLS + c) * tile : (COLS + c + 1) * tile] = low
        for c in range(4):
            col = c + COL0
            store(t_up, c, r, rows.packed((zc, zi), Z_UP, -4, r, col) if abs(col - (r - 4)) <= REACH else zero(tile))
            col = c + COL0 + 4
            store(t_down, c, r, rows.packed((zi, zc), Z_DOWN, 4, r, col) if abs(col - (r + 4)) <= REACH else zero(tile))
        for c in range(2):
            store(t_far_up, c, r, far_tile(rows, ((x0, x1)[r],), 1, r, c, tile))
            store(t_far_down, c, r, far_tile(rows, ((x0, x1)[r],), -1, r, c, tile))
        for side, (out, refs) in enumerate(((t_swap, (x0, x1)), (t_near, (n0, n1)))):
            first = 2 * rows.side_pair(side) + COL0
            for c in range(2 * SIDE):
                store(out, c, r, rows.side(refs[r], side, r, first + c))


def halves(turned, first, last, tile):
    part = turned[2 * first * tile : 2 * last * tile]
    return part[:, : 2 * tile], part[:, 2 * tile :]


def side_gram(rows, side, refs, turned, high, low, add, tile):
    first = 2 * rows.side_pair(side) + COL0
    for ref, r in rows.by_distance(refs):
        for c in range(2 * SIDE):
            put(high, low, r, c, tile, rows.side(ref, side, r, first + c))
    left = halves(turned, 0, SIDE, tile)
    for b in range(SIDE):
        n = slice(2 * b * tile, (2 * b + 2) * tile)
        block = dot3(*left, flat(high, slice(0, 2), n), flat(low, slice(0, 2), n))
        for a in range(SIDE):
            add(a, b, block[2 * a * tile : (2 * a + 2) * tile])


def gram_kernel(meta, t_own, t_up, t_down, t_swap, p0, p1, pi, pc, nearer, farther, gram, high, low, side_high, side_low):
    tile = p0.shape[-1]
    rows = Rows(meta)
    for r in range(2):
        for c in range(COLS):
            col = c + COL0
            put(high, low, r, c, tile, rows.own((p0, p1), r, col) if abs(col - r) <= REACH else zero(tile))
        for c in range(4):
            col = c + COL0
            value = rows.packed((pc, pi), UP, -4, r, col) if abs(col - (r - 4)) <= REACH else zero(tile)
            put(high, low, 2 + r, c, tile, value)
            col = c + COL0 + 4
            value = rows.packed((pi, pc), DOWN, 4, r, col) if abs(col - (r + 4)) <= REACH else zero(tile)
            put(high, low, 2 + r, 4 + c, tile, value)
    for b in range(PAIRS):
        n = slice(2 * b * tile, (2 * b + 2) * tile)
        first, last = max(0, b - 2), min(PAIRS, b + 3)
        block = dot3(*halves(t_own, first, last, tile), flat(high, slice(0, 2), n), flat(low, slice(0, 2), n))
        edge = dot3(
            *halves(t_up if b < 2 else t_down, 0, 2, tile), flat(high, slice(2, 4), n), flat(low, slice(2, 4), n)
        )
        for a in range(first, last):
            value = block[2 * (a - first) * tile : 2 * (a - first + 1) * tile]
            e = a if b < 2 else a - 2
            if 0 <= e < 2:
                value = value + edge[2 * e * tile : (2 * e + 2) * tile]
            gram[PAIRS * a + b] = value

    def add(a, b, value):
        index = PAIRS * a + b + (PAIRS + 1) * rows.side_pair(0)
        gram[index] = gram[index] + value

    side_gram(rows, 0, (nearer, farther), t_swap, side_high, side_low, add, tile)


def refine_kernel(
    meta, z, z_own, t_near, early, nearer, farther, far_up, far_down, refined, correction, high, low, late, d_high, d_low, dense, z_high, z_low,
):
    tile = z.shape[-1]
    rows = Rows(meta)

    def add(a, b, value):
        late[SIDE * a + b] = value

    side_gram(rows, 1, (nearer, farther), t_near, high, low, add, tile)
    eye = (
        lax.broadcasted_iota(jnp.int32, (tile, tile), 0) == lax.broadcasted_iota(jnp.int32, (tile, tile), 1)
    ).astype(F32)
    shift = rows.side_pair(1)
    for a in range(PAIRS):
        for b in range(PAIRS):
            if abs(a - b) > 2:
                continue
            gram = early[PAIRS * a + b]
            ia, ib = a - shift, b - shift
            there = (ia >= 0) & (ia < SIDE) & (ib >= 0) & (ib < SIDE)
            gram = gram + jnp.where(there, late[jnp.clip(SIDE * ia + ib, 0, SIDE * SIDE - 1)], 0.0)
            if a == b and a in (0, PAIRS - 1):
                gram = gram + (far_up if a == 0 else far_down)[...]
            for i in range(2):
                for j in range(2):
                    k, c = 2 * a + i, 2 * b + j
                    value = -gram[i * tile : (i + 1) * tile, j * tile : (j + 1) * tile]
                    if k == c:
                        value = value + eye
                    elif abs(k - c) <= REACH:
                        value = jnp.where(rows.present(k + COL0, c + COL0), value, 0.0)
                    else:
                        value = zero(tile)
                    put(d_high, d_low, k, c, tile, value)
                    if k + COL0 in (0, 1):
                        dense[k + COL0, c] = value
    for i in range(OWN):
        for slot in range(2 * REACH):
            correction[i, slot] = dense[i, rows.dense_slot(i, slot)]
    half = COLS * tile
    z_high[...] = z_own[:, :, :half]
    z_low[...] = z_own[:, :, half:]
    row_matmul(z_high, z_low, d_high, d_low, dense, tile)
    for i in range(OWN):
        for slot in range(2 * REACH):
            refined[i, slot] = z[i, slot] + 0.5 * dense[i, rows.dense_slot(i, slot)]


def body(correlation, factor, pattern):
    rows_here, slots, tile = correlation.shape[:3]
    total = pattern.shape[0]
    assert rows_here == OWN and slots == 2 * REACH and total >= WIDE
    device = lax.axis_index(AXES)
    rows = (device * OWN + jnp.arange(LEFT, LEFT + WIDE, dtype=jnp.int32)) % total
    offsets = (pattern[rows][:, 1:] - rows[:, None] + total // 2) % total - total // 2
    expected = jnp.array([-3, -2, -1, 1, 2], jnp.int32)
    dropped = jnp.sum((offsets == expected).astype(jnp.int32), axis=1)
    place = jnp.stack([0] * WIDE + [device % 2, device // 2 % 2]).astype(jnp.int32)
    meta = jnp.concatenate([dropped, (device % 2)[None], (device // 2 % 2)[None]]).astype(jnp.int32)

    vmem = pl.BlockSpec(memory_space=pltpu.VMEM)
    smem = pl.BlockSpec(memory_space=pltpu.SMEM)

    def call(kernel, ins, outs, scratch, flops, scalars=1):
        return pl.pallas_call(
            kernel,
            in_specs=[smem] * scalars + [vmem] * (len(ins) - scalars),
            out_specs=jax.tree.map(lambda _: vmem, outs),
            out_shape=outs,
            scratch_shapes=scratch,
            compiler_params=pltpu.CompilerParams(vmem_limit_bytes=VMEM_LIMIT),
            cost_estimate=pl.CostEstimate(flops=flops, bytes_accessed=4 << 20, transcendentals=0),
        )(*ins[:scalars], *(pltpu.with_memory_space_constraint(v, pltpu.VMEM) for v in ins[scalars:]))

    def shape(*dims, dtype=F32):
        return jax.ShapeDtypeStruct(dims, dtype)

    def halves_of(n, m):
        return [pltpu.VMEM((n, tile, m * tile), BF16)] * 2

    row = shape(1, slots, tile, tile)
    seven = shape(len(UP), tile, tile)
    nine = shape(len(Z_UP), tile, tile)
    block = shape(2 * tile, 2 * tile)
    parity = device % 2
    dense = pltpu.VMEM((OWN, COLS, tile, tile), F32)

    z0, z1, zi, zc = call(pack_kernel, (place, factor), (row, row, nine, nine), [], 1000)
    x = [send(v, swap) for v in (z0, z1)]
    zi, zc = send(zi, inside), send(zc, across)
    n = [send(x[r], near) for r in range(OWN)]
    sx = send(lax.dynamic_slice_in_dim(correlation, 1 - parity, 1, 0), swap)
    p0, p1, pf, pi, pc = call(
        product_kernel,
        (meta, correlation, factor, *x, *n, zi, zc),
        (row, row, row, seven, seven),
        halves_of(COLS, COLS) + halves_of(OWN, COLS) + [dense],
        int(2e9),
    )
    pc = send(pc, across)
    px = send(pf, swap)
    pi = send(pi, inside)
    width = 2 * REACH + 1
    ps = call(
        side_kernel,
        (meta, sx, factor, *x, *n, zi, zc),
        row,
        halves_of(width, width) + halves_of(1, width) + [pltpu.VMEM((width, tile, tile), F32)],
        int(2e9),
    )
    pn = (send(ps, near), send(px, near))

    def turned(columns):
        return shape(columns * tile, 4 * tile, dtype=BF16)

    t_own, t_up, t_down, t_swap, t_near, t_far_up, t_far_down, z_own = call(
        turn_kernel,
        (meta, factor, *x, *n, zi, zc),
        (turned(COLS), turned(4), turned(4), turned(2 * SIDE), turned(2 * SIDE), turned(2), turned(2),
         shape(OWN, tile, 2 * COLS * tile, dtype=BF16)),
        [],
        int(2e9),
    )
    gu, gd = call(far_kernel, (meta, t_far_up, t_far_down, ps, px), (block, block), halves_of(2, 4), int(1e8))
    gu, gd = send(gu, far_up), send(gd, far_down)
    early = call(
        gram_kernel,
        (meta, t_own, t_up, t_down, t_swap, p0, p1, pi, pc, ps, px),
        shape(PAIRS * PAIRS, 2 * tile, 2 * tile),
        halves_of(4, COLS) + halves_of(2, 2 * SIDE),
        int(4e9),
    )
    return call(
        refine_kernel,
        (meta, factor, z_own, t_near, early, *pn, gu, gd),
        (shape(*factor.shape), shape(*factor.shape)),
        halves_of(2, 2 * SIDE)
        + [pltpu.VMEM((SIDE * SIDE, 2 * tile, 2 * tile), F32)]
        + halves_of(COLS, COLS)
        + [dense]
        + halves_of(OWN, COLS),
        int(4e9),
    )


def solution(mesh):
    tiles = P(AXES, None, None, None)

    return jax.shard_map(body, mesh=mesh, in_specs=(tiles, tiles, P()), out_specs=(tiles, tiles), check_vma=False)
```

```python
import jax
import jax.numpy as jnp
from jax import lax
from jax.experimental import pallas as pl
from jax.experimental.pallas import tpu as pltpu
from jax.sharding import PartitionSpec as P


REACH = 3
AXES = ("blk", "sub")
OWN = 2
LEFT = -2 * REACH
WIDE = OWN + 4 * REACH
COL0 = -REACH
COLS = OWN + 2 * REACH
PAIRS = COLS // 2
SIDE = 3
VMEM_LIMIT = 24 << 20
F32 = jnp.float32
BF16 = jnp.bfloat16

UP = ((0, 3), (0, 4), (0, 5), (1, 0), (1, 3), (1, 4), (1, 5))
DOWN = ((0, 0), (0, 1), (0, 2), (0, 3), (1, 1), (1, 2), (1, 3))
Z_UP = ((0, 0), (0, 3), (0, 4), (0, 5), (1, 0), (1, 2), (1, 3), (1, 4), (1, 5))
Z_DOWN = ((0, 0), (0, 1), (0, 2), (0, 3), (0, 4), (1, 0), (1, 1), (1, 2), (1, 3))


def send(value, to):
    count = lax.axis_size(AXES)
    return lax.ppermute(value, AXES, [(i, to(i) % count) for i in range(count)])


def swap(i):
    return i ^ 1


def inside(i):
    return i ^ 2


def across(i):
    return i + 2 if i // 2 % 2 else i - 2


def near(i):
    return i + 2 if i % 2 == 0 else i - 2


def far_first(i):
    return i + (1, 1, -2, -4)[i % 4]


def far_second(i):
    return i + (4, 2, -1, -1)[i % 4]


def split(value):
    high = value.astype(BF16)
    low = (value - high.astype(F32)).astype(BF16)
    return high, low


def dot3(a_high, a_low, b_high, b_low):
    left = jnp.concatenate([a_high, a_low, a_high], axis=1)
    right = jnp.concatenate([b_high, b_high, b_low], axis=0)
    return jnp.dot(left, right, preferred_element_type=F32)


def slot_of(offset, dropped):
    pos = offset + REACH - jnp.where(offset > 0, 1, 0)
    slot = jnp.where(offset == 0, 0, pos + 1 - jnp.where(pos > dropped, 1, 0))
    there = (jnp.abs(offset) <= REACH) & ((offset == 0) | (pos != dropped))
    return jnp.clip(slot, 0, 2 * REACH - 1), there


class Rows:
    def __init__(self, meta):
        self.meta = meta
        self.parity = meta[WIDE]
        self.even_pair = meta[WIDE + 1] == 0

    def dropped(self, row):
        return self.meta[row - LEFT]

    def side_row(self, side):
        return 2 - 4 * jnp.bitwise_xor(self.parity, side)

    def side_pair(self, side):
        return 1 - jnp.bitwise_xor(self.parity, side)

    def present(self, row, col):
        return slot_of(jnp.int32(col - row), self.dropped(row))[1]

    def own(self, refs, row, col):
        slot, there = slot_of(jnp.int32(col - row), self.dropped(row))
        tile = refs[row][0, slot] if isinstance(refs, tuple) else refs[row, slot]
        return jnp.where(there, tile, 0.0)

    def packed(self, refs, layout, row0, r, col):
        slots = [s for rr, s in layout if rr == r]
        base = [j for j, (rr, _) in enumerate(layout) if rr == r][0]
        row = row0 + r
        if col == row:
            index = base + slots.index(0)
            return jnp.where(self.even_pair, refs[0][index], refs[1][index])
        slot, there = slot_of(jnp.int32(col - row), self.dropped(row))
        rest = [s for s in slots if s]
        index = base + slots.index(rest[0]) + jnp.clip(slot - rest[0], 0, len(rest) - 1)
        return jnp.where(there, jnp.where(self.even_pair, refs[0][index], refs[1][index]), 0.0)

    def side(self, ref, side, r, col):
        row = self.side_row(side) + r
        slot, there = slot_of(col - row, self.dropped(row))
        return jnp.where(there, ref[0, slot], 0.0)

    def by_distance(self, refs):
        return tuple(zip(refs, (self.parity, 1 - self.parity)))

    def dense_slot(self, row, slot):
        if slot == 0:
            return row - COL0
        pos = slot - 1 + jnp.where(slot - 1 >= self.dropped(row), 1, 0)
        return row - COL0 - REACH + pos + jnp.where(pos >= REACH, 1, 0)


def zero(tile):
    return jnp.zeros((tile, tile), F32)


def put(high, low, r, c, tile, value):
    h, l = split(value)
    high[r, :, c * tile : (c + 1) * tile] = h
    low[r, :, c * tile : (c + 1) * tile] = l


def flat(ref, rows, cols):
    value = ref[rows, :, cols]
    return value.reshape(value.shape[0] * value.shape[1], value.shape[2])


def row_matmul(left_high, left_low, right_high, right_low, out, tile):
    for c in range(0, COLS, 2):
        lo, hi = max(c - REACH, 0), min(c + 1 + REACH, COLS - 1) + 1
        k = slice(lo * tile, hi * tile)
        n = slice(c * tile, (c + 2) * tile)
        block = dot3(
            flat(left_high, slice(None), k),
            flat(left_low, slice(None), k),
            flat(right_high, slice(lo, hi), n),
            flat(right_low, slice(lo, hi), n),
        )
        for i in range(OWN):
            for j in range(2):
                out[i, c + j] = block[i * tile : (i + 1) * tile, j * tile : (j + 1) * tile]


def both(layouts, tile_of, rows, chip, link):
    for even, outs in ((True, (chip, link)), (False, (link, chip))):

        @pl.when(rows.even_pair == even)
        def _():
            for out, layout in zip(outs, layouts):
                for j, place in enumerate(layout):
                    out[j] = tile_of(*place)


def pack_kernel(meta, z, z0, z1, chip, link):
    for r, out in enumerate((z0, z1)):
        for slot in range(2 * REACH):
            out[0, slot] = z[r, slot]
    both((Z_UP, Z_DOWN), lambda i, slot: z[i, slot], Rows(meta), chip, link)


def hold_kernel(meta, s, s0, s1, nearer):
    for slot in range(2 * REACH):
        a, b = s[0, slot], s[1, slot]
        s0[0, slot] = a
        s1[0, slot] = b
        nearer[0, slot] = jnp.where(meta[WIDE] == 0, b, a)


def far_tile(rows, refs, sign, r, c, tile):
    if sign > 0:
        offset = REACH - c if r == 0 else REACH - 1 + c
        there = r == 1 or c == 0
    else:
        offset = -REACH + c if r == 0 else -REACH + 1 - c
        there = r == 0 or c == 1
    if not there:
        return zero(tile)
    slot, present = slot_of(jnp.int32(offset), rows.dropped(rows.side_row(0) + r))
    if len(refs) == 1:
        value = refs[0][0, slot]
    else:
        a, b = refs if r == 0 else refs[::-1]
        value = jnp.where(rows.parity == 0, a[0, slot], b[0, slot])
    return jnp.where(present, value, 0.0)


def far_kernel(meta, t_up, t_down, t_far_up, t_far_down, pi, pc, nearer, farther, first, second, high, low):
    tile = nearer.shape[-1]
    rows = Rows(meta)

    def block(turned, place, out, tile_of):
        for r in range(2):
            for c in range(2):
                put(high, low, r, c, tile, tile_of(r, c))
        out[...] = dot3(*halves(turned, place, place + 1, tile), flat(high, slice(None), slice(None)), flat(low, slice(None), slice(None)))

    def swapped(sign):
        return lambda r, c: far_tile(rows, (nearer, farther), sign, r, c, tile)

    def from_down(r, c):
        return rows.packed((pc, pi), UP, -4, r, c - 1) if c - 1 - (r - 4) <= REACH else zero(tile)

    def from_up(r, c):
        return rows.packed((pi, pc), DOWN, 4, r, c + 1) if r + 4 - (c + 1) <= REACH else zero(tile)

    @pl.when(rows.even_pair)
    def _():
        block(t_up, 1, first, from_down)
        block(t_far_up, 0, second, swapped(1))

    @pl.when(jnp.logical_not(rows.even_pair))
    def _():
        block(t_far_down, 0, first, swapped(-1))
        block(t_down, 0, second, from_up)


def product_kernel(meta, s0, s1, z0, z1, x0, x1, n0, n1, zi, zc, p0, p1, pf, chip, link, z_high, z_low, s_high, s_low, dense):
    tile = z0.shape[-1]
    rows = Rows(meta)
    s, z = (s0, s1), (z0, z1)
    for c in range(COLS):
        col = c + COL0
        for i in range(OWN):
            near_by = abs(col - i) <= REACH
            put(s_high, s_low, i, c, tile, rows.own(s, i, col) if near_by else zero(tile))
            put(z_high, z_low, i - COL0, c, tile, rows.own(z, i, col) if near_by else zero(tile))
        for side, refs in enumerate(((x0, x1), (n0, n1))):
            for r in range(2):
                where = rows.side_row(side) + r - COL0
                put(z_high, z_low, where, c, tile, rows.side(refs[r], side, r, col))
        row = -REACH
        put(z_high, z_low, 0, c, tile, rows.packed((zc, zi), Z_UP, -4, 1, col) if abs(col - row) <= REACH else zero(tile))
        row = OWN - 1 + REACH
        put(z_high, z_low, COLS - 1, c, tile, rows.packed((zi, zc), Z_DOWN, 4, 0, col) if abs(col - row) <= REACH else zero(tile))
    row_matmul(s_high, s_low, z_high, z_low, dense, tile)
    for i, ref in enumerate((p0, p1)):
        for slot in range(2 * REACH):
            ref[0, slot] = dense[i, rows.dense_slot(i, slot)]
    for slot in range(2 * REACH):
        pf[0, slot] = dense[rows.parity, rows.dense_slot(rows.parity, slot)]
    both((UP, DOWN), lambda i, slot: dense[i, rows.dense_slot(i, slot)], rows, chip, link)


def side_kernel(meta, s, z0, z1, x0, x1, n0, n1, zi, zc, out, z_high, z_low, s_high, s_low, dense):
    tile = s.shape[-1]
    rows = Rows(meta)
    width = 2 * REACH + 1

    def own():
        return lambda row, col: rows.own((z0, z1), row, col)

    def swapped(r):
        return lambda row, col: rows.side((x0, x1)[r], 0, r, col)

    def relayed(r):
        return lambda row, col: rows.side((n0, n1)[r], 1, r, col)

    def from_down(r):
        return lambda row, col: rows.packed((zc, zi), Z_UP, -4, r, col)

    def from_up(r):
        return lambda row, col: rows.packed((zi, zc), Z_DOWN, 4, r, col)

    even = (relayed(1), own(), own(), swapped(0), swapped(1), from_up(0), from_up(1))
    odd = (from_down(0), from_down(1), swapped(0), swapped(1), own(), own(), relayed(0))
    for parity, sources in ((0, even), (1, odd)):

        @pl.when(rows.parity == parity)
        def _():
            centre = OWN if parity == 0 else -1
            first = centre - REACH
            for k in range(width):
                for c in range(width):
                    there = abs(k - c) <= REACH
                    put(z_high, z_low, k, c, tile, sources[k](first + k, first + c) if there else zero(tile))

    centre = jnp.where(rows.parity == 0, OWN, -1)
    dropped = rows.dropped(centre)
    for c in range(width):
        slot, there = slot_of(jnp.int32(c - REACH), dropped)
        put(s_high, s_low, 0, c, tile, jnp.where(there, s[0, slot], 0.0))
    for c in range(0, width, 2):
        last = min(c + 2, width)
        lo, hi = max(c - REACH, 0), min(last - 1 + REACH, width - 1) + 1
        n = slice(c * tile, last * tile)
        k = slice(lo * tile, hi * tile)
        block = dot3(
            flat(s_high, slice(None), k),
            flat(s_low, slice(None), k),
            flat(z_high, slice(lo, hi), n),
            flat(z_low, slice(lo, hi), n),
        )
        for j in range(last - c):
            dense[c + j] = block[:, j * tile : (j + 1) * tile]
    for slot in range(2 * REACH):
        pos = slot - 1 + jnp.where(slot - 1 >= dropped, 1, 0)
        out[0, slot] = dense[REACH if slot == 0 else pos + jnp.where(pos >= REACH, 1, 0)]


def turn_kernel(meta, z0, z1, x0, x1, n0, n1, zi, zc, t_own, t_up, t_down, t_swap, t_near, t_far_up, t_far_down, z_own):
    tile = z0.shape[-1]
    rows = Rows(meta)
    z = (z0, z1)

    def store(out, c, r, value):
        high, low = split(value.T)
        out[c * tile : (c + 1) * tile, r * tile : (r + 1) * tile] = high
        out[c * tile : (c + 1) * tile, (2 + r) * tile : (3 + r) * tile] = low

    for r in range(2):
        for c in range(COLS):
            col = c + COL0
            value = rows.own(z, r, col) if abs(col - r) <= REACH else zero(tile)
            store(t_own, c, r, value)
            high, low = split(value)
            z_own[r, :, c * tile : (c + 1) * tile] = high
            z_own[r, :, (COLS + c) * tile : (COLS + c + 1) * tile] = low
        for c in range(4):
            col = c + COL0
            store(t_up, c, r, rows.packed((zc, zi), Z_UP, -4, r, col) if abs(col - (r - 4)) <= REACH else zero(tile))
            col = c + COL0 + 4
            store(t_down, c, r, rows.packed((zi, zc), Z_DOWN, 4, r, col) if abs(col - (r + 4)) <= REACH else zero(tile))
        for c in range(2):
            store(t_far_up, c, r, far_tile(rows, ((x0, x1)[r],), 1, r, c, tile))
            store(t_far_down, c, r, far_tile(rows, ((x0, x1)[r],), -1, r, c, tile))
        for side, (out, refs) in enumerate(((t_swap, (x0, x1)), (t_near, (n0, n1)))):
            first = 2 * rows.side_pair(side) + COL0
            for c in range(2 * SIDE):
                store(out, c, r, rows.side(refs[r], side, r, first + c))


def halves(turned, first, last, tile):
    part = turned[2 * first * tile : 2 * last * tile]
    return part[:, : 2 * tile], part[:, 2 * tile :]


def side_gram(rows, side, refs, turned, high, low, add, tile):
    first = 2 * rows.side_pair(side) + COL0
    for ref, r in rows.by_distance(refs):
        for c in range(2 * SIDE):
            put(high, low, r, c, tile, rows.side(ref, side, r, first + c))
    left = halves(turned, 0, SIDE, tile)
    for b in range(SIDE):
        n = slice(2 * b * tile, (2 * b + 2) * tile)
        block = dot3(*left, flat(high, slice(0, 2), n), flat(low, slice(0, 2), n))
        for a in range(SIDE):
            add(a, b, block[2 * a * tile : (2 * a + 2) * tile])


def gram_kernel(meta, t_own, t_up, t_down, t_swap, p0, p1, pi, pc, nearer, farther, gram, high, low, side_high, side_low):
    tile = p0.shape[-1]
    rows = Rows(meta)
    for r in range(2):
        for c in range(COLS):
            col = c + COL0
            put(high, low, r, c, tile, rows.own((p0, p1), r, col) if abs(col - r) <= REACH else zero(tile))
        for c in range(4):
            col = c + COL0
            value = rows.packed((pc, pi), UP, -4, r, col) if abs(col - (r - 4)) <= REACH else zero(tile)
            put(high, low, 2 + r, c, tile, value)
            col = c + COL0 + 4
            value = rows.packed((pi, pc), DOWN, 4, r, col) if abs(col - (r + 4)) <= REACH else zero(tile)
            put(high, low, 2 + r, 4 + c, tile, value)
    for b in range(PAIRS):
        n = slice(2 * b * tile, (2 * b + 2) * tile)
        first, last = max(0, b - 2), min(PAIRS, b + 3)
        block = dot3(*halves(t_own, first, last, tile), flat(high, slice(0, 2), n), flat(low, slice(0, 2), n))
        edge = dot3(
            *halves(t_up if b < 2 else t_down, 0, 2, tile), flat(high, slice(2, 4), n), flat(low, slice(2, 4), n)
        )
        for a in range(first, last):
            value = block[2 * (a - first) * tile : 2 * (a - first + 1) * tile]
            e = a if b < 2 else a - 2
            if 0 <= e < 2:
                value = value + edge[2 * e * tile : (2 * e + 2) * tile]
            gram[PAIRS * a + b] = value

    def add(a, b, value):
        index = PAIRS * a + b + (PAIRS + 1) * rows.side_pair(0)
        gram[index] = gram[index] + value

    side_gram(rows, 0, (nearer, farther), t_swap, side_high, side_low, add, tile)


def refine_kernel(
    meta, z0, z1, z_own, t_near, early, nearer, farther, first, second, refined, correction, high, low, late, d_high, d_low, dense, z_high, z_low,
):
    tile = z0.shape[-1]
    rows = Rows(meta)
    z = (z0, z1)
    ends = rows.parity != jnp.where(rows.even_pair, 0, 1)

    def add(a, b, value):
        late[SIDE * a + b] = value

    side_gram(rows, 1, (nearer, farther), t_near, high, low, add, tile)
    eye = (
        lax.broadcasted_iota(jnp.int32, (tile, tile), 0) == lax.broadcasted_iota(jnp.int32, (tile, tile), 1)
    ).astype(F32)
    shift = rows.side_pair(1)
    for a in range(PAIRS):
        for b in range(PAIRS):
            if abs(a - b) > 2:
                continue
            gram = early[PAIRS * a + b]
            ia, ib = a - shift, b - shift
            there = (ia >= 0) & (ia < SIDE) & (ib >= 0) & (ib < SIDE)
            gram = gram + jnp.where(there, late[jnp.clip(SIDE * ia + ib, 0, SIDE * SIDE - 1)], 0.0)
            if a == b and a in (0, PAIRS - 1):
                one, other = (first, second) if a == 0 else (second, first)
                gram = gram + jnp.where(ends, one[...], other[...])
            for i in range(2):
                for j in range(2):
                    k, c = 2 * a + i, 2 * b + j
                    value = -gram[i * tile : (i + 1) * tile, j * tile : (j + 1) * tile]
                    if k == c:
                        value = value + eye
                    elif abs(k - c) <= REACH:
                        value = jnp.where(rows.present(k + COL0, c + COL0), value, 0.0)
                    else:
                        value = zero(tile)
                    put(d_high, d_low, k, c, tile, value)
                    if k + COL0 in (0, 1):
                        dense[k + COL0, c] = value
    for i in range(OWN):
        for slot in range(2 * REACH):
            correction[i, slot] = dense[i, rows.dense_slot(i, slot)]
    half = COLS * tile
    z_high[...] = z_own[:, :, :half]
    z_low[...] = z_own[:, :, half:]
    row_matmul(z_high, z_low, d_high, d_low, dense, tile)
    for i in range(OWN):
        for slot in range(2 * REACH):
            refined[i, slot] = z[i][0, slot] + 0.5 * dense[i, rows.dense_slot(i, slot)]


def body(correlation, factor, pattern):
    rows_here, slots, tile = correlation.shape[:3]
    total = pattern.shape[0]
    assert rows_here == OWN and slots == 2 * REACH and total >= WIDE
    device = lax.axis_index(AXES)
    rows = (device * OWN + jnp.arange(LEFT, LEFT + WIDE, dtype=jnp.int32)) % total
    offsets = (pattern[rows][:, 1:] - rows[:, None] + total // 2) % total - total // 2
    expected = jnp.array([-3, -2, -1, 1, 2], jnp.int32)
    dropped = jnp.sum((offsets == expected).astype(jnp.int32), axis=1)
    place = jnp.stack([0] * WIDE + [device % 2, device // 2 % 2]).astype(jnp.int32)
    meta = jnp.concatenate([dropped, (device % 2)[None], (device // 2 % 2)[None]]).astype(jnp.int32)

    vmem = pl.BlockSpec(memory_space=pltpu.VMEM)
    smem = pl.BlockSpec(memory_space=pltpu.SMEM)

    def call(kernel, ins, outs, scratch, flops, scalars=1):
        return pl.pallas_call(
            kernel,
            in_specs=[smem] * scalars + [vmem] * (len(ins) - scalars),
            out_specs=jax.tree.map(lambda _: vmem, outs),
            out_shape=outs,
            scratch_shapes=scratch,
            compiler_params=pltpu.CompilerParams(vmem_limit_bytes=VMEM_LIMIT),
            cost_estimate=pl.CostEstimate(flops=flops, bytes_accessed=4 << 20, transcendentals=0),
        )(*ins[:scalars], *(pltpu.with_memory_space_constraint(v, pltpu.VMEM) for v in ins[scalars:]))

    def shape(*dims, dtype=F32):
        return jax.ShapeDtypeStruct(dims, dtype)

    def halves_of(n, m):
        return [pltpu.VMEM((n, tile, m * tile), BF16)] * 2

    row = shape(1, slots, tile, tile)
    seven = shape(len(UP), tile, tile)
    nine = shape(len(Z_UP), tile, tile)
    block = shape(2 * tile, 2 * tile)
    dense = pltpu.VMEM((OWN, COLS, tile, tile), F32)

    z0, z1, zi, zc = call(pack_kernel, (place, factor), (row, row, nine, nine), [], 1000)
    x = [send(v, swap) for v in (z0, z1)]
    zi, zc = send(zi, inside), send(zc, across)
    n = [send(x[r], near) for r in range(OWN)]
    s0, s1, near_row = call(hold_kernel, (place, correlation), (row, row, row), [], 1000)
    sx = send(near_row, swap)
    own = (z0, z1)
    p0, p1, pf, pi, pc = call(
        product_kernel,
        (meta, s0, s1, *own, *x, *n, zi, zc),
        (row, row, row, seven, seven),
        halves_of(COLS, COLS) + halves_of(OWN, COLS) + [dense],
        int(2e9),
    )
    pc = send(pc, across)
    px = send(pf, swap)
    pi = send(pi, inside)
    width = 2 * REACH + 1
    ps = call(
        side_kernel,
        (meta, sx, *own, *x, *n, zi, zc),
        row,
        halves_of(width, width) + halves_of(1, width) + [pltpu.VMEM((width, tile, tile), F32)],
        int(2e9),
    )
    pn = (send(ps, near), send(px, near))

    def turned(columns):
        return shape(columns * tile, 4 * tile, dtype=BF16)

    t_own, t_up, t_down, t_swap, t_near, t_far_up, t_far_down, z_own = call(
        turn_kernel,
        (meta, *own, *x, *n, zi, zc),
        (turned(COLS), turned(4), turned(4), turned(2 * SIDE), turned(2 * SIDE), turned(2), turned(2),
         shape(OWN, tile, 2 * COLS * tile, dtype=BF16)),
        [],
        int(2e9),
    )
    far = call(
        far_kernel,
        (meta, t_up, t_down, t_far_up, t_far_down, pi, pc, ps, px),
        (block, block),
        halves_of(2, 2),
        int(1e8),
    )
    far = (send(far[0], far_first), send(far[1], far_second))
    early = call(
        gram_kernel,
        (meta, t_own, t_up, t_down, t_swap, p0, p1, pi, pc, ps, px),
        shape(PAIRS * PAIRS, 2 * tile, 2 * tile),
        halves_of(4, COLS) + halves_of(2, 2 * SIDE),
        int(4e9),
    )
    return call(
        refine_kernel,
        (meta, *own, z_own, t_near, early, *pn, *far),
        (shape(*factor.shape), shape(*factor.shape)),
        halves_of(2, 2 * SIDE)
        + [pltpu.VMEM((SIDE * SIDE, 2 * tile, 2 * tile), F32)]
        + halves_of(COLS, COLS)
        + [dense]
        + halves_of(OWN, COLS),
        int(4e9),
    )


def solution(mesh):
    tiles = P(AXES, None, None, None)

    return jax.shard_map(body, mesh=mesh, in_specs=(tiles, tiles, P()), out_specs=(tiles, tiles), check_vma=False)
```

```python
import jax
import jax.numpy as jnp
from jax import lax
from jax.experimental import pallas as pl
from jax.experimental.pallas import tpu as pltpu
from jax.sharding import PartitionSpec as P


REACH = 3
AXES = ("blk", "sub")
OWN = 2
LEFT = -2 * REACH
WIDE = OWN + 4 * REACH
COL0 = -REACH
COLS = OWN + 2 * REACH
PAIRS = COLS // 2
SIDE = 3
VMEM_LIMIT = 24 << 20
F32 = jnp.float32
BF16 = jnp.bfloat16

UP = ((0, 3), (0, 4), (0, 5), (1, 0), (1, 3), (1, 4), (1, 5))
DOWN = ((0, 0), (0, 1), (0, 2), (0, 3), (1, 1), (1, 2), (1, 3))
Z_UP = ((0, 0), (0, 3), (0, 4), (0, 5), (1, 0), (1, 2), (1, 3), (1, 4), (1, 5))
Z_DOWN = ((0, 0), (0, 1), (0, 2), (0, 3), (0, 4), (1, 0), (1, 1), (1, 2), (1, 3))


def send(value, to):
    count = lax.axis_size(AXES)
    return lax.ppermute(value, AXES, [(i, to(i) % count) for i in range(count)])


def swap(i):
    return i ^ 1


def inside(i):
    return i ^ 2


def across(i):
    return i + 2 if i // 2 % 2 else i - 2


def near(i):
    return i + 2 if i % 2 == 0 else i - 2


def far_first(i):
    return i + (1, 1, -2, -4)[i % 4]


def far_second(i):
    return i + (4, 2, -1, -1)[i % 4]


def split(value):
    high = value.astype(BF16)
    low = (value - high.astype(F32)).astype(BF16)
    return high, low


def dot3(a_high, a_low, b_high, b_low):
    left = jnp.concatenate([a_high, a_low, a_high], axis=1)
    right = jnp.concatenate([b_high, b_high, b_low], axis=0)
    return jnp.dot(left, right, preferred_element_type=F32)


def slot_of(offset, dropped):
    pos = offset + REACH - jnp.where(offset > 0, 1, 0)
    slot = jnp.where(offset == 0, 0, pos + 1 - jnp.where(pos > dropped, 1, 0))
    there = (jnp.abs(offset) <= REACH) & ((offset == 0) | (pos != dropped))
    return jnp.clip(slot, 0, 2 * REACH - 1), there


class Rows:
    def __init__(self, meta):
        self.meta = meta
        self.parity = meta[WIDE]
        self.even_pair = meta[WIDE + 1] == 0

    def dropped(self, row):
        return self.meta[row - LEFT]

    def side_row(self, side):
        return 2 - 4 * jnp.bitwise_xor(self.parity, side)

    def side_pair(self, side):
        return 1 - jnp.bitwise_xor(self.parity, side)

    def present(self, row, col):
        return slot_of(jnp.int32(col - row), self.dropped(row))[1]

    def own(self, refs, row, col):
        slot, there = slot_of(jnp.int32(col - row), self.dropped(row))
        tile = refs[row][0, slot] if isinstance(refs, tuple) else refs[row, slot]
        return jnp.where(there, tile, 0.0)

    def packed(self, refs, layout, row0, r, col):
        slots = [s for rr, s in layout if rr == r]
        base = [j for j, (rr, _) in enumerate(layout) if rr == r][0]
        row = row0 + r
        if col == row:
            index = base + slots.index(0)
            return jnp.where(self.even_pair, refs[0][index], refs[1][index])
        slot, there = slot_of(jnp.int32(col - row), self.dropped(row))
        rest = [s for s in slots if s]
        index = base + slots.index(rest[0]) + jnp.clip(slot - rest[0], 0, len(rest) - 1)
        return jnp.where(there, jnp.where(self.even_pair, refs[0][index], refs[1][index]), 0.0)

    def side(self, ref, side, r, col):
        row = self.side_row(side) + r
        slot, there = slot_of(col - row, self.dropped(row))
        return jnp.where(there, ref[0, slot], 0.0)

    def by_distance(self, refs):
        return tuple(zip(refs, (self.parity, 1 - self.parity)))

    def dense_slot(self, row, slot):
        if slot == 0:
            return row - COL0
        pos = slot - 1 + jnp.where(slot - 1 >= self.dropped(row), 1, 0)
        return row - COL0 - REACH + pos + jnp.where(pos >= REACH, 1, 0)


def zero(tile):
    return jnp.zeros((tile, tile), F32)


def put(high, low, r, c, tile, value):
    h, l = split(value)
    high[r, :, c * tile : (c + 1) * tile] = h
    low[r, :, c * tile : (c + 1) * tile] = l


def flat(ref, rows, cols):
    value = ref[rows, :, cols]
    return value.reshape(value.shape[0] * value.shape[1], value.shape[2])


def row_matmul(left_high, left_low, right_high, right_low, out, tile):
    for c in range(0, COLS, 2):
        lo, hi = max(c - REACH, 0), min(c + 1 + REACH, COLS - 1) + 1
        k = slice(lo * tile, hi * tile)
        n = slice(c * tile, (c + 2) * tile)
        block = dot3(
            flat(left_high, slice(None), k),
            flat(left_low, slice(None), k),
            flat(right_high, slice(lo, hi), n),
            flat(right_low, slice(lo, hi), n),
        )
        for i in range(OWN):
            for j in range(2):
                out[i, c + j] = block[i * tile : (i + 1) * tile, j * tile : (j + 1) * tile]


def both(layouts, tile_of, rows, chip, link):
    for even, outs in ((True, (chip, link)), (False, (link, chip))):

        @pl.when(rows.even_pair == even)
        def _():
            for out, layout in zip(outs, layouts):
                for j, place in enumerate(layout):
                    out[j] = tile_of(*place)


def pack_kernel(meta, z, z0, z1, chip, link):
    for r, out in enumerate((z0, z1)):
        for slot in range(2 * REACH):
            out[0, slot] = z[r, slot]
    both((Z_UP, Z_DOWN), lambda i, slot: z[i, slot], Rows(meta), chip, link)


def far_tile(rows, refs, sign, r, c, tile):
    if sign > 0:
        offset = REACH - c if r == 0 else REACH - 1 + c
        there = r == 1 or c == 0
    else:
        offset = -REACH + c if r == 0 else -REACH + 1 - c
        there = r == 0 or c == 1
    if not there:
        return zero(tile)
    slot, present = slot_of(jnp.int32(offset), rows.dropped(rows.side_row(0) + r))
    if len(refs) == 1:
        value = refs[0][0, slot]
    else:
        a, b = refs if r == 0 else refs[::-1]
        value = jnp.where(rows.parity == 0, a[0, slot], b[0, slot])
    return jnp.where(present, value, 0.0)


def edge_kernel(
    meta, t_up, t_down, t_far_up, t_far_down, pi, pc, nearer, farther, early, edge, first, second,
    high, low, far_high, far_low,
):
    tile = nearer.shape[-1]
    rows = Rows(meta)
    for r in range(2):
        for c in range(4):
            col = c + COL0
            value = rows.packed((pc, pi), UP, -4, r, col) if abs(col - (r - 4)) <= REACH else zero(tile)
            put(high, low, r, c, tile, value)
            col = c + COL0 + 4
            value = rows.packed((pi, pc), DOWN, 4, r, col) if abs(col - (r + 4)) <= REACH else zero(tile)
            put(high, low, r, 4 + c, tile, value)
    for b in range(PAIRS):
        n = slice(2 * b * tile, (2 * b + 2) * tile)
        block = dot3(
            *halves(t_up if b < 2 else t_down, 0, 2, tile), flat(high, slice(None), n), flat(low, slice(None), n)
        )
        for e in range(2):
            edge[2 * b + e] = block[2 * e * tile : (2 * e + 2) * tile]

    def far_block(turned, sign, out):
        for r in range(2):
            for c in range(2):
                put(far_high, far_low, r, c, tile, far_tile(rows, (nearer, farther), sign, r, c, tile))
        whole = slice(None), slice(None)
        out[...] = dot3(*halves(turned, 0, 1, tile), flat(far_high, *whole), flat(far_low, *whole))

    @pl.when(rows.even_pair)
    def _():
        first[...] = edge[3]
        far_block(t_far_up, 1, second)

    @pl.when(jnp.logical_not(rows.even_pair))
    def _():
        far_block(t_far_down, -1, first)
        second[...] = edge[4]


def product_kernel(meta, s, z, x0, x1, n0, n1, zi, zc, p0, p1, pf, chip, link, z_high, z_low, s_high, s_low, dense):
    tile = z.shape[-1]
    rows = Rows(meta)
    for c in range(COLS):
        col = c + COL0
        for i in range(OWN):
            near_by = abs(col - i) <= REACH
            put(s_high, s_low, i, c, tile, rows.own(s, i, col) if near_by else zero(tile))
            put(z_high, z_low, i - COL0, c, tile, rows.own(z, i, col) if near_by else zero(tile))
        for side, refs in enumerate(((x0, x1), (n0, n1))):
            for r in range(2):
                where = rows.side_row(side) + r - COL0
                put(z_high, z_low, where, c, tile, rows.side(refs[r], side, r, col))
        row = -REACH
        put(z_high, z_low, 0, c, tile, rows.packed((zc, zi), Z_UP, -4, 1, col) if abs(col - row) <= REACH else zero(tile))
        row = OWN - 1 + REACH
        put(z_high, z_low, COLS - 1, c, tile, rows.packed((zi, zc), Z_DOWN, 4, 0, col) if abs(col - row) <= REACH else zero(tile))
    row_matmul(s_high, s_low, z_high, z_low, dense, tile)
    for i, ref in enumerate((p0, p1)):
        for slot in range(2 * REACH):
            ref[0, slot] = dense[i, rows.dense_slot(i, slot)]
    for slot in range(2 * REACH):
        pf[0, slot] = dense[rows.parity, rows.dense_slot(rows.parity, slot)]
    both((UP, DOWN), lambda i, slot: dense[i, rows.dense_slot(i, slot)], rows, chip, link)


def side_kernel(meta, s, z, x0, x1, n0, n1, zi, zc, out, z_high, z_low, s_high, s_low, dense):
    tile = s.shape[-1]
    rows = Rows(meta)
    width = 2 * REACH + 1

    def own():
        return lambda row, col: rows.own(z, row, col)

    def swapped(r):
        return lambda row, col: rows.side((x0, x1)[r], 0, r, col)

    def relayed(r):
        return lambda row, col: rows.side((n0, n1)[r], 1, r, col)

    def from_down(r):
        return lambda row, col: rows.packed((zc, zi), Z_UP, -4, r, col)

    def from_up(r):
        return lambda row, col: rows.packed((zi, zc), Z_DOWN, 4, r, col)

    even = (relayed(1), own(), own(), swapped(0), swapped(1), from_up(0), from_up(1))
    odd = (from_down(0), from_down(1), swapped(0), swapped(1), own(), own(), relayed(0))
    for parity, sources in ((0, even), (1, odd)):

        @pl.when(rows.parity == parity)
        def _():
            centre = OWN if parity == 0 else -1
            first = centre - REACH
            for k in range(width):
                for c in range(width):
                    there = abs(k - c) <= REACH
                    put(z_high, z_low, k, c, tile, sources[k](first + k, first + c) if there else zero(tile))

    centre = jnp.where(rows.parity == 0, OWN, -1)
    dropped = rows.dropped(centre)
    for c in range(width):
        slot, there = slot_of(jnp.int32(c - REACH), dropped)
        put(s_high, s_low, 0, c, tile, jnp.where(there, s[0, slot], 0.0))
    for c in range(0, width, 2):
        last = min(c + 2, width)
        lo, hi = max(c - REACH, 0), min(last - 1 + REACH, width - 1) + 1
        n = slice(c * tile, last * tile)
        k = slice(lo * tile, hi * tile)
        block = dot3(
            flat(s_high, slice(None), k),
            flat(s_low, slice(None), k),
            flat(z_high, slice(lo, hi), n),
            flat(z_low, slice(lo, hi), n),
        )
        for j in range(last - c):
            dense[c + j] = block[:, j * tile : (j + 1) * tile]
    for slot in range(2 * REACH):
        pos = slot - 1 + jnp.where(slot - 1 >= dropped, 1, 0)
        out[0, slot] = dense[REACH if slot == 0 else pos + jnp.where(pos >= REACH, 1, 0)]


def turn_kernel(meta, z, x0, x1, n0, n1, zi, zc, after, z_kept, t_own, t_up, t_down, t_swap, t_near, t_far_up, t_far_down, z_own):
    tile = z.shape[-1]
    rows = Rows(meta)

    z_kept[...] = z[...]

    def store(out, c, r, value):
        high, low = split(value.T)
        out[c * tile : (c + 1) * tile, r * tile : (r + 1) * tile] = high
        out[c * tile : (c + 1) * tile, (2 + r) * tile : (3 + r) * tile] = low

    for r in range(2):
        for c in range(COLS):
            col = c + COL0
            value = rows.own(z, r, col) if abs(col - r) <= REACH else zero(tile)
            store(t_own, c, r, value)
            high, low = split(value)
            z_own[r, :, c * tile : (c + 1) * tile] = high
            z_own[r, :, (COLS + c) * tile : (COLS + c + 1) * tile] = low
        for c in range(4):
            col = c + COL0
            store(t_up, c, r, rows.packed((zc, zi), Z_UP, -4, r, col) if abs(col - (r - 4)) <= REACH else zero(tile))
            col = c + COL0 + 4
            store(t_down, c, r, rows.packed((zi, zc), Z_DOWN, 4, r, col) if abs(col - (r + 4)) <= REACH else zero(tile))
        for c in range(2):
            store(t_far_up, c, r, far_tile(rows, ((x0, x1)[r],), 1, r, c, tile))
            store(t_far_down, c, r, far_tile(rows, ((x0, x1)[r],), -1, r, c, tile))
        for side, (out, refs) in enumerate(((t_swap, (x0, x1)), (t_near, (n0, n1)))):
            first = 2 * rows.side_pair(side) + COL0
            for c in range(2 * SIDE):
                store(out, c, r, rows.side(refs[r], side, r, first + c))


def halves(turned, first, last, tile):
    part = turned[2 * first * tile : 2 * last * tile]
    return part[:, : 2 * tile], part[:, 2 * tile :]


def side_gram(rows, side, refs, turned, high, low, add, tile):
    first = 2 * rows.side_pair(side) + COL0
    for ref, r in rows.by_distance(refs):
        for c in range(2 * SIDE):
            put(high, low, r, c, tile, rows.side(ref, side, r, first + c))
    left = halves(turned, 0, SIDE, tile)
    for b in range(SIDE):
        n = slice(2 * b * tile, (2 * b + 2) * tile)
        block = dot3(*left, flat(high, slice(0, 2), n), flat(low, slice(0, 2), n))
        for a in range(SIDE):
            add(a, b, block[2 * a * tile : (2 * a + 2) * tile])


def gram_kernel(meta, t_own, t_swap, p0, p1, nearer, farther, gram, high, low, side_high, side_low):
    tile = p0.shape[-1]
    rows = Rows(meta)
    for r in range(2):
        for c in range(COLS):
            col = c + COL0
            put(high, low, r, c, tile, rows.own((p0, p1), r, col) if abs(col - r) <= REACH else zero(tile))
    for b in range(PAIRS):
        n = slice(2 * b * tile, (2 * b + 2) * tile)
        first, last = max(0, b - 2), min(PAIRS, b + 3)
        block = dot3(*halves(t_own, first, last, tile), flat(high, slice(0, 2), n), flat(low, slice(0, 2), n))
        for a in range(first, last):
            gram[PAIRS * a + b] = block[2 * (a - first) * tile : 2 * (a - first + 1) * tile]

    def add(a, b, value):
        index = PAIRS * a + b + (PAIRS + 1) * rows.side_pair(0)
        gram[index] = gram[index] + value

    side_gram(rows, 0, (nearer, farther), t_swap, side_high, side_low, add, tile)


def refine_kernel(
    meta, z, z_own, t_near, early, edge, nearer, farther, first, second, refined, correction, high, low, late, d_high, d_low, dense, z_high, z_low,
):
    tile = z.shape[-1]
    rows = Rows(meta)
    ends = rows.parity != jnp.where(rows.even_pair, 0, 1)

    def add(a, b, value):
        late[SIDE * a + b] = value

    side_gram(rows, 1, (nearer, farther), t_near, high, low, add, tile)
    eye = (
        lax.broadcasted_iota(jnp.int32, (tile, tile), 0) == lax.broadcasted_iota(jnp.int32, (tile, tile), 1)
    ).astype(F32)
    shift = rows.side_pair(1)
    for a in range(PAIRS):
        for b in range(PAIRS):
            if abs(a - b) > 2:
                continue
            gram = early[PAIRS * a + b]
            ia, ib = a - shift, b - shift
            there = (ia >= 0) & (ia < SIDE) & (ib >= 0) & (ib < SIDE)
            gram = gram + jnp.where(there, late[jnp.clip(SIDE * ia + ib, 0, SIDE * SIDE - 1)], 0.0)
            e = a if b < 2 else a - 2
            if 0 <= e < 2:
                gram = gram + edge[2 * b + e]
            if a == b and a in (0, PAIRS - 1):
                one, other = (first, second) if a == 0 else (second, first)
                gram = gram + jnp.where(ends, one[...], other[...])
            for i in range(2):
                for j in range(2):
                    k, c = 2 * a + i, 2 * b + j
                    value = -gram[i * tile : (i + 1) * tile, j * tile : (j + 1) * tile]
                    if k == c:
                        value = value + eye
                    elif abs(k - c) <= REACH:
                        value = jnp.where(rows.present(k + COL0, c + COL0), value, 0.0)
                    else:
                        value = zero(tile)
                    put(d_high, d_low, k, c, tile, value)
                    if k + COL0 in (0, 1):
                        dense[k + COL0, c] = value
    for i in range(OWN):
        for slot in range(2 * REACH):
            correction[i, slot] = dense[i, rows.dense_slot(i, slot)]
    half = COLS * tile
    z_high[...] = z_own[:, :, :half]
    z_low[...] = z_own[:, :, half:]
    row_matmul(z_high, z_low, d_high, d_low, dense, tile)
    for i in range(OWN):
        for slot in range(2 * REACH):
            refined[i, slot] = z[i, slot] + 0.5 * dense[i, rows.dense_slot(i, slot)]


def body(correlation, factor, pattern):
    rows_here, slots, tile = correlation.shape[:3]
    total = pattern.shape[0]
    assert rows_here == OWN and slots == 2 * REACH and total >= WIDE
    device = lax.axis_index(AXES)
    rows = (device * OWN + jnp.arange(LEFT, LEFT + WIDE, dtype=jnp.int32)) % total
    offsets = (pattern[rows][:, 1:] - rows[:, None] + total // 2) % total - total // 2
    expected = jnp.array([-3, -2, -1, 1, 2], jnp.int32)
    dropped = jnp.sum((offsets == expected).astype(jnp.int32), axis=1)
    place = jnp.stack([0] * WIDE + [device % 2, device // 2 % 2]).astype(jnp.int32)
    meta = jnp.concatenate([dropped, (device % 2)[None], (device // 2 % 2)[None]]).astype(jnp.int32)

    vmem = pl.BlockSpec(memory_space=pltpu.VMEM)
    smem = pl.BlockSpec(memory_space=pltpu.SMEM)

    def resident(value):
        if value is factor or value is correlation:
            return pltpu.with_memory_space_constraint(value, pltpu.HBM)
        return pltpu.with_memory_space_constraint(value, pltpu.VMEM)

    def call(kernel, ins, outs, scratch, flops, scalars=1):
        return pl.pallas_call(
            kernel,
            in_specs=[smem] * scalars + [vmem] * (len(ins) - scalars),
            out_specs=jax.tree.map(lambda _: vmem, outs),
            out_shape=outs,
            scratch_shapes=scratch,
            compiler_params=pltpu.CompilerParams(vmem_limit_bytes=VMEM_LIMIT),
            cost_estimate=pl.CostEstimate(flops=flops, bytes_accessed=4 << 20, transcendentals=0),
        )(*ins[:scalars], *map(resident, ins[scalars:]))

    def shape(*dims, dtype=F32):
        return jax.ShapeDtypeStruct(dims, dtype)

    def halves_of(n, m):
        return [pltpu.VMEM((n, tile, m * tile), BF16)] * 2

    row = shape(1, slots, tile, tile)
    seven = shape(len(UP), tile, tile)
    nine = shape(len(Z_UP), tile, tile)
    block = shape(2 * tile, 2 * tile)
    dense = pltpu.VMEM((OWN, COLS, tile, tile), F32)

    z0, z1, zi, zc = call(pack_kernel, (place, factor), (row, row, nine, nine), [], 1000)
    x = [send(v, swap) for v in (z0, z1)]
    zi, zc = send(zi, inside), send(zc, across)
    n = [send(x[r], near) for r in range(OWN)]
    sx = send(lax.dynamic_slice_in_dim(correlation, 1 - device % 2, 1, 0), swap)
    p0, p1, pf, pi, pc = call(
        product_kernel,
        (meta, correlation, factor, *x, *n, zi, zc),
        (row, row, row, seven, seven),
        halves_of(COLS, COLS) + halves_of(OWN, COLS) + [dense],
        int(2e9),
    )
    pc = send(pc, across)
    px = send(pf, swap)
    pi = send(pi, inside)
    width = 2 * REACH + 1
    ps = call(
        side_kernel,
        (meta, sx, factor, *x, *n, zi, zc),
        row,
        halves_of(width, width) + halves_of(1, width) + [pltpu.VMEM((width, tile, tile), F32)],
        int(2e9),
    )
    pn = (send(ps, near), send(px, near))

    def turned(columns):
        return shape(columns * tile, 4 * tile, dtype=BF16)

    z_kept, t_own, t_up, t_down, t_swap, t_near, t_far_up, t_far_down, z_own = call(
        turn_kernel,
        (meta, factor, *x, *n, zi, zc, ps),
        (shape(*factor.shape), turned(COLS), turned(4), turned(4), turned(2 * SIDE), turned(2 * SIDE), turned(2), turned(2),
         shape(OWN, tile, 2 * COLS * tile, dtype=BF16)),
        [],
        int(2e9),
    )
    early = call(
        gram_kernel,
        (meta, t_own, t_swap, p0, p1, ps, px),
        shape(PAIRS * PAIRS, 2 * tile, 2 * tile),
        halves_of(2, COLS) + halves_of(2, 2 * SIDE),
        int(4e9),
    )
    edge, *far = call(
        edge_kernel,
        (meta, t_up, t_down, t_far_up, t_far_down, pi, pc, ps, px, early),
        (shape(2 * PAIRS, 2 * tile, 2 * tile), block, block),
        halves_of(2, COLS) + halves_of(2, 2),
        int(1e9),
    )
    far = (send(far[0], far_first), send(far[1], far_second))
    return call(
        refine_kernel,
        (meta, z_kept, z_own, t_near, early, edge, *pn, *far),
        (shape(*factor.shape), shape(*factor.shape)),
        halves_of(2, 2 * SIDE)
        + [pltpu.VMEM((SIDE * SIDE, 2 * tile, 2 * tile), F32)]
        + halves_of(COLS, COLS)
        + [dense]
        + halves_of(OWN, COLS),
        int(4e9),
    )


def solution(mesh):
    tiles = P(AXES, None, None, None)

    return jax.shard_map(body, mesh=mesh, in_specs=(tiles, tiles, P()), out_specs=(tiles, tiles), check_vma=False)
```

```python
import jax
import jax.numpy as jnp
from jax import lax
from jax.experimental import pallas as pl
from jax.experimental.pallas import tpu as pltpu
from jax.sharding import PartitionSpec as P


REACH = 3
AXES = ("blk", "sub")
OWN = 2
LEFT = -2 * REACH
WIDE = OWN + 4 * REACH
COL0 = -REACH
COLS = OWN + 2 * REACH
PAIRS = COLS // 2
SIDE = 3
VMEM_LIMIT = 24 << 20
F32 = jnp.float32
BF16 = jnp.bfloat16

UP = ((0, 3), (0, 4), (0, 5), (1, 0), (1, 3), (1, 4), (1, 5))
DOWN = ((0, 0), (0, 1), (0, 2), (0, 3), (1, 1), (1, 2), (1, 3))
Z_UP = ((0, 0), (0, 3), (0, 4), (0, 5), (1, 0), (1, 2), (1, 3), (1, 4), (1, 5))
Z_DOWN = ((0, 0), (0, 1), (0, 2), (0, 3), (0, 4), (1, 0), (1, 1), (1, 2), (1, 3))


def send(value, to):
    count = lax.axis_size(AXES)
    return lax.ppermute(value, AXES, [(i, to(i) % count) for i in range(count)])


def swap(i):
    return i ^ 1


def inside(i):
    return i ^ 2


def across(i):
    return i + 2 if i // 2 % 2 else i - 2


def near(i):
    return i + 2 if i % 2 == 0 else i - 2


def far_first(i):
    return i + (1, 1, -2, -4)[i % 4]


def far_second(i):
    return i + (4, 2, -1, -1)[i % 4]


def split(value):
    high = value.astype(BF16)
    low = (value - high.astype(F32)).astype(BF16)
    return high, low


def dot3(a_high, a_low, b_high, b_low):
    left = jnp.concatenate([a_high, a_low, a_high], axis=1)
    right = jnp.concatenate([b_high, b_high, b_low], axis=0)
    return jnp.dot(left, right, preferred_element_type=F32)


def slot_of(offset, dropped):
    pos = offset + REACH - jnp.where(offset > 0, 1, 0)
    slot = jnp.where(offset == 0, 0, pos + 1 - jnp.where(pos > dropped, 1, 0))
    there = (jnp.abs(offset) <= REACH) & ((offset == 0) | (pos != dropped))
    return jnp.clip(slot, 0, 2 * REACH - 1), there


class Rows:
    def __init__(self, meta):
        self.meta = meta
        self.parity = meta[WIDE]
        self.even_pair = meta[WIDE + 1] == 0

    def dropped(self, row):
        return self.meta[row - LEFT]

    def side_row(self, side):
        return 2 - 4 * jnp.bitwise_xor(self.parity, side)

    def side_pair(self, side):
        return 1 - jnp.bitwise_xor(self.parity, side)

    def present(self, row, col):
        return slot_of(jnp.int32(col - row), self.dropped(row))[1]

    def own(self, refs, row, col):
        slot, there = slot_of(jnp.int32(col - row), self.dropped(row))
        tile = refs[row][0, slot] if isinstance(refs, tuple) else refs[row, slot]
        return jnp.where(there, tile, 0.0)

    def packed(self, refs, layout, row0, r, col):
        slots = [s for rr, s in layout if rr == r]
        base = [j for j, (rr, _) in enumerate(layout) if rr == r][0]
        row = row0 + r
        if col == row:
            index = base + slots.index(0)
            return jnp.where(self.even_pair, refs[0][index], refs[1][index])
        slot, there = slot_of(jnp.int32(col - row), self.dropped(row))
        rest = [s for s in slots if s]
        index = base + slots.index(rest[0]) + jnp.clip(slot - rest[0], 0, len(rest) - 1)
        return jnp.where(there, jnp.where(self.even_pair, refs[0][index], refs[1][index]), 0.0)

    def side(self, ref, side, r, col):
        row = self.side_row(side) + r
        slot, there = slot_of(col - row, self.dropped(row))
        return jnp.where(there, ref[0, slot], 0.0)

    def by_distance(self, refs):
        return tuple(zip(refs, (self.parity, 1 - self.parity)))

    def dense_slot(self, row, slot):
        if slot == 0:
            return row - COL0
        pos = slot - 1 + jnp.where(slot - 1 >= self.dropped(row), 1, 0)
        return row - COL0 - REACH + pos + jnp.where(pos >= REACH, 1, 0)


def zero(tile):
    return jnp.zeros((tile, tile), F32)


def put(high, low, r, c, tile, value):
    h, l = split(value)
    high[r, :, c * tile : (c + 1) * tile] = h
    low[r, :, c * tile : (c + 1) * tile] = l


def flat(ref, rows, cols):
    value = ref[rows, :, cols]
    return value.reshape(value.shape[0] * value.shape[1], value.shape[2])


def row_matmul(left_high, left_low, right_high, right_low, out, tile, columns=range(0, COLS, 2)):
    for c in columns:
        lo, hi = max(c - REACH, 0), min(c + 1 + REACH, COLS - 1) + 1
        k = slice(lo * tile, hi * tile)
        n = slice(c * tile, (c + 2) * tile)
        block = dot3(
            flat(left_high, slice(None), k),
            flat(left_low, slice(None), k),
            flat(right_high, slice(lo, hi), n),
            flat(right_low, slice(lo, hi), n),
        )
        for i in range(OWN):
            for j in range(2):
                out[i, c + j] = block[i * tile : (i + 1) * tile, j * tile : (j + 1) * tile]


def both(layouts, tile_of, rows, chip, link):
    for even, outs in ((True, (chip, link)), (False, (link, chip))):

        @pl.when(rows.even_pair == even)
        def _():
            for out, layout in zip(outs, layouts):
                for j, place in enumerate(layout):
                    out[j] = tile_of(*place)


def pack_kernel(meta, z, z0, z1, chip, link):
    for r, out in enumerate((z0, z1)):
        for slot in range(2 * REACH):
            out[0, slot] = z[r, slot]
    both((Z_UP, Z_DOWN), lambda i, slot: z[i, slot], Rows(meta), chip, link)


def far_tile(rows, refs, sign, r, c, tile):
    if sign > 0:
        offset = REACH - c if r == 0 else REACH - 1 + c
        there = r == 1 or c == 0
    else:
        offset = -REACH + c if r == 0 else -REACH + 1 - c
        there = r == 0 or c == 1
    if not there:
        return zero(tile)
    slot, present = slot_of(jnp.int32(offset), rows.dropped(rows.side_row(0) + r))
    if len(refs) == 1:
        value = refs[0][0, slot]
    else:
        a, b = refs if r == 0 else refs[::-1]
        value = jnp.where(rows.parity == 0, a[0, slot], b[0, slot])
    return jnp.where(present, value, 0.0)


def edge_kernel(
    meta, t_up, t_down, t_far_up, t_far_down, pi, pc, nearer, farther, early, edge, first, second,
    high, low, far_high, far_low,
):
    tile = nearer.shape[-1]
    rows = Rows(meta)
    for r in range(2):
        for c in range(4):
            col = c + COL0
            value = rows.packed((pc, pi), UP, -4, r, col) if abs(col - (r - 4)) <= REACH else zero(tile)
            put(high, low, r, c, tile, value)
            col = c + COL0 + 4
            value = rows.packed((pi, pc), DOWN, 4, r, col) if abs(col - (r + 4)) <= REACH else zero(tile)
            put(high, low, r, 4 + c, tile, value)
    for b in range(PAIRS):
        n = slice(2 * b * tile, (2 * b + 2) * tile)
        block = dot3(
            *halves(t_up if b < 2 else t_down, 0, 2, tile), flat(high, slice(None), n), flat(low, slice(None), n)
        )
        for e in range(2):
            edge[2 * b + e] = block[2 * e * tile : (2 * e + 2) * tile]

    def far_block(turned, sign, out):
        for r in range(2):
            for c in range(2):
                put(far_high, far_low, r, c, tile, far_tile(rows, (nearer, farther), sign, r, c, tile))
        whole = slice(None), slice(None)
        out[...] = dot3(*halves(turned, 0, 1, tile), flat(far_high, *whole), flat(far_low, *whole))

    @pl.when(rows.even_pair)
    def _():
        first[...] = edge[3]
        far_block(t_far_up, 1, second)

    @pl.when(jnp.logical_not(rows.even_pair))
    def _():
        far_block(t_far_down, -1, first)
        second[...] = edge[4]


def prepare_kernel(meta, s, z, x0, x1, z_high, z_low, s_high, s_low):
    tile = z.shape[-1]
    rows = Rows(meta)
    for c in range(COLS):
        col = c + COL0
        for i in range(OWN):
            near_by = abs(col - i) <= REACH
            put(s_high, s_low, i, c, tile, rows.own(s, i, col) if near_by else zero(tile))
            put(z_high, z_low, i - COL0, c, tile, rows.own(z, i, col) if near_by else zero(tile))
            put(z_high, z_low, rows.side_row(0) + i - COL0, c, tile, rows.side((x0, x1)[i], 0, i, col))


def product_kernel(
    meta, z_high_in, z_low_in, s_high, s_low, n0, n1, zi, zc, p0, p1, pf, chip, link, z_high, z_low, dense
):
    tile = n0.shape[-1]
    rows = Rows(meta)
    for c in range(COLS):
        col = c + COL0
        for r, ref in enumerate((n0, n1)):
            put(z_high, z_low, rows.side_row(1) + r - COL0, c, tile, rows.side(ref, 1, r, col))
        value = rows.packed((zc, zi), Z_UP, -4, 1, col) if col <= 0 else zero(tile)
        put(z_high, z_low, 0, c, tile, value)
        value = rows.packed((zi, zc), Z_DOWN, 4, 0, col) if col >= 1 else zero(tile)
        put(z_high, z_low, COLS - 1, c, tile, value)
    row_matmul(s_high, s_low, z_high, z_low, dense, tile)
    for i, ref in enumerate((p0, p1)):
        for slot in range(2 * REACH):
            ref[0, slot] = dense[i, rows.dense_slot(i, slot)]
    for slot in range(2 * REACH):
        pf[0, slot] = dense[rows.parity, rows.dense_slot(rows.parity, slot)]
    both((UP, DOWN), lambda i, slot: dense[i, rows.dense_slot(i, slot)], rows, chip, link)


def side_kernel(meta, s, z, x0, x1, n0, n1, zi, zc, out, z_high, z_low, s_high, s_low, dense):
    tile = s.shape[-1]
    rows = Rows(meta)
    width = 2 * REACH + 1

    def own():
        return lambda row, col: rows.own(z, row, col)

    def swapped(r):
        return lambda row, col: rows.side((x0, x1)[r], 0, r, col)

    def relayed(r):
        return lambda row, col: rows.side((n0, n1)[r], 1, r, col)

    def from_down(r):
        return lambda row, col: rows.packed((zc, zi), Z_UP, -4, r, col)

    def from_up(r):
        return lambda row, col: rows.packed((zi, zc), Z_DOWN, 4, r, col)

    even = (relayed(1), own(), own(), swapped(0), swapped(1), from_up(0), from_up(1))
    odd = (from_down(0), from_down(1), swapped(0), swapped(1), own(), own(), relayed(0))
    for parity, sources in ((0, even), (1, odd)):

        @pl.when(rows.parity == parity)
        def _():
            centre = OWN if parity == 0 else -1
            first = centre - REACH
            for k in range(width):
                for c in range(width):
                    there = abs(k - c) <= REACH
                    put(z_high, z_low, k, c, tile, sources[k](first + k, first + c) if there else zero(tile))

    centre = jnp.where(rows.parity == 0, OWN, -1)
    dropped = rows.dropped(centre)
    for c in range(width):
        slot, there = slot_of(jnp.int32(c - REACH), dropped)
        put(s_high, s_low, 0, c, tile, jnp.where(there, s[0, slot], 0.0))
    for c in range(0, width, 2):
        last = min(c + 2, width)
        lo, hi = max(c - REACH, 0), min(last - 1 + REACH, width - 1) + 1
        n = slice(c * tile, last * tile)
        k = slice(lo * tile, hi * tile)
        block = dot3(
            flat(s_high, slice(None), k),
            flat(s_low, slice(None), k),
            flat(z_high, slice(lo, hi), n),
            flat(z_low, slice(lo, hi), n),
        )
        for j in range(last - c):
            dense[c + j] = block[:, j * tile : (j + 1) * tile]
    for slot in range(2 * REACH):
        pos = slot - 1 + jnp.where(slot - 1 >= dropped, 1, 0)
        out[0, slot] = dense[REACH if slot == 0 else pos + jnp.where(pos >= REACH, 1, 0)]


def turn_kernel(meta, z, x0, x1, n0, n1, zi, zc, after, z_kept, t_own, t_up, t_down, t_swap, t_near, t_far_up, t_far_down, z_high, z_low):
    tile = z.shape[-1]
    rows = Rows(meta)

    z_kept[...] = z[...]

    def store(out, c, r, value):
        high, low = split(value.T)
        out[c * tile : (c + 1) * tile, r * tile : (r + 1) * tile] = high
        out[c * tile : (c + 1) * tile, (2 + r) * tile : (3 + r) * tile] = low

    for r in range(2):
        for c in range(COLS):
            col = c + COL0
            value = rows.own(z, r, col) if abs(col - r) <= REACH else zero(tile)
            store(t_own, c, r, value)
            put(z_high, z_low, r, c, tile, value)
        for c in range(4):
            col = c + COL0
            store(t_up, c, r, rows.packed((zc, zi), Z_UP, -4, r, col) if abs(col - (r - 4)) <= REACH else zero(tile))
            col = c + COL0 + 4
            store(t_down, c, r, rows.packed((zi, zc), Z_DOWN, 4, r, col) if abs(col - (r + 4)) <= REACH else zero(tile))
        for c in range(2):
            store(t_far_up, c, r, far_tile(rows, ((x0, x1)[r],), 1, r, c, tile))
            store(t_far_down, c, r, far_tile(rows, ((x0, x1)[r],), -1, r, c, tile))
        for side, (out, refs) in enumerate(((t_swap, (x0, x1)), (t_near, (n0, n1)))):
            first = 2 * rows.side_pair(side) + COL0
            for c in range(2 * SIDE):
                store(out, c, r, rows.side(refs[r], side, r, first + c))


def halves(turned, first, last, tile):
    part = turned[2 * first * tile : 2 * last * tile]
    return part[:, : 2 * tile], part[:, 2 * tile :]


def side_gram(rows, side, refs, turned, high, low, add, tile):
    first = 2 * rows.side_pair(side) + COL0
    for ref, r in rows.by_distance(refs):
        for c in range(2 * SIDE):
            put(high, low, r, c, tile, rows.side(ref, side, r, first + c))
    left = halves(turned, 0, SIDE, tile)
    for b in range(SIDE):
        n = slice(2 * b * tile, (2 * b + 2) * tile)
        block = dot3(*left, flat(high, slice(0, 2), n), flat(low, slice(0, 2), n))
        for a in range(SIDE):
            add(a, b, block[2 * a * tile : (2 * a + 2) * tile])


def gram_kernel(meta, t_own, t_swap, p0, p1, nearer, farther, gram, high, low, side_high, side_low):
    tile = p0.shape[-1]
    rows = Rows(meta)
    for r in range(2):
        for c in range(COLS):
            col = c + COL0
            put(high, low, r, c, tile, rows.own((p0, p1), r, col) if abs(col - r) <= REACH else zero(tile))
    for b in range(PAIRS):
        n = slice(2 * b * tile, (2 * b + 2) * tile)
        first, last = max(0, b - 2), min(PAIRS, b + 3)
        block = dot3(*halves(t_own, first, last, tile), flat(high, slice(0, 2), n), flat(low, slice(0, 2), n))
        for a in range(first, last):
            gram[PAIRS * a + b] = block[2 * (a - first) * tile : 2 * (a - first + 1) * tile]

    def add(a, b, value):
        index = PAIRS * a + b + (PAIRS + 1) * rows.side_pair(0)
        gram[index] = gram[index] + value

    side_gram(rows, 0, (nearer, farther), t_swap, side_high, side_low, add, tile)


def refine_kernel(
    meta, z, z_high, z_low, t_near, early, edge, nearer, farther, first, second, refined, correction,
    high, low, late, d_high, d_low, d_own, update,
):
    tile = z.shape[-1]
    rows = Rows(meta)
    ends = rows.parity != jnp.where(rows.even_pair, 0, 1)

    def add(a, b, value):
        late[SIDE * a + b] = value

    side_gram(rows, 1, (nearer, farther), t_near, high, low, add, tile)
    eye = (
        lax.broadcasted_iota(jnp.int32, (tile, tile), 0) == lax.broadcasted_iota(jnp.int32, (tile, tile), 1)
    ).astype(F32)
    shift = rows.side_pair(1)
    for b in range(PAIRS):
        for a in range(max(0, b - 2), min(PAIRS, b + 3)):
            gram = early[PAIRS * a + b]
            ia, ib = a - shift, b - shift
            there = (ia >= 0) & (ia < SIDE) & (ib >= 0) & (ib < SIDE)
            part = late[jnp.clip(SIDE * ia + ib, 0, SIDE * SIDE - 1)]
            always = 0 < a < SIDE and 0 < b < SIDE
            gram = gram + (part if always else jnp.where(there, part, 0.0))
            e = a if b < 2 else a - 2
            if 0 <= e < 2:
                gram = gram + edge[2 * b + e]
            if a == b and a in (0, PAIRS - 1):
                one, other = (first, second) if a == 0 else (second, first)
                gram = gram + jnp.where(ends, one[...], other[...])
            for i in range(2):
                for j in range(2):
                    k, c = 2 * a + i, 2 * b + j
                    value = -gram[i * tile : (i + 1) * tile, j * tile : (j + 1) * tile]
                    if k == c:
                        value = value + eye
                    elif abs(k - c) <= REACH:
                        value = jnp.where(rows.present(k + COL0, c + COL0), value, 0.0)
                    else:
                        value = zero(tile)
                    put(d_high, d_low, k, c, tile, value)
                    if k + COL0 in (0, 1):
                        d_own[k + COL0, c] = value
        row_matmul(z_high, z_low, d_high, d_low, update, tile, (2 * b,))
    for i in range(OWN):
        for slot in range(2 * REACH):
            correction[i, slot] = d_own[i, rows.dense_slot(i, slot)]
            refined[i, slot] = z[i, slot] + 0.5 * update[i, rows.dense_slot(i, slot)]


def body(correlation, factor, pattern):
    rows_here, slots, tile = correlation.shape[:3]
    total = pattern.shape[0]
    assert rows_here == OWN and slots == 2 * REACH and total >= WIDE
    device = lax.axis_index(AXES)
    rows = (device * OWN + jnp.arange(LEFT, LEFT + WIDE, dtype=jnp.int32)) % total
    offsets = (pattern[rows][:, 1:] - rows[:, None] + total // 2) % total - total // 2
    expected = jnp.array([-3, -2, -1, 1, 2], jnp.int32)
    dropped = jnp.sum((offsets == expected).astype(jnp.int32), axis=1)
    place = jnp.stack([0] * WIDE + [device % 2, device // 2 % 2]).astype(jnp.int32)
    meta = jnp.concatenate([dropped, (device % 2)[None], (device // 2 % 2)[None]]).astype(jnp.int32)

    vmem = pl.BlockSpec(memory_space=pltpu.VMEM)
    smem = pl.BlockSpec(memory_space=pltpu.SMEM)

    def resident(value):
        if value is factor or value is correlation:
            return pltpu.with_memory_space_constraint(value, pltpu.HBM)
        return pltpu.with_memory_space_constraint(value, pltpu.VMEM)

    def call(kernel, ins, outs, scratch, flops, aliases={}):
        scalars = 1
        return pl.pallas_call(
            kernel,
            in_specs=[smem] * scalars + [vmem] * (len(ins) - scalars),
            out_specs=jax.tree.map(lambda _: vmem, outs),
            out_shape=outs,
            scratch_shapes=scratch,
            input_output_aliases=aliases,
            compiler_params=pltpu.CompilerParams(vmem_limit_bytes=VMEM_LIMIT),
            cost_estimate=pl.CostEstimate(flops=flops, bytes_accessed=4 << 20, transcendentals=0),
        )(*ins[:scalars], *map(resident, ins[scalars:]))

    def shape(*dims, dtype=F32):
        return jax.ShapeDtypeStruct(dims, dtype)

    def halves_of(n, m):
        return [pltpu.VMEM((n, tile, m * tile), BF16)] * 2

    row = shape(1, slots, tile, tile)
    seven = shape(len(UP), tile, tile)
    nine = shape(len(Z_UP), tile, tile)
    block = shape(2 * tile, 2 * tile)
    dense = pltpu.VMEM((OWN, COLS, tile, tile), F32)

    z0, z1, zi, zc = call(pack_kernel, (place, factor), (row, row, nine, nine), [], 1000)
    x = [send(v, swap) for v in (z0, z1)]
    zi, zc = send(zi, inside), send(zc, across)
    n = [send(x[r], near) for r in range(OWN)]
    sx = send(lax.dynamic_slice_in_dim(correlation, 1 - device % 2, 1, 0), swap)
    square = shape(COLS, tile, COLS * tile, dtype=BF16)
    pair = shape(OWN, tile, COLS * tile, dtype=BF16)
    ready = call(prepare_kernel, (meta, correlation, factor, *x), (square, square, pair, pair), [], int(1e9))
    p0, p1, pf, pi, pc, *_ = call(
        product_kernel,
        (meta, *ready, *n, zi, zc),
        (row, row, row, seven, seven, square, square),
        [dense],
        int(2e9),
        aliases={1: 5, 2: 6},
    )
    pc = send(pc, across)
    px = send(pf, swap)
    pi = send(pi, inside)
    width = 2 * REACH + 1
    ps = call(
        side_kernel,
        (meta, sx, factor, *x, *n, zi, zc),
        row,
        halves_of(width, width) + halves_of(1, width) + [pltpu.VMEM((width, tile, tile), F32)],
        int(2e9),
    )
    pn = (send(ps, near), send(px, near))

    def turned(columns):
        return shape(columns * tile, 4 * tile, dtype=BF16)

    z_kept, t_own, t_up, t_down, t_swap, t_near, t_far_up, t_far_down, *z_own = call(
        turn_kernel,
        (meta, factor, *x, *n, zi, zc, ps),
        (shape(*factor.shape), turned(COLS), turned(4), turned(4), turned(2 * SIDE), turned(2 * SIDE), turned(2), turned(2),
         *[shape(OWN, tile, COLS * tile, dtype=BF16)] * 2),
        [],
        int(2e9),
    )
    early = call(
        gram_kernel,
        (meta, t_own, t_swap, p0, p1, ps, px),
        shape(PAIRS * PAIRS, 2 * tile, 2 * tile),
        halves_of(2, COLS) + halves_of(2, 2 * SIDE),
        int(4e9),
    )
    edge, *far = call(
        edge_kernel,
        (meta, t_up, t_down, t_far_up, t_far_down, pi, pc, ps, px, early),
        (shape(2 * PAIRS, 2 * tile, 2 * tile), block, block),
        halves_of(2, COLS) + halves_of(2, 2),
        int(1e9),
    )
    far = (send(far[0], far_first), send(far[1], far_second))
    return call(
        refine_kernel,
        (meta, z_kept, *z_own, t_near, early, edge, *pn, *far),
        (shape(*factor.shape), shape(*factor.shape)),
        halves_of(2, 2 * SIDE)
        + [pltpu.VMEM((SIDE * SIDE, 2 * tile, 2 * tile), F32)]
        + halves_of(COLS, COLS)
        + [dense, dense],
        int(4e9),
    )


def solution(mesh):
    tiles = P(AXES, None, None, None)

    return jax.shard_map(body, mesh=mesh, in_specs=(tiles, tiles, P()), out_specs=(tiles, tiles), check_vma=False)
```

```python
import jax
import jax.numpy as jnp
from jax import lax
from jax.experimental import pallas as pl
from jax.experimental.pallas import tpu as pltpu
from jax.sharding import PartitionSpec as P


REACH = 3
AXES = ("blk", "sub")
OWN = 2
LEFT = -2 * REACH
WIDE = OWN + 4 * REACH
COL0 = -REACH
COLS = OWN + 2 * REACH
PAIRS = COLS // 2
SIDE = 3
VMEM_LIMIT = 24 << 20
F32 = jnp.float32
BF16 = jnp.bfloat16

UP = ((0, 3), (0, 4), (0, 5), (1, 0), (1, 3), (1, 4), (1, 5))
DOWN = ((0, 0), (0, 1), (0, 2), (0, 3), (1, 1), (1, 2), (1, 3))
Z_UP = ((0, 0), (0, 3), (0, 4), (0, 5), (1, 0), (1, 2), (1, 3), (1, 4), (1, 5))
Z_DOWN = ((0, 0), (0, 1), (0, 2), (0, 3), (0, 4), (1, 0), (1, 1), (1, 2), (1, 3))


def send(value, to):
    count = lax.axis_size(AXES)
    return lax.ppermute(value, AXES, [(i, to(i) % count) for i in range(count)])


def swap(i):
    return i ^ 1


def inside(i):
    return i ^ 2


def across(i):
    return i + 2 if i // 2 % 2 else i - 2


def near(i):
    return i + 2 if i % 2 == 0 else i - 2


def far_first(i):
    return i + (1, 1, -2, -4)[i % 4]


def far_second(i):
    return i + (4, 2, -1, -1)[i % 4]


def split(value):
    high = value.astype(BF16)
    low = (value - high.astype(F32)).astype(BF16)
    return high, low


def dot3(a_high, a_low, b_high, b_low):
    left = jnp.concatenate([a_high, a_low, a_high], axis=1)
    right = jnp.concatenate([b_high, b_high, b_low], axis=0)
    return jnp.dot(left, right, preferred_element_type=F32)


def slot_of(offset, dropped):
    pos = offset + REACH - jnp.where(offset > 0, 1, 0)
    slot = jnp.where(offset == 0, 0, pos + 1 - jnp.where(pos > dropped, 1, 0))
    there = (jnp.abs(offset) <= REACH) & ((offset == 0) | (pos != dropped))
    return jnp.clip(slot, 0, 2 * REACH - 1), there


class Rows:
    def __init__(self, meta):
        self.meta = meta
        self.parity = meta[WIDE]
        self.even_pair = meta[WIDE + 1] == 0

    def dropped(self, row):
        return self.meta[row - LEFT]

    def side_row(self, side):
        return 2 - 4 * jnp.bitwise_xor(self.parity, side)

    def side_pair(self, side):
        return 1 - jnp.bitwise_xor(self.parity, side)

    def present(self, row, col):
        return slot_of(jnp.int32(col - row), self.dropped(row))[1]

    def own(self, refs, row, col):
        slot, there = slot_of(jnp.int32(col - row), self.dropped(row))
        tile = refs[row][0, slot] if isinstance(refs, tuple) else refs[row, slot]
        return jnp.where(there, tile, 0.0)

    def packed(self, refs, layout, row0, r, col):
        slots = [s for rr, s in layout if rr == r]
        base = [j for j, (rr, _) in enumerate(layout) if rr == r][0]
        row = row0 + r
        if col == row:
            index = base + slots.index(0)
            return jnp.where(self.even_pair, refs[0][index], refs[1][index])
        slot, there = slot_of(jnp.int32(col - row), self.dropped(row))
        rest = [s for s in slots if s]
        index = base + slots.index(rest[0]) + jnp.clip(slot - rest[0], 0, len(rest) - 1)
        return jnp.where(there, jnp.where(self.even_pair, refs[0][index], refs[1][index]), 0.0)

    def side(self, ref, side, r, col):
        row = self.side_row(side) + r
        slot, there = slot_of(col - row, self.dropped(row))
        return jnp.where(there, ref[0, slot], 0.0)

    def by_distance(self, refs):
        return tuple(zip(refs, (self.parity, 1 - self.parity)))

    def dense_slot(self, row, slot):
        if slot == 0:
            return row - COL0
        pos = slot - 1 + jnp.where(slot - 1 >= self.dropped(row), 1, 0)
        return row - COL0 - REACH + pos + jnp.where(pos >= REACH, 1, 0)


def zero(tile):
    return jnp.zeros((tile, tile), F32)


def put(high, low, r, c, tile, value):
    h, l = split(value)
    high[r, :, c * tile : (c + 1) * tile] = h
    low[r, :, c * tile : (c + 1) * tile] = l


def flat(ref, rows, cols):
    value = ref[rows, :, cols]
    return value.reshape(value.shape[0] * value.shape[1], value.shape[2])


def row_matmul(left_high, left_low, right_high, right_low, out, tile, columns=range(0, COLS, 2)):
    for c in columns:
        lo, hi = max(c - REACH, 0), min(c + 1 + REACH, COLS - 1) + 1
        k = slice(lo * tile, hi * tile)
        n = slice(c * tile, (c + 2) * tile)
        block = dot3(
            flat(left_high, slice(None), k),
            flat(left_low, slice(None), k),
            flat(right_high, slice(lo, hi), n),
            flat(right_low, slice(lo, hi), n),
        )
        for i in range(OWN):
            for j in range(2):
                out[i, c + j] = block[i * tile : (i + 1) * tile, j * tile : (j + 1) * tile]


def both(layouts, tile_of, rows, chip, link):
    for even, outs in ((True, (chip, link)), (False, (link, chip))):

        @pl.when(rows.even_pair == even)
        def _():
            for out, layout in zip(outs, layouts):
                for j, place in enumerate(layout):
                    out[j] = tile_of(*place)


def pack_kernel(meta, z, z0, z1, chip, link):
    for r, out in enumerate((z0, z1)):
        for slot in range(2 * REACH):
            out[0, slot] = z[r, slot]
    both((Z_UP, Z_DOWN), lambda i, slot: z[i, slot], Rows(meta), chip, link)


def far_tile(rows, refs, sign, r, c, tile):
    if sign > 0:
        offset = REACH - c if r == 0 else REACH - 1 + c
        there = r == 1 or c == 0
    else:
        offset = -REACH + c if r == 0 else -REACH + 1 - c
        there = r == 0 or c == 1
    if not there:
        return zero(tile)
    slot, present = slot_of(jnp.int32(offset), rows.dropped(rows.side_row(0) + r))
    if len(refs) == 1:
        value = refs[0][0, slot]
    else:
        a, b = refs if r == 0 else refs[::-1]
        value = jnp.where(rows.parity == 0, a[0, slot], b[0, slot])
    return jnp.where(present, value, 0.0)


def tiles_of(tile, columns=range(PAIRS)):
    for b in columns:
        for a in range(max(0, b - 2), min(PAIRS, b + 3)):
            for i in range(2):
                for j in range(2):
                    yield a, b, 2 * a + i, 2 * b + j, (pl.ds(i * tile, tile), pl.ds(j * tile, tile))


def edge_kernel(
    meta, t_up, t_down, t_far_up, t_far_down, pi, pc, nearer, farther, early, base, first, second,
    high, low, far_high, far_low, edge,
):
    tile = nearer.shape[-1]
    rows = Rows(meta)
    for r in range(2):
        for c in range(4):
            col = c + COL0
            value = rows.packed((pc, pi), UP, -4, r, col) if abs(col - (r - 4)) <= REACH else zero(tile)
            put(high, low, r, c, tile, value)
            col = c + COL0 + 4
            value = rows.packed((pi, pc), DOWN, 4, r, col) if abs(col - (r + 4)) <= REACH else zero(tile)
            put(high, low, r, 4 + c, tile, value)
    for b in range(PAIRS):
        n = slice(2 * b * tile, (2 * b + 2) * tile)
        block = dot3(
            *halves(t_up if b < 2 else t_down, 0, 2, tile), flat(high, slice(None), n), flat(low, slice(None), n)
        )
        for e in range(2):
            edge[2 * b + e] = block[2 * e * tile : (2 * e + 2) * tile]

    def far_block(turned, sign, out):
        for r in range(2):
            for c in range(2):
                put(far_high, far_low, r, c, tile, far_tile(rows, (nearer, farther), sign, r, c, tile))
        whole = slice(None), slice(None)
        out[...] = dot3(*halves(turned, 0, 1, tile), flat(far_high, *whole), flat(far_low, *whole))

    @pl.when(rows.even_pair)
    def _():
        first[...] = edge[3]
        far_block(t_far_up, 1, second)

    @pl.when(jnp.logical_not(rows.even_pair))
    def _():
        far_block(t_far_down, -1, first)
        second[...] = edge[4]

    eye = (
        lax.broadcasted_iota(jnp.int32, (tile, tile), 0) == lax.broadcasted_iota(jnp.int32, (tile, tile), 1)
    ).astype(F32)
    for a, b, k, c, inner in tiles_of(tile):
        gram = early[PAIRS * a + b, inner[0], inner[1]]
        e = a if b < 2 else a - 2
        if 0 <= e < 2:
            gram = gram + edge[2 * b + e, inner[0], inner[1]]
        value = -gram
        if k == c:
            value = value + eye
        elif abs(k - c) <= REACH:
            value = jnp.where(rows.present(k + COL0, c + COL0), value, 0.0)
        else:
            value = zero(tile)
        base[PAIRS * a + b, inner[0], inner[1]] = value


def prepare_kernel(meta, s, z, x0, x1, z_high, z_low, s_high, s_low):
    tile = z.shape[-1]
    rows = Rows(meta)
    for c in range(COLS):
        col = c + COL0
        for i in range(OWN):
            near_by = abs(col - i) <= REACH
            put(s_high, s_low, i, c, tile, rows.own(s, i, col) if near_by else zero(tile))
            put(z_high, z_low, i - COL0, c, tile, rows.own(z, i, col) if near_by else zero(tile))
            put(z_high, z_low, rows.side_row(0) + i - COL0, c, tile, rows.side((x0, x1)[i], 0, i, col))


def product_kernel(
    meta, z_high_in, z_low_in, s_high, s_low, n0, n1, zi, zc, p0, p1, pf, chip, link, z_high, z_low, dense
):
    tile = n0.shape[-1]
    rows = Rows(meta)
    for c in range(COLS):
        col = c + COL0
        for r, ref in enumerate((n0, n1)):
            put(z_high, z_low, rows.side_row(1) + r - COL0, c, tile, rows.side(ref, 1, r, col))
        value = rows.packed((zc, zi), Z_UP, -4, 1, col) if col <= 0 else zero(tile)
        put(z_high, z_low, 0, c, tile, value)
        value = rows.packed((zi, zc), Z_DOWN, 4, 0, col) if col >= 1 else zero(tile)
        put(z_high, z_low, COLS - 1, c, tile, value)
    row_matmul(s_high, s_low, z_high, z_low, dense, tile)
    for i, ref in enumerate((p0, p1)):
        for slot in range(2 * REACH):
            ref[0, slot] = dense[i, rows.dense_slot(i, slot)]
    for slot in range(2 * REACH):
        pf[0, slot] = dense[rows.parity, rows.dense_slot(rows.parity, slot)]
    both((UP, DOWN), lambda i, slot: dense[i, rows.dense_slot(i, slot)], rows, chip, link)


def side_kernel(meta, s, z, x0, x1, n0, n1, zi, zc, out, z_high, z_low, s_high, s_low, dense):
    tile = s.shape[-1]
    rows = Rows(meta)
    width = 2 * REACH + 1

    def own():
        return lambda row, col: rows.own(z, row, col)

    def swapped(r):
        return lambda row, col: rows.side((x0, x1)[r], 0, r, col)

    def relayed(r):
        return lambda row, col: rows.side((n0, n1)[r], 1, r, col)

    def from_down(r):
        return lambda row, col: rows.packed((zc, zi), Z_UP, -4, r, col)

    def from_up(r):
        return lambda row, col: rows.packed((zi, zc), Z_DOWN, 4, r, col)

    even = (relayed(1), own(), own(), swapped(0), swapped(1), from_up(0), from_up(1))
    odd = (from_down(0), from_down(1), swapped(0), swapped(1), own(), own(), relayed(0))
    for parity, sources in ((0, even), (1, odd)):

        @pl.when(rows.parity == parity)
        def _():
            centre = OWN if parity == 0 else -1
            first = centre - REACH
            for k in range(width):
                for c in range(width):
                    there = abs(k - c) <= REACH
                    put(z_high, z_low, k, c, tile, sources[k](first + k, first + c) if there else zero(tile))

    centre = jnp.where(rows.parity == 0, OWN, -1)
    dropped = rows.dropped(centre)
    for c in range(width):
        slot, there = slot_of(jnp.int32(c - REACH), dropped)
        put(s_high, s_low, 0, c, tile, jnp.where(there, s[0, slot], 0.0))
    for c in range(0, width, 2):
        last = min(c + 2, width)
        lo, hi = max(c - REACH, 0), min(last - 1 + REACH, width - 1) + 1
        n = slice(c * tile, last * tile)
        k = slice(lo * tile, hi * tile)
        block = dot3(
            flat(s_high, slice(None), k),
            flat(s_low, slice(None), k),
            flat(z_high, slice(lo, hi), n),
            flat(z_low, slice(lo, hi), n),
        )
        for j in range(last - c):
            dense[c + j] = block[:, j * tile : (j + 1) * tile]
    for slot in range(2 * REACH):
        pos = slot - 1 + jnp.where(slot - 1 >= dropped, 1, 0)
        out[0, slot] = dense[REACH if slot == 0 else pos + jnp.where(pos >= REACH, 1, 0)]


def turn_kernel(meta, z, x0, x1, n0, n1, zi, zc, after, z_kept, t_own, t_up, t_down, t_swap, t_near, t_far_up, t_far_down, z_high, z_low):
    tile = z.shape[-1]
    rows = Rows(meta)

    z_kept[...] = z[...]

    def store(out, c, r, value):
        high, low = split(value.T)
        out[c * tile : (c + 1) * tile, r * tile : (r + 1) * tile] = high
        out[c * tile : (c + 1) * tile, (2 + r) * tile : (3 + r) * tile] = low

    for r in range(2):
        for c in range(COLS):
            col = c + COL0
            value = rows.own(z, r, col) if abs(col - r) <= REACH else zero(tile)
            store(t_own, c, r, value)
            put(z_high, z_low, r, c, tile, value)
        for c in range(4):
            col = c + COL0
            store(t_up, c, r, rows.packed((zc, zi), Z_UP, -4, r, col) if abs(col - (r - 4)) <= REACH else zero(tile))
            col = c + COL0 + 4
            store(t_down, c, r, rows.packed((zi, zc), Z_DOWN, 4, r, col) if abs(col - (r + 4)) <= REACH else zero(tile))
        for c in range(2):
            store(t_far_up, c, r, far_tile(rows, ((x0, x1)[r],), 1, r, c, tile))
            store(t_far_down, c, r, far_tile(rows, ((x0, x1)[r],), -1, r, c, tile))
        for side, (out, refs) in enumerate(((t_swap, (x0, x1)), (t_near, (n0, n1)))):
            first = 2 * rows.side_pair(side) + COL0
            for c in range(2 * SIDE):
                store(out, c, r, rows.side(refs[r], side, r, first + c))


def halves(turned, first, last, tile):
    part = turned[2 * first * tile : 2 * last * tile]
    return part[:, : 2 * tile], part[:, 2 * tile :]


def side_gram(rows, side, refs, turned, high, low, add, tile):
    first = 2 * rows.side_pair(side) + COL0
    for ref, r in rows.by_distance(refs):
        for c in range(2 * SIDE):
            put(high, low, r, c, tile, rows.side(ref, side, r, first + c))
    left = halves(turned, 0, SIDE, tile)
    for b in range(SIDE):
        n = slice(2 * b * tile, (2 * b + 2) * tile)
        block = dot3(*left, flat(high, slice(0, 2), n), flat(low, slice(0, 2), n))
        for a in range(SIDE):
            add(a, b, block[2 * a * tile : (2 * a + 2) * tile])
        yield


def gram_kernel(meta, t_own, t_swap, p0, p1, nearer, farther, gram, high, low, side_high, side_low):
    tile = p0.shape[-1]
    rows = Rows(meta)
    for r in range(2):
        for c in range(COLS):
            col = c + COL0
            put(high, low, r, c, tile, rows.own((p0, p1), r, col) if abs(col - r) <= REACH else zero(tile))
    for b in range(PAIRS):
        n = slice(2 * b * tile, (2 * b + 2) * tile)
        first, last = max(0, b - 2), min(PAIRS, b + 3)
        block = dot3(*halves(t_own, first, last, tile), flat(high, slice(0, 2), n), flat(low, slice(0, 2), n))
        for a in range(first, last):
            gram[PAIRS * a + b] = block[2 * (a - first) * tile : 2 * (a - first + 1) * tile]

    def add(a, b, value):
        index = PAIRS * a + b + (PAIRS + 1) * rows.side_pair(0)
        gram[index] = gram[index] + value

    for _ in side_gram(rows, 0, (nearer, farther), t_swap, side_high, side_low, add, tile):
        pass


def refine_kernel(
    meta, z, z_high, z_low, t_near, base, nearer, farther, first, second, refined, correction,
    high, low, late, d_high, d_low, d_own, update, d_out, z_out, sems,
):
    tile = z.shape[-1]
    rows = Rows(meta)
    ends = rows.parity != jnp.where(rows.even_pair, 0, 1)
    shift = rows.side_pair(1)

    def add(a, b, value):
        late[SIDE * a + b] = value

    def finish(column):
        for a, b, k, c, inner in tiles_of(tile, (column,)):
            value = base[PAIRS * a + b, inner[0], inner[1]]
            if abs(k - c) <= REACH:
                ia, ib = a - shift, b - shift
                there = rows.present(k + COL0, c + COL0)
                if not (0 < a < SIDE and 0 < b < SIDE):
                    there = there & (ia >= 0) & (ia < SIDE) & (ib >= 0) & (ib < SIDE)
                gram = late[jnp.clip(SIDE * ia + ib, 0, SIDE * SIDE - 1), inner[0], inner[1]]
                value = value - jnp.where(there, gram, 0.0)
                if a == b and a in (0, PAIRS - 1):
                    one, other = (first, second) if a == 0 else (second, first)
                    far = jnp.where(ends, one[inner[0], inner[1]], other[inner[0], inner[1]])
                    value = value - (far if k == c else jnp.where(rows.present(k + COL0, c + COL0), far, 0.0))
            put(d_high, d_low, k, c, tile, value)
            if k + COL0 in (0, 1):
                d_own[k + COL0, c] = value

    def multiply(column):
        row_matmul(z_high, z_low, d_high, d_low, update, tile, (2 * column,))

    steps = side_gram(rows, 1, (nearer, farther), t_near, high, low, add, tile)
    next(steps)
    next(steps)
    finish(0)
    next(steps)
    finish(1)
    multiply(0)
    finish(2)
    multiply(1)
    finish(3)
    multiply(2)
    for i in range(OWN):
        for slot in range(2 * REACH):
            d_out[i, slot] = d_own[i, rows.dense_slot(i, slot)]
    copies = [pltpu.make_async_copy(d_out, correction, sems.at[OWN])]
    copies[0].start()
    multiply(3)
    for i in range(OWN):
        for slot in range(2 * REACH):
            z_out[i, slot] = z[i, slot] + 0.5 * update[i, rows.dense_slot(i, slot)]
        copies.append(pltpu.make_async_copy(z_out.at[i], refined.at[i], sems.at[i]))
        copies[-1].start()
    for copy in copies:
        copy.wait()


def body(correlation, factor, pattern):
    rows_here, slots, tile = correlation.shape[:3]
    total = pattern.shape[0]
    assert rows_here == OWN and slots == 2 * REACH and total >= WIDE
    device = lax.axis_index(AXES)
    rows = (device * OWN + jnp.arange(LEFT, LEFT + WIDE, dtype=jnp.int32)) % total
    offsets = (pattern[rows][:, 1:] - rows[:, None] + total // 2) % total - total // 2
    expected = jnp.array([-3, -2, -1, 1, 2], jnp.int32)
    dropped = jnp.sum((offsets == expected).astype(jnp.int32), axis=1)
    place = jnp.stack([0] * WIDE + [device % 2, device // 2 % 2]).astype(jnp.int32)
    meta = jnp.concatenate([dropped, (device % 2)[None], (device // 2 % 2)[None]]).astype(jnp.int32)

    vmem = pl.BlockSpec(memory_space=pltpu.VMEM)
    smem = pl.BlockSpec(memory_space=pltpu.SMEM)

    def resident(value):
        if value is factor or value is correlation:
            return pltpu.with_memory_space_constraint(value, pltpu.HBM)
        return pltpu.with_memory_space_constraint(value, pltpu.VMEM)

    def call(kernel, ins, outs, scratch, flops, aliases={}, where=pltpu.VMEM):
        scalars = 1
        return pl.pallas_call(
            kernel,
            in_specs=[smem] * scalars + [vmem] * (len(ins) - scalars),
            out_specs=jax.tree.map(lambda _: pl.BlockSpec(memory_space=where), outs),
            out_shape=outs,
            scratch_shapes=scratch,
            input_output_aliases=aliases,
            compiler_params=pltpu.CompilerParams(vmem_limit_bytes=VMEM_LIMIT),
            cost_estimate=pl.CostEstimate(flops=flops, bytes_accessed=4 << 20, transcendentals=0),
        )(*ins[:scalars], *map(resident, ins[scalars:]))

    def shape(*dims, dtype=F32):
        return jax.ShapeDtypeStruct(dims, dtype)

    def halves_of(n, m):
        return [pltpu.VMEM((n, tile, m * tile), BF16)] * 2

    row = shape(1, slots, tile, tile)
    seven = shape(len(UP), tile, tile)
    nine = shape(len(Z_UP), tile, tile)
    block = shape(2 * tile, 2 * tile)
    dense = pltpu.VMEM((OWN, COLS, tile, tile), F32)

    z0, z1, zi, zc = call(pack_kernel, (place, factor), (row, row, nine, nine), [], 1000)
    x = [send(v, swap) for v in (z0, z1)]
    zi, zc = send(zi, inside), send(zc, across)
    n = [send(x[r], near) for r in range(OWN)]
    sx = send(lax.dynamic_slice_in_dim(correlation, 1 - device % 2, 1, 0), swap)
    square = shape(COLS, tile, COLS * tile, dtype=BF16)
    pair = shape(OWN, tile, COLS * tile, dtype=BF16)
    ready = call(prepare_kernel, (meta, correlation, factor, *x), (square, square, pair, pair), [], int(1e9))
    p0, p1, pf, pi, pc, *_ = call(
        product_kernel,
        (meta, *ready, *n, zi, zc),
        (row, row, row, seven, seven, square, square),
        [dense],
        int(2e9),
        aliases={1: 5, 2: 6},
    )
    pc = send(pc, across)
    px = send(pf, swap)
    pi = send(pi, inside)
    width = 2 * REACH + 1
    ps = call(
        side_kernel,
        (meta, sx, factor, *x, *n, zi, zc),
        row,
        halves_of(width, width) + halves_of(1, width) + [pltpu.VMEM((width, tile, tile), F32)],
        int(2e9),
    )
    pn = (send(ps, near), send(px, near))

    def turned(columns):
        return shape(columns * tile, 4 * tile, dtype=BF16)

    z_kept, t_own, t_up, t_down, t_swap, t_near, t_far_up, t_far_down, *z_own = call(
        turn_kernel,
        (meta, factor, *x, *n, zi, zc, ps),
        (shape(*factor.shape), turned(COLS), turned(4), turned(4), turned(2 * SIDE), turned(2 * SIDE), turned(2), turned(2),
         *[shape(OWN, tile, COLS * tile, dtype=BF16)] * 2),
        [],
        int(2e9),
    )
    early = call(
        gram_kernel,
        (meta, t_own, t_swap, p0, p1, ps, px),
        shape(PAIRS * PAIRS, 2 * tile, 2 * tile),
        halves_of(2, COLS) + halves_of(2, 2 * SIDE),
        int(4e9),
    )
    base, *far = call(
        edge_kernel,
        (meta, t_up, t_down, t_far_up, t_far_down, pi, pc, ps, px, early),
        (shape(PAIRS * PAIRS, 2 * tile, 2 * tile), block, block),
        halves_of(2, COLS) + halves_of(2, 2) + [pltpu.VMEM((2 * PAIRS, 2 * tile, 2 * tile), F32)],
        int(1e9),
    )
    far = (send(far[0], far_first), send(far[1], far_second))
    return call(
        refine_kernel,
        (meta, z_kept, *z_own, t_near, base, *pn, *far),
        (shape(*factor.shape), shape(*factor.shape)),
        halves_of(2, 2 * SIDE)
        + [pltpu.VMEM((SIDE * SIDE, 2 * tile, 2 * tile), F32)]
        + halves_of(COLS, COLS)
        + [dense, dense, pltpu.VMEM(factor.shape, F32), pltpu.VMEM(factor.shape, F32), pltpu.SemaphoreType.DMA((OWN + 1,))],
        int(4e9),
        where=pl.ANY,
    )


def solution(mesh):
    tiles = P(AXES, None, None, None)

    return jax.shard_map(body, mesh=mesh, in_specs=(tiles, tiles, P()), out_specs=(tiles, tiles), check_vma=False)
```

```python
import jax
import jax.numpy as jnp
from jax import lax
from jax.experimental import pallas as pl
from jax.experimental.pallas import tpu as pltpu
from jax.sharding import PartitionSpec as P


REACH = 3
AXES = ("blk", "sub")
OWN = 2
LEFT = -2 * REACH
WIDE = OWN + 4 * REACH
COL0 = -REACH
COLS = OWN + 2 * REACH
PAIRS = COLS // 2
SIDE = 3
VMEM_LIMIT = 24 << 20
F32 = jnp.float32
BF16 = jnp.bfloat16

UP = ((0, 3), (0, 4), (0, 5), (1, 0), (1, 3), (1, 4), (1, 5))
DOWN = ((0, 0), (0, 1), (0, 2), (0, 3), (1, 1), (1, 2), (1, 3))
Z_UP = ((0, 0), (0, 3), (0, 4), (0, 5), (1, 0), (1, 2), (1, 3), (1, 4), (1, 5))
Z_DOWN = ((0, 0), (0, 1), (0, 2), (0, 3), (0, 4), (1, 0), (1, 1), (1, 2), (1, 3))


def send(value, to):
    count = lax.axis_size(AXES)
    return lax.ppermute(value, AXES, [(i, to(i) % count) for i in range(count)])


def swap(i):
    return i ^ 1


def inside(i):
    return i ^ 2


def across(i):
    return i + 2 if i // 2 % 2 else i - 2


def near(i):
    return i + 2 if i % 2 == 0 else i - 2


def far_first(i):
    return i + (1, 1, -2, -4)[i % 4]


def far_second(i):
    return i + (4, 2, -1, -1)[i % 4]


def split(value):
    high = value.astype(BF16)
    low = (value - high.astype(F32)).astype(BF16)
    return high, low


def dot3(a_high, a_low, b_high, b_low):
    left = jnp.concatenate([a_high, a_low, a_high], axis=1)
    right = jnp.concatenate([b_high, b_high, b_low], axis=0)
    return jnp.dot(left, right, preferred_element_type=F32)


def slot_of(offset, dropped):
    pos = offset + REACH - jnp.where(offset > 0, 1, 0)
    slot = jnp.where(offset == 0, 0, pos + 1 - jnp.where(pos > dropped, 1, 0))
    there = (jnp.abs(offset) <= REACH) & ((offset == 0) | (pos != dropped))
    return jnp.clip(slot, 0, 2 * REACH - 1), there


class Rows:
    def __init__(self, meta):
        self.meta = meta
        self.parity = meta[WIDE]
        self.even_pair = meta[WIDE + 1] == 0

    def dropped(self, row):
        return self.meta[row - LEFT]

    def side_row(self, side):
        return 2 - 4 * jnp.bitwise_xor(self.parity, side)

    def side_pair(self, side):
        return 1 - jnp.bitwise_xor(self.parity, side)

    def present(self, row, col):
        return slot_of(jnp.int32(col - row), self.dropped(row))[1]

    def own(self, refs, row, col):
        slot, there = slot_of(jnp.int32(col - row), self.dropped(row))
        tile = refs[row][0, slot] if isinstance(refs, tuple) else refs[row, slot]
        return jnp.where(there, tile, 0.0)

    def packed(self, refs, layout, row0, r, col):
        slots = [s for rr, s in layout if rr == r]
        base = [j for j, (rr, _) in enumerate(layout) if rr == r][0]
        row = row0 + r
        if col == row:
            index = base + slots.index(0)
            return jnp.where(self.even_pair, refs[0][index], refs[1][index])
        slot, there = slot_of(jnp.int32(col - row), self.dropped(row))
        rest = [s for s in slots if s]
        index = base + slots.index(rest[0]) + jnp.clip(slot - rest[0], 0, len(rest) - 1)
        return jnp.where(there, jnp.where(self.even_pair, refs[0][index], refs[1][index]), 0.0)

    def side(self, ref, side, r, col):
        row = self.side_row(side) + r
        slot, there = slot_of(col - row, self.dropped(row))
        return jnp.where(there, ref[0, slot], 0.0)

    def by_distance(self, refs):
        return tuple(zip(refs, (self.parity, 1 - self.parity)))

    def dense_slot(self, row, slot):
        if slot == 0:
            return row - COL0
        pos = slot - 1 + jnp.where(slot - 1 >= self.dropped(row), 1, 0)
        return row - COL0 - REACH + pos + jnp.where(pos >= REACH, 1, 0)


def zero(tile):
    return jnp.zeros((tile, tile), F32)


def put(high, low, r, c, tile, value):
    h, l = split(value)
    high[r, :, c * tile : (c + 1) * tile] = h
    low[r, :, c * tile : (c + 1) * tile] = l


def flat(ref, rows, cols):
    value = ref[rows, :, cols]
    return value.reshape(value.shape[0] * value.shape[1], value.shape[2])


def row_matmul(left_high, left_low, right_high, right_low, out, tile, columns=range(0, COLS, 2)):
    for c in columns:
        lo, hi = max(c - REACH, 0), min(c + 1 + REACH, COLS - 1) + 1
        k = slice(lo * tile, hi * tile)
        n = slice(c * tile, (c + 2) * tile)
        block = dot3(
            flat(left_high, slice(None), k),
            flat(left_low, slice(None), k),
            flat(right_high, slice(lo, hi), n),
            flat(right_low, slice(lo, hi), n),
        )
        for i in range(OWN):
            for j in range(2):
                out[i, c + j] = block[i * tile : (i + 1) * tile, j * tile : (j + 1) * tile]


def both(layouts, tile_of, rows, chip, link):
    for even, outs in ((True, (chip, link)), (False, (link, chip))):

        @pl.when(rows.even_pair == even)
        def _():
            for out, layout in zip(outs, layouts):
                for j, place in enumerate(layout):
                    out[j] = tile_of(*place)


def pack_kernel(meta, z, z0, z1, chip, link):
    for r, out in enumerate((z0, z1)):
        for slot in range(2 * REACH):
            out[0, slot] = z[r, slot]
    both((Z_UP, Z_DOWN), lambda i, slot: z[i, slot], Rows(meta), chip, link)


def far_tile(rows, refs, sign, r, c, tile):
    if sign > 0:
        offset = REACH - c if r == 0 else REACH - 1 + c
        there = r == 1 or c == 0
    else:
        offset = -REACH + c if r == 0 else -REACH + 1 - c
        there = r == 0 or c == 1
    if not there:
        return zero(tile)
    slot, present = slot_of(jnp.int32(offset), rows.dropped(rows.side_row(0) + r))
    if len(refs) == 1:
        value = refs[0][0, slot]
    else:
        a, b = refs if r == 0 else refs[::-1]
        value = jnp.where(rows.parity == 0, a[0, slot], b[0, slot])
    return jnp.where(present, value, 0.0)


def far_kernel(meta, t_up, t_down, t_far_up, t_far_down, pi, pc, nearer, farther, after, first, second, high, low):
    tile = nearer.shape[-1]
    rows = Rows(meta)

    def block(turned, place, out, tile_of):
        for r in range(2):
            for c in range(2):
                put(high, low, r, c, tile, tile_of(r, c))
        out[...] = dot3(*halves(turned, place, place + 1, tile), flat(high, slice(None), slice(None)), flat(low, slice(None), slice(None)))

    def swapped(sign):
        return lambda r, c: far_tile(rows, (nearer, farther), sign, r, c, tile)

    def from_down(r, c):
        return rows.packed((pc, pi), UP, -4, r, c - 1) if c - 1 - (r - 4) <= REACH else zero(tile)

    def from_up(r, c):
        return rows.packed((pi, pc), DOWN, 4, r, c + 1) if r + 4 - (c + 1) <= REACH else zero(tile)

    @pl.when(rows.even_pair)
    def _():
        block(t_up, 1, first, from_down)
        block(t_far_up, 0, second, swapped(1))

    @pl.when(jnp.logical_not(rows.even_pair))
    def _():
        block(t_far_down, 0, first, swapped(-1))
        block(t_down, 0, second, from_up)


def tiles_of(tile, columns=range(PAIRS)):
    for b in columns:
        for a in range(max(0, b - 2), min(PAIRS, b + 3)):
            for i in range(2):
                for j in range(2):
                    yield a, b, 2 * a + i, 2 * b + j, (pl.ds(i * tile, tile), pl.ds(j * tile, tile))


def edge_kernel(
    meta, t_up, t_down, pi, pc, early, base, high, low, edge,
):
    tile = pi.shape[-1]
    rows = Rows(meta)
    for r in range(2):
        for c in range(4):
            col = c + COL0
            value = rows.packed((pc, pi), UP, -4, r, col) if abs(col - (r - 4)) <= REACH else zero(tile)
            put(high, low, r, c, tile, value)
            col = c + COL0 + 4
            value = rows.packed((pi, pc), DOWN, 4, r, col) if abs(col - (r + 4)) <= REACH else zero(tile)
            put(high, low, r, 4 + c, tile, value)
    for b in range(PAIRS):
        n = slice(2 * b * tile, (2 * b + 2) * tile)
        block = dot3(
            *halves(t_up if b < 2 else t_down, 0, 2, tile), flat(high, slice(None), n), flat(low, slice(None), n)
        )
        for e in range(2):
            edge[2 * b + e] = block[2 * e * tile : (2 * e + 2) * tile]

    eye = (
        lax.broadcasted_iota(jnp.int32, (tile, tile), 0) == lax.broadcasted_iota(jnp.int32, (tile, tile), 1)
    ).astype(F32)
    for a, b, k, c, inner in tiles_of(tile):
        gram = early[PAIRS * a + b, inner[0], inner[1]]
        e = a if b < 2 else a - 2
        if 0 <= e < 2:
            gram = gram + edge[2 * b + e, inner[0], inner[1]]
        value = -gram
        if k == c:
            value = value + eye
        elif abs(k - c) <= REACH:
            value = jnp.where(rows.present(k + COL0, c + COL0), value, 0.0)
        else:
            value = zero(tile)
        base[PAIRS * a + b, inner[0], inner[1]] = value


def prepare_kernel(meta, s, z, x0, x1, z_high, z_low, s_high, s_low):
    tile = z.shape[-1]
    rows = Rows(meta)
    for c in range(COLS):
        col = c + COL0
        for i in range(OWN):
            near_by = abs(col - i) <= REACH
            put(s_high, s_low, i, c, tile, rows.own(s, i, col) if near_by else zero(tile))
            put(z_high, z_low, i - COL0, c, tile, rows.own(z, i, col) if near_by else zero(tile))
            put(z_high, z_low, rows.side_row(0) + i - COL0, c, tile, rows.side((x0, x1)[i], 0, i, col))


def product_kernel(
    meta, z_high_in, z_low_in, s_high, s_low, n0, n1, zi, zc, p0, p1, pf, chip, link, z_high, z_low, dense
):
    tile = n0.shape[-1]
    rows = Rows(meta)
    for c in range(COLS):
        col = c + COL0
        for r, ref in enumerate((n0, n1)):
            put(z_high, z_low, rows.side_row(1) + r - COL0, c, tile, rows.side(ref, 1, r, col))
        value = rows.packed((zc, zi), Z_UP, -4, 1, col) if col <= 0 else zero(tile)
        put(z_high, z_low, 0, c, tile, value)
        value = rows.packed((zi, zc), Z_DOWN, 4, 0, col) if col >= 1 else zero(tile)
        put(z_high, z_low, COLS - 1, c, tile, value)
    row_matmul(s_high, s_low, z_high, z_low, dense, tile)
    for i, ref in enumerate((p0, p1)):
        for slot in range(2 * REACH):
            ref[0, slot] = dense[i, rows.dense_slot(i, slot)]
    for slot in range(2 * REACH):
        pf[0, slot] = dense[rows.parity, rows.dense_slot(rows.parity, slot)]
    both((UP, DOWN), lambda i, slot: dense[i, rows.dense_slot(i, slot)], rows, chip, link)


def side_kernel(meta, s, z, x0, x1, n0, n1, zi, zc, out, z_high, z_low, s_high, s_low, dense):
    tile = s.shape[-1]
    rows = Rows(meta)
    width = 2 * REACH + 1

    def own():
        return lambda row, col: rows.own(z, row, col)

    def swapped(r):
        return lambda row, col: rows.side((x0, x1)[r], 0, r, col)

    def relayed(r):
        return lambda row, col: rows.side((n0, n1)[r], 1, r, col)

    def from_down(r):
        return lambda row, col: rows.packed((zc, zi), Z_UP, -4, r, col)

    def from_up(r):
        return lambda row, col: rows.packed((zi, zc), Z_DOWN, 4, r, col)

    even = (relayed(1), own(), own(), swapped(0), swapped(1), from_up(0), from_up(1))
    odd = (from_down(0), from_down(1), swapped(0), swapped(1), own(), own(), relayed(0))
    for parity, sources in ((0, even), (1, odd)):

        @pl.when(rows.parity == parity)
        def _():
            centre = OWN if parity == 0 else -1
            first = centre - REACH
            for k in range(width):
                for c in range(width):
                    there = abs(k - c) <= REACH
                    put(z_high, z_low, k, c, tile, sources[k](first + k, first + c) if there else zero(tile))

    centre = jnp.where(rows.parity == 0, OWN, -1)
    dropped = rows.dropped(centre)
    for c in range(width):
        slot, there = slot_of(jnp.int32(c - REACH), dropped)
        put(s_high, s_low, 0, c, tile, jnp.where(there, s[0, slot], 0.0))
    for c in range(0, width, 2):
        last = min(c + 2, width)
        lo, hi = max(c - REACH, 0), min(last - 1 + REACH, width - 1) + 1
        n = slice(c * tile, last * tile)
        k = slice(lo * tile, hi * tile)
        block = dot3(
            flat(s_high, slice(None), k),
            flat(s_low, slice(None), k),
            flat(z_high, slice(lo, hi), n),
            flat(z_low, slice(lo, hi), n),
        )
        for j in range(last - c):
            dense[c + j] = block[:, j * tile : (j + 1) * tile]
    for slot in range(2 * REACH):
        pos = slot - 1 + jnp.where(slot - 1 >= dropped, 1, 0)
        out[0, slot] = dense[REACH if slot == 0 else pos + jnp.where(pos >= REACH, 1, 0)]


def turn_kernel(meta, z, x0, x1, n0, n1, zi, zc, after, z_kept, t_own, t_up, t_down, t_swap, t_near, t_far_up, t_far_down, z_high, z_low):
    tile = z.shape[-1]
    rows = Rows(meta)

    z_kept[...] = z[...]

    def store(out, c, r, value):
        high, low = split(value.T)
        out[c * tile : (c + 1) * tile, r * tile : (r + 1) * tile] = high
        out[c * tile : (c + 1) * tile, (2 + r) * tile : (3 + r) * tile] = low

    for r in range(2):
        for c in range(COLS):
            col = c + COL0
            value = rows.own(z, r, col) if abs(col - r) <= REACH else zero(tile)
            store(t_own, c, r, value)
            put(z_high, z_low, r, c, tile, value)
        for c in range(4):
            col = c + COL0
            store(t_up, c, r, rows.packed((zc, zi), Z_UP, -4, r, col) if abs(col - (r - 4)) <= REACH else zero(tile))
            col = c + COL0 + 4
            store(t_down, c, r, rows.packed((zi, zc), Z_DOWN, 4, r, col) if abs(col - (r + 4)) <= REACH else zero(tile))
        for c in range(2):
            store(t_far_up, c, r, far_tile(rows, ((x0, x1)[r],), 1, r, c, tile))
            store(t_far_down, c, r, far_tile(rows, ((x0, x1)[r],), -1, r, c, tile))
        for side, (out, refs) in enumerate(((t_swap, (x0, x1)), (t_near, (n0, n1)))):
            first = 2 * rows.side_pair(side) + COL0
            for c in range(2 * SIDE):
                store(out, c, r, rows.side(refs[r], side, r, first + c))


def halves(turned, first, last, tile):
    part = turned[2 * first * tile : 2 * last * tile]
    return part[:, : 2 * tile], part[:, 2 * tile :]


def side_gram(rows, side, refs, turned, high, low, add, tile):
    first = 2 * rows.side_pair(side) + COL0
    for ref, r in rows.by_distance(refs):
        for c in range(2 * SIDE):
            put(high, low, r, c, tile, rows.side(ref, side, r, first + c))
    left = halves(turned, 0, SIDE, tile)
    for b in range(SIDE):
        n = slice(2 * b * tile, (2 * b + 2) * tile)
        block = dot3(*left, flat(high, slice(0, 2), n), flat(low, slice(0, 2), n))
        for a in range(SIDE):
            add(a, b, block[2 * a * tile : (2 * a + 2) * tile])
        yield


def gram_kernel(meta, t_own, t_swap, p0, p1, nearer, farther, gram, high, low, side_high, side_low):
    tile = p0.shape[-1]
    rows = Rows(meta)
    for r in range(2):
        for c in range(COLS):
            col = c + COL0
            put(high, low, r, c, tile, rows.own((p0, p1), r, col) if abs(col - r) <= REACH else zero(tile))
    for b in range(PAIRS):
        n = slice(2 * b * tile, (2 * b + 2) * tile)
        first, last = max(0, b - 2), min(PAIRS, b + 3)
        block = dot3(*halves(t_own, first, last, tile), flat(high, slice(0, 2), n), flat(low, slice(0, 2), n))
        for a in range(first, last):
            gram[PAIRS * a + b] = block[2 * (a - first) * tile : 2 * (a - first + 1) * tile]

    def add(a, b, value):
        index = PAIRS * a + b + (PAIRS + 1) * rows.side_pair(0)
        gram[index] = gram[index] + value

    for _ in side_gram(rows, 0, (nearer, farther), t_swap, side_high, side_low, add, tile):
        pass


def refine_kernel(
    meta, z, z_high, z_low, t_near, base, nearer, farther, first, second, refined, correction,
    high, low, late, d_high, d_low, d_own, update, d_out, z_out, sems,
):
    tile = z.shape[-1]
    rows = Rows(meta)
    ends = rows.parity != jnp.where(rows.even_pair, 0, 1)
    shift = rows.side_pair(1)

    def add(a, b, value):
        late[SIDE * a + b] = value

    def finish(column):
        for a, b, k, c, inner in tiles_of(tile, (column,)):
            value = base[PAIRS * a + b, inner[0], inner[1]]
            if abs(k - c) <= REACH:
                ia, ib = a - shift, b - shift
                there = rows.present(k + COL0, c + COL0)
                if not (0 < a < SIDE and 0 < b < SIDE):
                    there = there & (ia >= 0) & (ia < SIDE) & (ib >= 0) & (ib < SIDE)
                gram = late[jnp.clip(SIDE * ia + ib, 0, SIDE * SIDE - 1), inner[0], inner[1]]
                value = value - jnp.where(there, gram, 0.0)
                if a == b and a in (0, PAIRS - 1):
                    one, other = (first, second) if a == 0 else (second, first)
                    far = jnp.where(ends, one[inner[0], inner[1]], other[inner[0], inner[1]])
                    value = value - (far if k == c else jnp.where(rows.present(k + COL0, c + COL0), far, 0.0))
            put(d_high, d_low, k, c, tile, value)
            if k + COL0 in (0, 1):
                d_own[k + COL0, c] = value

    def multiply(column):
        row_matmul(z_high, z_low, d_high, d_low, update, tile, (2 * column,))

    steps = side_gram(rows, 1, (nearer, farther), t_near, high, low, add, tile)
    next(steps)
    next(steps)
    finish(0)
    next(steps)
    finish(1)
    multiply(0)
    finish(2)
    multiply(1)
    finish(3)
    multiply(2)
    for i in range(OWN):
        for slot in range(2 * REACH):
            d_out[i, slot] = d_own[i, rows.dense_slot(i, slot)]
    copies = [pltpu.make_async_copy(d_out, correction, sems.at[OWN])]
    copies[0].start()
    multiply(3)
    for i in range(OWN):
        for slot in range(2 * REACH):
            z_out[i, slot] = z[i, slot] + 0.5 * update[i, rows.dense_slot(i, slot)]
        copies.append(pltpu.make_async_copy(z_out.at[i], refined.at[i], sems.at[i]))
        copies[-1].start()
    for copy in copies:
        copy.wait()


def body(correlation, factor, pattern):
    rows_here, slots, tile = correlation.shape[:3]
    total = pattern.shape[0]
    assert rows_here == OWN and slots == 2 * REACH and total >= WIDE
    device = lax.axis_index(AXES)
    rows = (device * OWN + jnp.arange(LEFT, LEFT + WIDE, dtype=jnp.int32)) % total
    offsets = (pattern[rows][:, 1:] - rows[:, None] + total // 2) % total - total // 2
    expected = jnp.array([-3, -2, -1, 1, 2], jnp.int32)
    dropped = jnp.sum((offsets == expected).astype(jnp.int32), axis=1)
    place = jnp.stack([0] * WIDE + [device % 2, device // 2 % 2]).astype(jnp.int32)
    meta = jnp.concatenate([dropped, (device % 2)[None], (device // 2 % 2)[None]]).astype(jnp.int32)

    vmem = pl.BlockSpec(memory_space=pltpu.VMEM)
    smem = pl.BlockSpec(memory_space=pltpu.SMEM)

    def resident(value):
        if value is factor or value is correlation:
            return pltpu.with_memory_space_constraint(value, pltpu.HBM)
        return pltpu.with_memory_space_constraint(value, pltpu.VMEM)

    def call(kernel, ins, outs, scratch, flops, aliases={}, where=pltpu.VMEM):
        scalars = 1
        return pl.pallas_call(
            kernel,
            in_specs=[smem] * scalars + [vmem] * (len(ins) - scalars),
            out_specs=jax.tree.map(lambda _: pl.BlockSpec(memory_space=where), outs),
            out_shape=outs,
            scratch_shapes=scratch,
            input_output_aliases=aliases,
            compiler_params=pltpu.CompilerParams(vmem_limit_bytes=VMEM_LIMIT),
            cost_estimate=pl.CostEstimate(flops=flops, bytes_accessed=4 << 20, transcendentals=0),
        )(*ins[:scalars], *map(resident, ins[scalars:]))

    def shape(*dims, dtype=F32):
        return jax.ShapeDtypeStruct(dims, dtype)

    def halves_of(n, m):
        return [pltpu.VMEM((n, tile, m * tile), BF16)] * 2

    row = shape(1, slots, tile, tile)
    seven = shape(len(UP), tile, tile)
    nine = shape(len(Z_UP), tile, tile)
    block = shape(2 * tile, 2 * tile)
    dense = pltpu.VMEM((OWN, COLS, tile, tile), F32)

    z0, z1, zi, zc = call(pack_kernel, (place, factor), (row, row, nine, nine), [], 1000)
    x = [send(v, swap) for v in (z0, z1)]
    zi, zc = send(zi, inside), send(zc, across)
    n = [send(x[r], near) for r in range(OWN)]
    sx = send(lax.dynamic_slice_in_dim(correlation, 1 - device % 2, 1, 0), swap)
    square = shape(COLS, tile, COLS * tile, dtype=BF16)
    pair = shape(OWN, tile, COLS * tile, dtype=BF16)
    ready = call(prepare_kernel, (meta, correlation, factor, *x), (square, square, pair, pair), [], int(1e9))
    p0, p1, pf, pi, pc, *_ = call(
        product_kernel,
        (meta, *ready, *n, zi, zc),
        (row, row, row, seven, seven, square, square),
        [dense],
        int(2e9),
        aliases={1: 5, 2: 6},
    )
    pc = send(pc, across)
    px = send(pf, swap)
    pi = send(pi, inside)
    width = 2 * REACH + 1
    ps = call(
        side_kernel,
        (meta, sx, factor, *x, *n, zi, zc),
        row,
        halves_of(width, width) + halves_of(1, width) + [pltpu.VMEM((width, tile, tile), F32)],
        int(2e9),
    )
    pn = (send(ps, near), send(px, near))

    def turned(columns):
        return shape(columns * tile, 4 * tile, dtype=BF16)

    z_kept, t_own, t_up, t_down, t_swap, t_near, t_far_up, t_far_down, *z_own = call(
        turn_kernel,
        (meta, factor, *x, *n, zi, zc, ps),
        (shape(*factor.shape), turned(COLS), turned(4), turned(4), turned(2 * SIDE), turned(2 * SIDE), turned(2), turned(2),
         *[shape(OWN, tile, COLS * tile, dtype=BF16)] * 2),
        [],
        int(2e9),
    )
    early = call(
        gram_kernel,
        (meta, t_own, t_swap, p0, p1, ps, px),
        shape(PAIRS * PAIRS, 2 * tile, 2 * tile),
        halves_of(2, COLS) + halves_of(2, 2 * SIDE),
        int(4e9),
    )
    far = call(
        far_kernel,
        (meta, t_up, t_down, t_far_up, t_far_down, pi, pc, ps, px, early),
        (block, block),
        halves_of(2, 2),
        int(1e8),
    )
    far = (send(far[0], far_first), send(far[1], far_second))
    base = call(
        edge_kernel,
        (meta, t_up, t_down, pi, pc, early),
        shape(PAIRS * PAIRS, 2 * tile, 2 * tile),
        halves_of(2, COLS) + [pltpu.VMEM((2 * PAIRS, 2 * tile, 2 * tile), F32)],
        int(1e9),
    )
    return call(
        refine_kernel,
        (meta, z_kept, *z_own, t_near, base, *pn, *far),
        (shape(*factor.shape), shape(*factor.shape)),
        halves_of(2, 2 * SIDE)
        + [pltpu.VMEM((SIDE * SIDE, 2 * tile, 2 * tile), F32)]
        + halves_of(COLS, COLS)
        + [dense, dense, pltpu.VMEM(factor.shape, F32), pltpu.VMEM(factor.shape, F32), pltpu.SemaphoreType.DMA((OWN + 1,))],
        int(4e9),
        where=pl.ANY,
    )


def solution(mesh):
    tiles = P(AXES, None, None, None)

    return jax.shard_map(body, mesh=mesh, in_specs=(tiles, tiles, P()), out_specs=(tiles, tiles), check_vma=False)
```
